32 devices in a mesh: groups: 2 (over y), sample: 2 (over core), space: 8 (over z, x).
Axes of the slice: x: 2, y: 2, z: 4, core: 2. Of those that a mesh axis runs over, the one named last changes fastest.
Arguments:
- features: bfloat16 [4, 16, 16, 16, 128], P(('groups', 'sample'), 'space'), parts along dimension 0, may hold values from -6 to 6
- w_fine: bfloat16 [27, 128, 128], replicated, may hold values from -0.109375 to 0.109375
- w_down: bfloat16 [8, 128, 256], replicated, may hold values from -0.1875 to 0.1875
- mixing: bfloat16 [8, 8], replicated, may hold values from -2 to 2
- cotangent: bfloat16 [4, 8, 16384], P(('groups', 'sample'), None, 'space'), parts along dimension 0, may hold values from -6 to 6
Outputs:
- bottleneck: bfloat16 [4, 8, 16384], P(('groups', 'sample'), None, 'space'), parts along dimension 0
- feature_grad: bfloat16 [4, 16, 16, 16, 128], P(('groups', 'sample'), 'space'), parts along dimension 0
- fine_grad: float32 [884736], P(('groups', 'space')), parts along dimension 0
- down_grad: float32 [524288], P(('groups', 'space')), parts along dimension 0
- mixing_grad: float32 [16, 8], P(('groups', 'space')), parts along dimension 0
The draws below stay inside these ranges and needn't reach their ends.
There are 2 independent parts, one for each index of `groups`. The reference program is written for one: setup_inputs(seed, part) draws one part's arguments, and reference() takes and returns one part's arrays. A program takes and returns all parts, laid end to end along the dimension named above; an argument that names none is the same for every part. Nothing has to cross between parts.
All inputs are finite; a program needn't handle non-finite values.
Results may differ from the reference program's by a relative error of at most 0.0065.
Values may be sent and summed in bfloat16 or wider, within the bound.
A program may use at most 64 MiB of HBM per device.

```python
import jax
import jax.numpy as jnp
from jax import lax

C1 = 128
C2 = 256
WX = 16
WZ = 16
BATCH = 2
NY = 16
NYC = 8
PLANE = 64


def block_scale(own_key, dims, split, least, top_value):
    loudness, own = 1.0, jax.random.fold_in(own_key, 6)
    for dim, parts in split:
        draws = jnp.exp(jax.random.uniform(jax.random.fold_in(own, dim), (parts,), jnp.float32, least / len(split), top_value / len(split)))
        loudness = loudness * jnp.repeat(draws, dims[dim] // parts).reshape([-1 if axis == dim else 1 for axis in range(len(dims))])
    return loudness


def normal_values(rng, extent, scale, limit, cuts=(), kind=jnp.bfloat16):
    array = scale * jax.random.normal(rng, extent, jnp.float32)
    if cuts:
        array = array * block_scale(rng, extent, cuts, -0.22, 0.18)
    return jnp.clip(array, -limit, limit).astype(kind)


def setup_inputs(seed: int = 0, part: int = 0) -> dict:
    seeds = jax.random.split(jax.random.key(seed), 6)
    part_splits = jax.random.split(jax.random.fold_in(seeds[5], part), 6)
    features = normal_values(part_splits[0], (BATCH, NY, WX, WZ, C1), 1.0, 6.0, ((0, 2), (1, 8)))
    w_fine = normal_values(seeds[1], (27, C1, C1), (27 * C1) ** -0.5, 0.109375)
    w_down = normal_values(seeds[2], (8, C1, C2), (8 * C1) ** -0.5, 0.1875)
    mixing = normal_values(seeds[3], (NYC, NYC), NYC ** -0.5, 2.0)
    cotangent = normal_values(part_splits[4], (BATCH, NYC, PLANE * C2), 1.0, 6.0, ((0, 2), (2, 8)))
    return {"features": features, "w_fine": w_fine, "w_down": w_down, "mixing": mixing, "cotangent": cotangent}


def forward_conv(padded, weight, count):
    extent_x = padded.shape[2] - 2
    extent_z = padded.shape[3] - 2
    channels = padded.shape[4]
    total = None
    for shift_y in range(3):
        for shift_x in range(3):
            pieces = [padded[:, shift_y:shift_y + count, shift_x:shift_x + extent_x, shift_z:shift_z + extent_z, :] for shift_z in range(3)]
            stacked = jnp.concatenate(pieces, axis=-1).reshape(-1, 3 * channels)
            first = shift_y * 9 + shift_x * 3
            kernel = weight[first:first + 3].reshape(3 * channels, weight.shape[2])
            term = jnp.dot(stacked, kernel, preferred_element_type=jnp.float32)
            total = term if total is None else total + term
    return total.reshape(padded.shape[0], count, extent_x, extent_z, weight.shape[2])


def transposed_conv(padded, weight, count):
    extent_x = padded.shape[2] - 2
    extent_z = padded.shape[3] - 2
    channels = padded.shape[4]
    total = None
    for shift_y in range(3):
        for shift_x in range(3):
            pieces = [padded[:, 2 - shift_y:2 - shift_y + count, 2 - shift_x:2 - shift_x + extent_x, 2 - shift_z:2 - shift_z + extent_z, :] for shift_z in range(3)]
            stacked = jnp.concatenate(pieces, axis=-1).reshape(-1, 3 * channels)
            first = shift_y * 9 + shift_x * 3
            kernel = jnp.swapaxes(weight[first:first + 3], 1, 2).reshape(3 * channels, weight.shape[1])
            term = jnp.dot(stacked, kernel, preferred_element_type=jnp.float32)
            total = term if total is None else total + term
    return total.reshape(padded.shape[0], count, extent_x, extent_z, weight.shape[1])


def weight_terms(padded, grad, count):
    extent_x = padded.shape[2] - 2
    extent_z = padded.shape[3] - 2
    channels = padded.shape[4]
    flat_grad = grad.reshape(-1, grad.shape[4])
    blocks = []
    for shift_y in range(3):
        for shift_x in range(3):
            pieces = [padded[:, shift_y:shift_y + count, shift_x:shift_x + extent_x, shift_z:shift_z + extent_z, :] for shift_z in range(3)]
            stacked = jnp.concatenate(pieces, axis=-1).reshape(-1, 3 * channels)
            blocks.append(lax.dot_general(stacked, flat_grad, (((0,), (0,)), ((), ())), preferred_element_type=jnp.float32))
    return jnp.concatenate(blocks, axis=0).reshape(-1)


def fold_taps(hidden):
    batch, rows_here, extent_x, extent_z, channels = hidden.shape
    shaped = hidden.reshape(batch, rows_here // 2, 2, extent_x // 2, 2, extent_z // 2, 2, channels)
    return shaped.transpose(0, 1, 3, 5, 2, 4, 6, 7).reshape(-1, 8 * channels)


def unfold_taps(values, batch, rows_here, extent_x, extent_z, channels):
    shaped = values.reshape(batch, rows_here // 2, extent_x // 2, extent_z // 2, 2, 2, 2, channels)
    return shaped.transpose(0, 1, 4, 2, 5, 3, 6, 7).reshape(batch, rows_here, extent_x, extent_z, channels)


def silu_slope(value):
    sigma = jax.nn.sigmoid(value)
    return sigma * (1.0 + value * (1.0 - sigma))


def reference(features, w_fine, w_down, mixing, cotangent):
    batch, rows_here, extent_x, extent_z, channels = features.shape
    coarse_ch = w_down.shape[2]
    xpadded = jnp.pad(features, ((0, 0), (1, 1), (1, 1), (1, 1), (0, 0)))
    act = forward_conv(xpadded, w_fine, rows_here)
    hidden = (features.astype(jnp.float32) + jax.nn.silu(act)).astype(jnp.bfloat16)
    folded = fold_taps(hidden)
    down_matrix = w_down.reshape(8 * channels, coarse_ch)
    coarse = jnp.dot(folded, down_matrix, preferred_element_type=jnp.float32).astype(jnp.bfloat16)
    coarse = coarse.reshape(batch, rows_here // 2, -1)
    mixed = jnp.stack([jnp.dot(mixing, coarse[item], preferred_element_type=jnp.float32) for item in range(batch)])
    bottleneck = (coarse.astype(jnp.float32) + jax.nn.silu(mixed)).astype(jnp.bfloat16)
    cot = cotangent.astype(jnp.float32)
    mixed_grad = (cot * silu_slope(mixed)).astype(jnp.bfloat16)
    scale = float(batch * rows_here * extent_x * extent_z) ** -0.5
    mixing_grad = None
    spread_list = []
    for item in range(batch):
        term = lax.dot_general(mixed_grad[item], coarse[item], (((1,), (1,)), ((), ())), preferred_element_type=jnp.float32)
        mixing_grad = term if mixing_grad is None else mixing_grad + term
        spread_list.append(lax.dot_general(mixing, mixed_grad[item], (((0,), (0,)), ((), ())), preferred_element_type=jnp.float32))
    mixing_grad = mixing_grad * scale
    coarse_grad = (cot + jnp.stack(spread_list)).astype(jnp.bfloat16)
    flat_coarse = coarse_grad.reshape(-1, coarse_ch)
    down_grad = lax.dot_general(folded, flat_coarse, (((0,), (0,)), ((), ())), preferred_element_type=jnp.float32).reshape(-1) * scale
    hidden_grad = unfold_taps(jnp.dot(flat_coarse, down_matrix.T, preferred_element_type=jnp.float32), batch, rows_here, extent_x, extent_z, channels)
    act_grad = (hidden_grad * silu_slope(act)).astype(jnp.bfloat16)
    gpadded = jnp.pad(act_grad, ((0, 0), (1, 1), (1, 1), (1, 1), (0, 0)))
    feature_grad = (hidden_grad + transposed_conv(gpadded, w_fine, rows_here)).astype(jnp.bfloat16)
    fine_grad = weight_terms(xpadded, act_grad, rows_here) * scale
    return (bottleneck, feature_grad, fine_grad, down_grad, mixing_grad)
```

```python
import functools

import jax
import jax.numpy as jnp
from jax import lax
from jax.experimental import pallas as pl
from jax.experimental.pallas import tpu as pltpu
from jax.sharding import PartitionSpec as P

MESH = pl.DeviceIdType.MESH
F32 = jnp.float32
BF16 = jnp.bfloat16
CONTRACT_LAST = (((1,), (1,)), ((), ()))
CONTRACT_FIRST = (((0,), (0,)), ((), ()))


def fused_body(
    cfg,
    features_in, w_fine_in, w_down_in, mixing_in, cotangent_in,
    bottleneck, feature_grad, fine_out, down_out, mixing_out,
    features, w_fine, w_down, mixing, cotangent, load_s,
    x_halo, g_halo, grad16, pad, x3, g3, xt, act, hid, folded, folded_t,
    stage, fwd_send, fwd_recv, back_send, back_recv, hid_grad,
    fine16, fine_peer, fine_pair, fine_met, fine_send, fine_recv,
    down16, down_peer, down_pair, down_met, down_send, down_recv,
    mix_send, mix_recv, mix_total, mix_peer,
    fine_half, fine_half_peer, down_half, down_half_peer,
    halo_s, halo_r, fwd_s, fwd_r, back_s, back_r, mix_s, mix_r,
    ghalo_s, ghalo_r, peer_s, peer_r, dpeer_s, dpeer_r,
    pair_s, pair_r, dpair_s, dpair_r, fine_s, fine_r, down_s, down_r, last_s, last_r,
):
    n, ex, ez, ch, cc, scale = cfg
    plane = ex * ez
    hx, hz = ex // 2, ez // 2
    lanes = 128
    rows = hx * hz * cc // lanes // n
    halves = cc // lanes
    fine_rows = 27 * ch // n
    part = fine_send.shape[1]
    fine_step = fine_rows - part
    fine_mine = fine_rows // 2
    down_rows = 8 * ch // n
    down_part = down_rows // 2
    me = lax.axis_index("space")
    core = lax.axis_index("sample")
    other = 1 - core

    def to_space(src, dst, send, recv, who):
        return pltpu.make_async_remote_copy(
            src_ref=src, dst_ref=dst, send_sem=send, recv_sem=recv,
            device_id={"space": who}, device_id_type=MESH,
        )

    def to_peer(src, dst, send, recv):
        return pltpu.make_async_remote_copy(
            src_ref=src, dst_ref=dst, send_sem=send, recv_sem=recv,
            device_id={"sample": other}, device_id_type=MESH,
        )

    has_prev, has_next = me > 0, me < n - 1
    groups = n // 2
    group, side_of = me // 2, lax.rem(me, 2)
    partner = me + 1 - 2 * side_of

    barrier = pltpu.get_barrier_semaphore()
    for k in range(1, n):
        pl.semaphore_signal(
            barrier, inc=1, device_id={"space": lax.rem(me + k, n)}, device_id_type=MESH
        )
    pl.semaphore_signal(barrier, inc=1, device_id={"sample": other}, device_id_type=MESH)
    loads = [
        pltpu.make_async_copy(source, dest, load_s.at[i])
        for i, (source, dest) in enumerate(
            (
                (features_in, features),
                (w_fine_in, w_fine),
                (w_down_in, w_down),
                (mixing_in, mixing),
                (cotangent_in, cotangent),
            )
        )
    ]
    for load in loads:
        load.start()

    def halo_copies(first, last, halo, send, recv):
        down = to_space(first, halo.at[1], send.at[0], recv.at[1], me - 1)
        up = to_space(last, halo.at[0], send.at[1], recv.at[0], me + 1)
        return down, up

    def start_halo(copies):
        pl.when(has_prev)(copies[0].start)
        pl.when(has_next)(copies[1].start)

    def wait_halo(copies):
        def with_prev():
            copies[0].wait_send()
            copies[1].wait_recv()

        def with_next():
            copies[1].wait_send()
            copies[0].wait_recv()

        pl.when(has_prev)(with_prev)
        pl.when(has_next)(with_next)

    x_copies = halo_copies(features_in.at[0, 0], features_in.at[0, 1], x_halo, halo_s, halo_r)
    pl.semaphore_wait(barrier, n)
    start_halo(x_copies)

    @pl.when(me == 0)
    def _():
        x_halo[0] = jnp.zeros(x_halo.shape[1:], BF16)
        g_halo[0] = jnp.zeros(g_halo.shape[1:], BF16)

    @pl.when(me == n - 1)
    def _():
        x_halo[1] = jnp.zeros(x_halo.shape[1:], BF16)
        g_halo[1] = jnp.zeros(g_halo.shape[1:], BF16)

    pad[:, :, 0:8, :] = jnp.zeros((2, ex, 8, ch), F32)
    pad[:, :, 8 + ez : 16 + ez, :] = jnp.zeros((2, ex, 8, ch), F32)
    for rim in (0, ex + 1):
        x3[:, rim] = jnp.zeros((4, ez, 3 * ch), BF16)
        g3[:, rim] = jnp.zeros((4, ez, 3 * ch), BF16)

    def spread_rows(dest, index, row, slot):
        pad[slot, :, 8 : 8 + ez, :] = row.astype(F32)
        dest[index, 1 : 1 + ex, :, 0:ch] = pad[slot, :, 7 : 7 + ez, :].astype(BF16)
        dest[index, 1 : 1 + ex, :, ch : 2 * ch] = row
        dest[index, 1 : 1 + ex, :, 2 * ch : 3 * ch] = pad[slot, :, 9 : 9 + ez, :].astype(BF16)

    def window(source, index, shift):
        return source[index, shift : shift + ex].reshape(plane, 3 * ch)

    def taps(sy, sx):
        first = sy * 9 + sx * 3
        return w_fine[first : first + 3].reshape(3 * ch, ch)

    def mm(a, b):
        return jnp.dot(a, b, preferred_element_type=F32)

    loads[0].wait()
    spread_rows(x3, 1, features[0, 0], 0)
    spread_rows(x3, 2, features[0, 1], 1)
    loads[1].wait()
    total = None
    for sx in range(3):
        term = mm(window(x3, 1, sx), jnp.concatenate([taps(1, sx), taps(0, sx)], axis=1))
        total = term if total is None else total + term
        total = total + mm(
            window(x3, 2, sx), jnp.concatenate([taps(2, sx), taps(1, sx)], axis=1)
        )
    act[...] = total
    wait_halo(x_copies)
    spread_rows(x3, 0, x_halo[0], 0)
    spread_rows(x3, 3, x_halo[1], 1)
    for side in range(2):
        total = act[:, side * ch : (side + 1) * ch]
        for sx in range(3):
            total = total + mm(window(x3, 3 * side, sx), taps(2 * side, sx))
        act[:, side * ch : (side + 1) * ch] = total
        value = features[0, side].reshape(plane, ch).astype(F32) + total * jax.nn.sigmoid(total)
        hid[side] = value.astype(BF16).astype(F32).reshape(hx, 2, ez, ch)

    for t in range(8):
        i, j, k = t // 4, t // 2 % 2, t % 2
        piece = hid[i, :, j, pl.ds(k, hz, stride=2), :].reshape(hx * hz, ch)
        folded[:, t * ch : (t + 1) * ch] = piece.astype(BF16)
    loads[2].wait()
    coarse = mm(folded[...], w_down[...].reshape(8 * ch, cc)).astype(BF16).astype(F32)
    for h in range(halves):
        stage[pl.ds(h, hx * hz, stride=halves), :] = coarse[:, h * lanes : (h + 1) * lanes]
    fwd_send[...] = stage[...].astype(BF16).reshape(n, rows, lanes)

    def exchange(src_of, slots, send, recv):
        out = []
        for k in range(1, n):
            who = lax.rem(me + k, n)
            copy = to_space(src_of(who), slots.at[me], send.at[k - 1], recv.at[k - 1], who)
            copy.start()
            out.append(copy)
        return out

    coarse_copies = exchange(lambda who: fwd_send.at[who], fwd_recv, fwd_s, fwd_r)
    fwd_recv[me] = fwd_send[me]

    loads[3].wait()
    loads[4].wait()
    folded_t[...] = folded[...].T
    for sx in range(3):
        for j in range(4):
            xt[sx, :, j * plane : (j + 1) * plane] = window(x3, j, sx).T

    for copy in coarse_copies:
        copy.wait()
    stage[...] = fwd_recv[...].reshape(n * rows, lanes).astype(F32)
    columns = jnp.concatenate([stage[pl.ds(r, n, stride=rows), :] for r in range(rows)], axis=1)
    columns16 = columns.astype(BF16)
    mix = mixing[...]
    mixed = mm(mix, columns16)
    sigma = jax.nn.sigmoid(mixed)
    bottleneck[0] = (columns + mixed * sigma).astype(BF16)
    cot = cotangent[0].astype(F32)
    mixed_grad = (cot * (sigma * (1.0 + mixed * (1.0 - sigma)))).astype(BF16)
    spread = lax.dot_general(mix, mixed_grad, CONTRACT_FIRST, preferred_element_type=F32)
    column_grad = cot + spread
    for r in range(rows):
        stage[pl.ds(r, n, stride=rows), :] = column_grad[:, r * lanes : (r + 1) * lanes]
    back_send[...] = stage[...].astype(BF16).reshape(n, rows, lanes)
    back_copies = exchange(lambda who: back_send.at[who], back_recv, back_s, back_r)
    back_recv[me] = back_send[me]
    term = lax.dot_general(mixed_grad, columns16, CONTRACT_LAST, preferred_element_type=F32)
    mix_send[...] = jnp.zeros(mix_send.shape, F32)
    mix_send[:, 0:n] = term
    mix_copies = exchange(lambda who: mix_send, mix_recv, mix_s, mix_r)
    mix_recv[me] = mix_send[...]
    value = act[...]
    sig = jax.nn.sigmoid(value)
    act[...] = sig * (1.0 + value * (1.0 - sig))

    for copy in back_copies:
        copy.wait()
    stage[...] = back_recv[...].reshape(n * rows, lanes).astype(F32)
    flat = jnp.concatenate(
        [stage[pl.ds(h, hx * hz, stride=halves), :] for h in range(halves)], axis=1
    ).astype(BF16)

    for t in range(8):
        i, j, k = t // 4, t // 2 % 2, t % 2
        piece = lax.dot_general(flat, w_down[t], CONTRACT_LAST, preferred_element_type=F32)
        hid_grad[i, :, j, pl.ds(k, hz, stride=2), :] = piece.reshape(hx, hz, ch)
    for side in range(2):
        grad = hid_grad[side].reshape(plane, ch) * act[:, side * ch : (side + 1) * ch]
        grad16[side] = grad.astype(BF16).reshape(ex, ez, ch)
    g_copies = halo_copies(grad16.at[0], grad16.at[1], g_halo, ghalo_s, ghalo_r)

    down16[...] = mm(folded_t[...], flat).astype(BF16).reshape(n, down_rows, cc)
    dpeer = to_peer(
        down16.at[:, pl.ds(pl.multiple_of(other * down_part, 16), down_part), :],
        down_peer, dpeer_s, dpeer_r,
    )
    dpeer.start()

    def down_mine(who):
        rows_of = pl.ds(pl.multiple_of(core * down_part, 16), down_part)
        return down16[who, rows_of, :].astype(F32) + down_peer[who].astype(F32)

    def leave(met, outgoing, incoming, send, recv, k, to):
        if k == groups - 1:
            incoming[group] = met
            return []
        outgoing[k] = met
        copy = to_space(
            outgoing.at[k], incoming.at[group], send.at[k], recv.at[k], 2 * to + side_of
        )
        copy.start()
        return [copy]

    flat_grad = grad16[...].reshape(2 * plane, ch)
    peer_copies = []
    done = 0
    down_copies = []
    for t in range(9):
        sy, sx = t // 3, t % 3
        block = mm(xt[sx, :, sy * plane : (sy + 2) * plane], flat_grad)
        fine16[t * 3 * ch : (t + 1) * 3 * ch, :] = block.astype(BF16)
        while done < n and (done + 1) * fine_rows <= (t + 1) * 3 * ch:
            start = pl.multiple_of(done * fine_rows + other * fine_step, 16)
            copy = to_peer(
                fine16.at[pl.ds(start, part), :], fine_peer.at[done],
                peer_s.at[done], peer_r.at[done],
            )
            copy.start()
            peer_copies.append(copy)
            done += 1

    dpeer.wait()
    dpair_copies = []
    for k in range(groups):
        to = lax.rem(group + 1 + k, groups)
        down_pair[to] = down_mine(2 * to + 1 - side_of).astype(BF16)
        copy = to_space(down_pair.at[to], down_met.at[to], dpair_s.at[k], dpair_r.at[k], partner)
        copy.start()
        dpair_copies.append(copy)

    for copy in peer_copies:
        copy.wait()

    def fine_own(who):
        start = pl.multiple_of(who * fine_rows + core * fine_step, 16)
        return fine16[pl.ds(start, part), :].astype(F32) + fine_peer[who].astype(F32)

    pair_copies = []
    for k in range(groups):
        to = lax.rem(group + 1 + k, groups)
        fine_pair[to] = fine_own(2 * to + 1 - side_of).astype(BF16)
        copy = to_space(fine_pair.at[to], fine_met.at[to], pair_s.at[k], pair_r.at[k], partner)
        copy.start()
        pair_copies.append(copy)
    start_halo(g_copies)

    for k in range(groups):
        to = lax.rem(group + 1 + k, groups)
        dpair_copies[k].wait()
        met = (down_mine(2 * to + side_of) + down_met[to].astype(F32)).astype(BF16)
        down_copies += leave(met, down_send, down_recv, down_s, down_r, k, to)

    fine_copies = []

    def pass_on(k):
        to = lax.rem(group + 1 + k, groups)
        pair_copies[k].wait()
        met = (fine_own(2 * to + side_of) + fine_met[to].astype(F32)).astype(BF16)
        fine_copies.extend(leave(met, fine_send, fine_recv, fine_s, fine_r, k, to))

    def turned(i, sx):
        first = i * 9 + sx * 3
        return jnp.concatenate([w_fine[first + 2 - m] for m in range(3)], axis=1)

    def mt(a, b):
        return lax.dot_general(a, b, CONTRACT_LAST, preferred_element_type=F32)

    spread_rows(g3, 1, grad16[0], 0)
    spread_rows(g3, 2, grad16[1], 1)
    total = None
    for sx in range(3):
        term = mt(window(g3, 1, 2 - sx), jnp.concatenate([turned(1, sx), turned(2, sx)], axis=0))
        total = term if total is None else total + term
        total = total + mt(
            window(g3, 2, 2 - sx), jnp.concatenate([turned(0, sx), turned(1, sx)], axis=0)
        )
        if sx == 1:
            act[...] = total
            pass_on(0)
            total = act[...]
    act[...] = total
    for k in range(1, groups - 2):
        pass_on(k)
    wait_halo(g_copies)
    spread_rows(g3, 0, g_halo[0], 0)
    spread_rows(g3, 3, g_halo[1], 1)
    for side in range(2):
        total = act[:, side * ch : (side + 1) * ch] + hid_grad[side].reshape(plane, ch)
        for sx in range(3):
            total = total + mt(window(g3, 3 * side, 2 - sx), turned(2 - 2 * side, sx))
        feature_grad[0, side] = total.astype(BF16).reshape(ex, ez, ch)
        pass_on(groups - 2 + side)

    for copy in mix_copies:
        copy.wait()
    mix_total[...] = sum(mix_recv[s] for s in range(n)) * scale
    mix_swap = to_peer(mix_total, mix_peer, last_s.at[0], last_r.at[0])
    mix_swap.start()

    for copy in down_copies:
        copy.wait()
    value = sum(down_recv[s].astype(F32) for s in range(groups)) * scale
    for h in range(halves):
        down_half[pl.ds(h, down_part, stride=halves), :] = value[:, h * lanes : (h + 1) * lanes]
    down_swap = to_peer(down_half, down_half_peer, last_s.at[1], last_r.at[1])
    down_swap.start()

    for copy in fine_copies:
        copy.wait()
    value = sum(fine_recv[s].astype(F32) for s in range(groups)) * scale
    begin = fine_mine - fine_step
    fine_half[...] = jnp.where(core == 0, value[0:fine_mine], value[begin : begin + fine_mine])
    fine_swap = to_peer(fine_half, fine_half_peer, last_s.at[2], last_r.at[2])
    fine_swap.start()

    down_len = down_part * halves
    fine_out[pl.ds(pl.multiple_of(core * fine_mine, 8), fine_mine), :] = fine_half[...]
    down_out[pl.ds(pl.multiple_of(core * down_len, 8), down_len), :] = down_half[...]
    mix_swap.wait()
    mix_total[...] = mix_total[...] + mix_peer[...]
    mixing_out[...] = mix_total[pl.ds(me, 1), 0:n]
    down_swap.wait()
    down_out[pl.ds(pl.multiple_of(other * down_len, 8), down_len), :] = down_half_peer[...]
    fine_swap.wait()
    fine_out[pl.ds(pl.multiple_of(other * fine_mine, 8), fine_mine), :] = fine_half_peer[...]


def put_out(*refs):
    sources, dests, done = refs[:5], refs[5:10], refs[10]
    copies = [
        pltpu.make_async_copy(source, dest, done.at[i])
        for i, (source, dest) in enumerate(zip(sources, dests))
    ]
    for copy in copies:
        copy.start()
    for copy in copies:
        copy.wait()


def fused_fits(mesh, features, w_down):
    n = mesh.shape["space"]
    batch, ny, ex, ez, ch = features.shape
    cc = w_down.shape[2]
    spots = ex * ez // 4
    return (
        batch == mesh.shape["groups"] * mesh.shape["sample"]
        and ny == 2 * n
        and mesh.shape["sample"] == 2
        and n % 8 == 0
        and ch == 128
        and cc % 128 == 0
        and ez % 16 == 0
        and ex % 2 == 0
        and spots % 8 == 0
        and (spots * cc) % (n * 128 * 16) == 0
        and (27 * ch) % (n * 16) == 0
        and (8 * ch) % (n * 32) == 0
    )


def fused(mesh, features, w_fine, w_down, mixing, cotangent):
    n = lax.axis_size("space")
    _, _, ex, ez, ch = features.shape
    cc = w_down.shape[2]
    batch = lax.axis_size("sample")
    scale = float(batch * 2 * n * ex * ez) ** (-0.5)
    plane, spots, lanes = ex * ez, ex * ez // 4, 128
    rows = spots * cc // lanes // n
    fine_rows, down_rows = 27 * ch // n, 8 * ch // n
    half = fine_rows // 2
    part = -(-half // 16) * 16
    down_part = down_rows // 2
    down_len = down_part * cc // lanes
    vm = pltpu.VMEM
    dma = pltpu.SemaphoreType.DMA
    groups = n // 2
    arrays = (features, w_fine, w_down, mixing, cotangent)
    scratch = [
        *[vm(array.shape, BF16) for array in arrays], dma((5,)),
        vm((2, ex, ez, ch), BF16), vm((2, ex, ez, ch), BF16), vm((2, ex, ez, ch), BF16),
        vm((2, ex, ez + 16, ch), F32),
        vm((4, ex + 2, ez, 3 * ch), BF16), vm((4, ex + 2, ez, 3 * ch), BF16),
        vm((3, 3 * ch, 4 * plane), BF16),
        vm((plane, 2 * ch), F32),
        vm((2, ex // 2, 2, ez, ch), F32),
        vm((spots, 8 * ch), BF16), vm((8 * ch, spots), BF16),
        vm((n * rows, lanes), F32),
        vm((n, rows, lanes), BF16), vm((n, rows, lanes), BF16),
        vm((n, rows, lanes), BF16), vm((n, rows, lanes), BF16),
        vm((2, ex // 2, 2, ez, ch), F32),
        vm((27 * ch, ch), BF16),
        vm((n, part, ch), BF16), *[vm((groups, part, ch), BF16)] * 4,
        vm((n, down_rows, cc), BF16),
        vm((n, down_part, cc), BF16), *[vm((groups, down_part, cc), BF16)] * 4,
        vm((n, lanes), F32), vm((n, n, lanes), F32), vm((n, lanes), F32), vm((n, lanes), F32),
        vm((half, ch), F32), vm((half, ch), F32),
        vm((down_len, lanes), F32), vm((down_len, lanes), F32),
        dma((2,)), dma((2,)), dma((n - 1,)), dma((n - 1,)), dma((n - 1,)), dma((n - 1,)),
        dma((n - 1,)), dma((n - 1,)),
        dma((2,)), dma((2,)), dma((n,)), dma((n,)), dma, dma,
        *[dma((groups,))] * 4,
        *[dma((groups - 1,))] * 4, dma((3,)), dma((3,)),
    ]
    spec = pl.BlockSpec(memory_space=pltpu.VMEM)
    far = pl.BlockSpec(memory_space=pltpu.HBM)
    shapes = (
        jax.ShapeDtypeStruct(cotangent.shape, BF16),
        jax.ShapeDtypeStruct(features.shape, BF16),
        jax.ShapeDtypeStruct((fine_rows, ch), F32),
        jax.ShapeDtypeStruct((down_rows * cc // lanes, lanes), F32),
        jax.ShapeDtypeStruct((1, n), F32),
    )
    results = pl.pallas_call(
        functools.partial(fused_body, (n, ex, ez, ch, cc, scale)),
        out_shape=shapes,
        in_specs=[far] * 5,
        out_specs=tuple([spec] * 5),
        scratch_shapes=scratch,
        compiler_params=pltpu.CompilerParams(
            collective_id=0, has_side_effects=True, vmem_limit_bytes=65472 * 1024
        ),
    )(*arrays)
    a, b, c, d, e = pl.pallas_call(
        put_out,
        out_shape=shapes,
        in_specs=[spec] * 5,
        out_specs=tuple([far] * 5),
        scratch_shapes=[dma((5,))],
        compiler_params=pltpu.CompilerParams(vmem_limit_bytes=65472 * 1024),
    )(*results)
    return a, b, c.reshape(-1), d.reshape(-1), e


def with_halo(array, sides, width):
    for axis, dim in sides:
        devices, length = (lax.axis_size(axis), array.shape[dim])
        up = [(i, (i + 1) % devices) for i in range(devices - 1)]
        down = [(j, i) for i, j in up]
        last = lax.slice_in_dim(array, length - width, length, axis=dim)
        initial = lax.slice_in_dim(array, 0, width, axis=dim)
        before = lax.ppermute(last, axis, up)
        after = lax.ppermute(initial, axis, down)
        array = jnp.concatenate([before, array, after], axis=dim)
    return array


def forward_conv(padded, weight, count):
    extent_x = padded.shape[2] - 2
    extent_z = padded.shape[3] - 2
    channels = padded.shape[4]
    total = None
    for shift_y in range(3):
        for shift_x in range(3):
            pieces = [
                padded[
                    :,
                    shift_y : shift_y + count,
                    shift_x : shift_x + extent_x,
                    shift_z : shift_z + extent_z,
                    :,
                ]
                for shift_z in range(3)
            ]
            stacked = jnp.concatenate(pieces, axis=-1).reshape(-1, 3 * channels)
            first = shift_y * 9 + shift_x * 3
            kernel = weight[first : first + 3].reshape(3 * channels, weight.shape[2])
            term = jnp.dot(stacked, kernel, preferred_element_type=jnp.float32)
            total = term if total is None else total + term
    return total.reshape(padded.shape[0], count, extent_x, extent_z, weight.shape[2])


def transposed_conv(padded, weight, count):
    extent_x = padded.shape[2] - 2
    extent_z = padded.shape[3] - 2
    channels = padded.shape[4]
    total = None
    for shift_y in range(3):
        for shift_x in range(3):
            pieces = [
                padded[
                    :,
                    2 - shift_y : 2 - shift_y + count,
                    2 - shift_x : 2 - shift_x + extent_x,
                    2 - shift_z : 2 - shift_z + extent_z,
                    :,
                ]
                for shift_z in range(3)
            ]
            stacked = jnp.concatenate(pieces, axis=-1).reshape(-1, 3 * channels)
            first = shift_y * 9 + shift_x * 3
            kernel = jnp.swapaxes(weight[first : first + 3], 1, 2).reshape(
                3 * channels, weight.shape[1]
            )
            term = jnp.dot(stacked, kernel, preferred_element_type=jnp.float32)
            total = term if total is None else total + term
    return total.reshape(padded.shape[0], count, extent_x, extent_z, weight.shape[1])


def weight_terms(padded, grad, count):
    extent_x = padded.shape[2] - 2
    extent_z = padded.shape[3] - 2
    channels = padded.shape[4]
    flat_grad = grad.reshape(-1, grad.shape[4])
    blocks = []
    for shift_y in range(3):
        for shift_x in range(3):
            pieces = [
                padded[
                    :,
                    shift_y : shift_y + count,
                    shift_x : shift_x + extent_x,
                    shift_z : shift_z + extent_z,
                    :,
                ]
                for shift_z in range(3)
            ]
            stacked = jnp.concatenate(pieces, axis=-1).reshape(-1, 3 * channels)
            blocks.append(
                lax.dot_general(
                    stacked, flat_grad, (((0,), (0,)), ((), ())), preferred_element_type=jnp.float32
                )
            )
    return jnp.concatenate(blocks, axis=0).reshape(-1)


def fold_taps(hidden):
    batch, rows_here, extent_x, extent_z, channels = hidden.shape
    shaped = hidden.reshape(batch, rows_here // 2, 2, extent_x // 2, 2, extent_z // 2, 2, channels)
    return shaped.transpose(0, 1, 3, 5, 2, 4, 6, 7).reshape(-1, 8 * channels)


def unfold_taps(values, batch, rows_here, extent_x, extent_z, channels):
    shaped = values.reshape(batch, rows_here // 2, extent_x // 2, extent_z // 2, 2, 2, 2, channels)
    return shaped.transpose(0, 1, 4, 2, 5, 3, 6, 7).reshape(
        batch, rows_here, extent_x, extent_z, channels
    )


def silu_slope(value):
    sigma = jax.nn.sigmoid(value)
    return sigma * (1.0 + value * (1.0 - sigma))


def local(features, w_fine, w_down, mixing, cotangent):
    batch, rows_here, extent_x, extent_z, channels = features.shape
    coarse_ch = w_down.shape[2]
    rimmed = with_halo(features, (("space", 1),), 1)
    xpadded = jnp.pad(rimmed, ((0, 0), (0, 0), (1, 1), (1, 1), (0, 0)))
    act = forward_conv(xpadded, w_fine, rows_here)
    hidden = (features.astype(jnp.float32) + jax.nn.silu(act)).astype(jnp.bfloat16)
    folded = fold_taps(hidden)
    down_matrix = w_down.reshape(8 * channels, coarse_ch)
    coarse = jnp.dot(folded, down_matrix, preferred_element_type=jnp.float32).astype(jnp.bfloat16)
    coarse = coarse.reshape(batch, rows_here // 2, -1)
    columns = lax.all_to_all(coarse, "space", split_axis=2, concat_axis=1, tiled=True)
    mixed = jnp.stack([jnp.dot(mixing, columns[0], preferred_element_type=jnp.float32)])
    bottleneck = (columns.astype(jnp.float32) + jax.nn.silu(mixed)).astype(jnp.bfloat16)
    cot = cotangent.astype(jnp.float32)
    mixed_grad = (cot * silu_slope(mixed)).astype(jnp.bfloat16)
    term = lax.dot_general(
        mixed_grad[0], columns[0], (((1,), (1,)), ((), ())), preferred_element_type=jnp.float32
    )
    spread_list = [
        lax.dot_general(
            mixing, mixed_grad[0], (((0,), (0,)), ((), ())), preferred_element_type=jnp.float32
        )
    ]
    column_grad = (cot + jnp.stack(spread_list)).astype(jnp.bfloat16)
    coarse_grad = lax.all_to_all(column_grad, "space", split_axis=1, concat_axis=2, tiled=True)
    flat_coarse = coarse_grad.reshape(-1, coarse_ch)
    down_terms = lax.dot_general(
        folded, flat_coarse, (((0,), (0,)), ((), ())), preferred_element_type=jnp.float32
    ).reshape(-1)
    hidden_grad = unfold_taps(
        jnp.dot(flat_coarse, down_matrix.T, preferred_element_type=jnp.float32),
        batch,
        rows_here,
        extent_x,
        extent_z,
        channels,
    )
    act_grad = (hidden_grad * silu_slope(act)).astype(jnp.bfloat16)
    grad_rim = with_halo(act_grad, (("space", 1),), 1)
    gpadded = jnp.pad(grad_rim, ((0, 0), (0, 0), (1, 1), (1, 1), (0, 0)))
    spread = transposed_conv(gpadded, w_fine, rows_here)
    feature_grad = (hidden_grad + spread).astype(jnp.bfloat16)
    fine_terms = weight_terms(xpadded, act_grad, rows_here)
    scale = float(
        batch * lax.axis_size("sample") * rows_here * lax.axis_size("space") * extent_x * extent_z
    ) ** (-0.5)
    shares = (
        lax.psum_scatter(fine_terms, "space", scatter_dimension=0, tiled=True),
        lax.psum_scatter(down_terms, "space", scatter_dimension=0, tiled=True),
        lax.psum_scatter(term, "space", scatter_dimension=0, tiled=True),
    )
    totals = lax.psum((shares[0], shares[1], shares[2]), "sample")
    return (bottleneck, feature_grad, totals[0] * scale, totals[1] * scale, totals[2] * scale)


def solution(mesh):
    placed = (
        P(("groups", "sample"), "space", None, None, None),
        P(),
        P(),
        P(),
        P(("groups", "sample"), None, "space"),
    )
    out_specs = (
        P(("groups", "sample"), None, "space"),
        P(("groups", "sample"), "space", None, None, None),
        P(("groups", "space")),
        P(("groups", "space")),
        P(("groups", "space"), None),
    )

    def step(features, w_fine, w_down, mixing, cotangent):
        kernel = functools.partial(fused, mesh) if fused_fits(mesh, features, w_down) else local
        mapped = jax.shard_map(
            kernel, mesh=mesh, in_specs=placed, out_specs=out_specs, check_vma=False
        )
        return mapped(features, w_fine, w_down, mixing, cotangent)

    return step
```

```python
import functools

import jax
import jax.numpy as jnp
from jax import lax
from jax.experimental import pallas as pl
from jax.experimental.pallas import tpu as pltpu
from jax.sharding import PartitionSpec as P

MESH = pl.DeviceIdType.MESH
F32 = jnp.float32
BF16 = jnp.bfloat16
CONTRACT_LAST = (((1,), (1,)), ((), ()))
CONTRACT_FIRST = (((0,), (0,)), ((), ()))


def fused_body(
    cfg,
    features_in, w_fine_in, w_down_in, mixing_in, cotangent_in,
    bottleneck, feature_grad, fine_out, down_out, mixing_out,
    features, w_fine, w_down, mixing, cotangent, load_s,
    x_halo, g_halo, grad16, pad, x3, g3, xt, act, hid, folded, fold_met, folded_t,
    stage, fwd_send, fwd_recv, back_send, back_recv, hid_grad,
    fine16, fine_peer, fine_pair, fine_met, fine_send, fine_recv,
    down16, down_peer, down_send, down_recv,
    mix_send, mix_recv, mix_total, mix_peer,
    fine_half, fine_half_peer, down_half, down_half_peer,
    halo_s, halo_r, fwd_s, fwd_r, back_s, back_r, mix_s, mix_r,
    ghalo_s, ghalo_r, peer_s, peer_r, dpeer_s, dpeer_r,
    pair_s, pair_r, fold_s, fold_r, fine_s, fine_r, down_s, down_r, last_s, last_r,
):
    n, ex, ez, ch, cc, scale = cfg
    plane = ex * ez
    hx, hz = ex // 2, ez // 2
    lanes = 128
    rows = hx * hz * cc // lanes // n
    halves = cc // lanes
    fine_rows = 27 * ch // n
    part = fine_send.shape[1]
    fine_step = fine_rows - part
    fine_mine = fine_rows // 2
    down_rows = 8 * ch // n
    down_part = down_rows // 2
    me = lax.axis_index("space")
    core = lax.axis_index("sample")
    other = 1 - core

    def to_space(src, dst, send, recv, who):
        return pltpu.make_async_remote_copy(
            src_ref=src, dst_ref=dst, send_sem=send, recv_sem=recv,
            device_id={"space": who}, device_id_type=MESH,
        )

    def to_peer(src, dst, send, recv):
        return pltpu.make_async_remote_copy(
            src_ref=src, dst_ref=dst, send_sem=send, recv_sem=recv,
            device_id={"sample": other}, device_id_type=MESH,
        )

    has_prev, has_next = me > 0, me < n - 1
    groups = n // 2
    group, side_of = me // 2, lax.rem(me, 2)
    partner = me + 1 - 2 * side_of

    barrier = pltpu.get_barrier_semaphore()
    for k in range(1, n):
        pl.semaphore_signal(
            barrier, inc=1, device_id={"space": lax.rem(me + k, n)}, device_id_type=MESH
        )
    pl.semaphore_signal(barrier, inc=1, device_id={"sample": other}, device_id_type=MESH)
    loads = [
        pltpu.make_async_copy(source, dest, load_s.at[i])
        for i, (source, dest) in enumerate(
            (
                (features_in, features),
                (w_fine_in, w_fine),
                (w_down_in, w_down),
                (mixing_in, mixing),
                (cotangent_in, cotangent),
            )
        )
    ]
    for load in loads:
        load.start()

    @pl.when(me == 0)
    def _():
        x_halo[0] = jnp.zeros(x_halo.shape[1:], BF16)
        g_halo[0] = jnp.zeros(g_halo.shape[1:], BF16)

    @pl.when(me == n - 1)
    def _():
        x_halo[1] = jnp.zeros(x_halo.shape[1:], BF16)
        g_halo[1] = jnp.zeros(g_halo.shape[1:], BF16)

    def halo_copies(first, last, halo, send, recv):
        down = to_space(first, halo.at[1], send.at[0], recv.at[1], me - 1)
        up = to_space(last, halo.at[0], send.at[1], recv.at[0], me + 1)
        return down, up

    def start_halo(copies):
        pl.when(has_prev)(copies[0].start)
        pl.when(has_next)(copies[1].start)

    def wait_halo(copies):
        def with_prev():
            copies[0].wait_send()
            copies[1].wait_recv()

        def with_next():
            copies[1].wait_send()
            copies[0].wait_recv()

        pl.when(has_prev)(with_prev)
        pl.when(has_next)(with_next)

    pad[:, :, 0:8, :] = jnp.zeros((2, ex, 8, ch), F32)
    pad[:, :, 8 + ez : 16 + ez, :] = jnp.zeros((2, ex, 8, ch), F32)
    for rim in (0, ex + 1):
        x3[:, rim] = jnp.zeros((4, ez, 3 * ch), BF16)
        g3[:, rim] = jnp.zeros((4, ez, 3 * ch), BF16)

    def spread_rows(dest, index, row, slot):
        pad[slot, :, 8 : 8 + ez, :] = row.astype(F32)
        dest[index, 1 : 1 + ex, :, 0:ch] = pad[slot, :, 7 : 7 + ez, :].astype(BF16)
        dest[index, 1 : 1 + ex, :, ch : 2 * ch] = row
        dest[index, 1 : 1 + ex, :, 2 * ch : 3 * ch] = pad[slot, :, 9 : 9 + ez, :].astype(BF16)

    def window(source, index, shift):
        return source[index, shift : shift + ex].reshape(plane, 3 * ch)

    def taps(sy, sx):
        first = sy * 9 + sx * 3
        return w_fine[first : first + 3].reshape(3 * ch, ch)

    def mm(a, b):
        return jnp.dot(a, b, preferred_element_type=F32)

    loads[0].wait()
    spread_rows(x3, 1, features[0, 0], 0)
    spread_rows(x3, 2, features[0, 1], 1)
    loads[1].wait()
    total = None
    x_copies = halo_copies(features.at[0, 0], features.at[0, 1], x_halo, halo_s, halo_r)
    for sx in range(3):
        term = mm(window(x3, 1, sx), jnp.concatenate([taps(1, sx), taps(0, sx)], axis=1))
        total = term if total is None else total + term
        total = total + mm(
            window(x3, 2, sx), jnp.concatenate([taps(2, sx), taps(1, sx)], axis=1)
        )
        if sx == 0:
            act[...] = total
            pl.semaphore_wait(barrier, n)
            start_halo(x_copies)
            total = act[...]
    act[...] = total
    wait_halo(x_copies)
    spread_rows(x3, 0, x_halo[0], 0)
    spread_rows(x3, 3, x_halo[1], 1)
    for side in range(2):
        total = act[:, side * ch : (side + 1) * ch]
        for sx in range(3):
            total = total + mm(window(x3, 3 * side, sx), taps(2 * side, sx))
        act[:, side * ch : (side + 1) * ch] = total
        value = features[0, side].reshape(plane, ch).astype(F32) + total * jax.nn.sigmoid(total)
        hid[side] = value.astype(BF16).astype(F32).reshape(hx, 2, ez, ch)

    for t in range(8):
        i, j, k = t // 4, t // 2 % 2, t % 2
        piece = hid[i, :, j, pl.ds(k, hz, stride=2), :].reshape(hx * hz, ch)
        folded[k, :, t // 2 * ch : (t // 2 + 1) * ch] = piece.astype(BF16)
    loads[2].wait()
    coarse = mm(folded[0], jnp.concatenate([w_down[t] for t in range(0, 8, 2)], axis=0))
    coarse = coarse + mm(folded[1], jnp.concatenate([w_down[t] for t in range(1, 8, 2)], axis=0))
    coarse = coarse.astype(BF16).astype(F32)
    for h in range(halves):
        stage[pl.ds(h, hx * hz, stride=halves), :] = coarse[:, h * lanes : (h + 1) * lanes]
    fwd_send[...] = stage[...].astype(BF16).reshape(n, rows, lanes)

    def exchange(src_of, slot, send, recv):
        out = []
        for k in range(1, n):
            who = lax.rem(me + k, n)
            copy = to_space(src_of(who), slot(), send.at[k - 1], recv.at[k - 1], who)
            copy.start()
            out.append(copy)
        return out

    coarse_copies = exchange(
        lambda who: fwd_send.at[who], lambda: fwd_recv.at[me], fwd_s, fwd_r
    )
    fold_copy = to_space(folded.at[1 - side_of], fold_met, fold_s, fold_r, partner)
    fold_copy.start()
    fwd_recv[me] = fwd_send[me]

    loads[3].wait()
    loads[4].wait()
    for sx in range(3):
        for j in range(4):
            xt[sx, :, j * plane : (j + 1) * plane] = window(x3, j, sx).T

    for copy in coarse_copies:
        copy.wait()
    stage[...] = fwd_recv[...].reshape(n * rows, lanes).astype(F32)
    columns = jnp.concatenate([stage[pl.ds(r, n, stride=rows), :] for r in range(rows)], axis=1)
    columns16 = columns.astype(BF16)
    mix = mixing[...]
    mixed = mm(mix, columns16)
    sigma = jax.nn.sigmoid(mixed)
    bottleneck[0] = (columns + mixed * sigma).astype(BF16)
    cot = cotangent[0].astype(F32)
    mixed_grad = (cot * (sigma * (1.0 + mixed * (1.0 - sigma)))).astype(BF16)
    spread = lax.dot_general(mix, mixed_grad, CONTRACT_FIRST, preferred_element_type=F32)
    column_grad = cot + spread
    for r in range(rows):
        stage[pl.ds(r, n, stride=rows), :] = column_grad[:, r * lanes : (r + 1) * lanes]
    back_send[...] = stage[...].astype(BF16).reshape(n, rows, lanes)
    back_copies = exchange(
        lambda who: back_send.at[pl.ds(who // 2 * 2, 2)], lambda: back_recv.at[:, me],
        back_s, back_r,
    )
    for side in range(2):
        back_recv[side, me] = back_send[2 * group + side]
    term = lax.dot_general(mixed_grad, columns16, CONTRACT_LAST, preferred_element_type=F32)
    mix_send[...] = jnp.zeros(mix_send.shape, F32)
    mix_send[:, 0:n] = term
    mix_copies = exchange(lambda who: mix_send, lambda: mix_recv.at[me], mix_s, mix_r)
    mix_recv[me] = mix_send[...]
    value = act[...]
    sig = jax.nn.sigmoid(value)
    act[...] = sig * (1.0 + value * (1.0 - sig))

    fold_copy.wait()
    folded_t[...] = jnp.concatenate([folded[side_of], fold_met[...]], axis=0).T

    def flat_of(side):
        stage[...] = back_recv[side].reshape(n * rows, lanes).astype(F32)
        return jnp.concatenate(
            [stage[pl.ds(h, hx * hz, stride=halves), :] for h in range(halves)], axis=1
        ).astype(BF16)

    for copy in back_copies:
        copy.wait()
    flat = flat_of(side_of)

    for t in range(8):
        i, j, k = t // 4, t // 2 % 2, t % 2
        piece = lax.dot_general(flat, w_down[t], CONTRACT_LAST, preferred_element_type=F32)
        hid_grad[i, :, j, pl.ds(k, hz, stride=2), :] = piece.reshape(hx, hz, ch)
    for side in range(2):
        grad = hid_grad[side].reshape(plane, ch) * act[:, side * ch : (side + 1) * ch]
        grad16[side] = grad.astype(BF16).reshape(ex, ez, ch)
    g_copies = halo_copies(grad16.at[0], grad16.at[1], g_halo, ghalo_s, ghalo_r)

    upper = group >= groups // 2

    def owner(k):
        if k == groups - 1:
            return group
        first, last = k, groups - 1 - k
        first = first + (first >= group).astype(jnp.int32)
        last = last - (last <= group).astype(jnp.int32)
        return jnp.where(upper, first, last)

    def leave(met, outgoing, incoming, send, recv, k):
        to = owner(k)
        if k == groups - 1:
            incoming[group] = met
            return
        step = lax.rem(to - group + groups, groups) - 1
        outgoing[step] = met
        to_space(
            outgoing.at[step], incoming.at[group], send.at[step], recv.at[step], 2 * to + side_of
        ).start()

    def wait_left(outgoing, incoming, send, recv):
        for step in range(groups - 1):
            source = lax.rem(group - 1 - step + groups, groups)
            to_space(
                outgoing.at[step], incoming.at[source], send.at[step], recv.at[step], partner
            ).wait()

    flat_grad = grad16[...].reshape(2 * plane, ch)

    def fine_block(i):
        t = jnp.where(upper, i, 8 - i)
        sy, sx = t // 3, lax.rem(t, 3)
        window_t = xt[sx, :, pl.ds(pl.multiple_of(sy * plane, lanes), 2 * plane)]
        start = pl.multiple_of(t * 3 * ch, lanes)
        fine16[pl.ds(start, 3 * ch), :] = mm(window_t, flat_grad).astype(BF16)

    peer_copies = []

    def fine_to_peer(k):
        for j in range(2):
            who = 2 * owner(k) + j
            start = pl.multiple_of(who * fine_rows + other * fine_step, 16)
            copy = to_peer(
                fine16.at[pl.ds(start, part), :], fine_peer.at[who],
                peer_s.at[2 * k + j], peer_r.at[2 * k + j],
            )
            copy.start()
            peer_copies.append(copy)

    def fine_own(who):
        start = pl.multiple_of(who * fine_rows + core * fine_step, 16)
        return fine16[pl.ds(start, part), :].astype(F32) + fine_peer[who].astype(F32)

    pair_copies = []

    def fine_to_pair(k):
        peer_copies[2 * k].wait()
        peer_copies[2 * k + 1].wait()
        fine_pair[k] = fine_own(2 * owner(k) + 1 - side_of).astype(BF16)
        copy = to_space(fine_pair.at[k], fine_met.at[k], pair_s.at[k], pair_r.at[k], partner)
        copy.start()
        pair_copies.append(copy)

    def pass_on(k):
        pair_copies[k].wait()
        met = fine_own(2 * owner(k) + side_of) + fine_met[k].astype(F32)
        leave(met.astype(BF16), fine_send, fine_recv, fine_s, fine_r, k)

    ready = [-(-(k + 1) * 2 * fine_rows // (3 * ch)) if 2 * k < groups else 9 for k in range(groups)]
    sent = 0
    for i in range(9):
        fine_block(i)
        while sent < groups and ready[sent] <= i + 1:
            fine_to_peer(sent)
            if sent == 0:
                both = jnp.concatenate([flat, flat_of(1 - side_of)], axis=0)
                down16[...] = mm(folded_t[...], both).astype(BF16).reshape(groups, down_rows, cc)
                down_copy = to_peer(
                    down16.at[:, pl.ds(pl.multiple_of(other * down_part, 16), down_part), :],
                    down_peer, dpeer_s, dpeer_r,
                )
                down_copy.start()
            sent += 1
    fine_to_pair(0)
    down_copy.wait()
    for k in range(groups):
        to = owner(k)
        mine = down16[to, pl.ds(pl.multiple_of(core * down_part, 16), down_part), :]
        total = mine.astype(F32) + down_peer[to].astype(F32)
        leave(total.astype(BF16), down_send, down_recv, down_s, down_r, k)
    for k in range(1, groups):
        fine_to_pair(k)

    def turned(i, sx):
        first = i * 9 + sx * 3
        return jnp.concatenate([w_fine[first + 2 - m] for m in range(3)], axis=1)

    def mt(a, b):
        return lax.dot_general(a, b, CONTRACT_LAST, preferred_element_type=F32)

    spread_rows(g3, 1, grad16[0], 0)
    spread_rows(g3, 2, grad16[1], 1)
    total = None
    for sx in range(3):
        term = mt(window(g3, 1, 2 - sx), jnp.concatenate([turned(1, sx), turned(2, sx)], axis=0))
        total = term if total is None else total + term
        total = total + mt(
            window(g3, 2, 2 - sx), jnp.concatenate([turned(0, sx), turned(1, sx)], axis=0)
        )
    act[...] = total
    pass_on(0)
    start_halo(g_copies)
    for k in range(1, groups):
        pass_on(k)
    wait_halo(g_copies)
    spread_rows(g3, 0, g_halo[0], 0)
    spread_rows(g3, 3, g_halo[1], 1)
    for side in range(2):
        total = act[:, side * ch : (side + 1) * ch] + hid_grad[side].reshape(plane, ch)
        for sx in range(3):
            total = total + mt(window(g3, 3 * side, 2 - sx), turned(2 - 2 * side, sx))
        feature_grad[0, side] = total.astype(BF16).reshape(ex, ez, ch)

    for copy in mix_copies:
        copy.wait()
    mix_total[...] = sum(mix_recv[s] for s in range(n)) * scale
    mix_swap = to_peer(mix_total, mix_peer, last_s.at[0], last_r.at[0])
    mix_swap.start()

    wait_left(down_send, down_recv, down_s, down_r)
    value = sum(down_recv[s].astype(F32) for s in range(groups)) * scale
    for h in range(halves):
        down_half[pl.ds(h, down_part, stride=halves), :] = value[:, h * lanes : (h + 1) * lanes]
    down_swap = to_peer(down_half, down_half_peer, last_s.at[1], last_r.at[1])
    down_swap.start()

    wait_left(fine_send, fine_recv, fine_s, fine_r)
    value = sum(fine_recv[s].astype(F32) for s in range(groups)) * scale
    begin = fine_mine - fine_step
    fine_half[...] = jnp.where(core == 0, value[0:fine_mine], value[begin : begin + fine_mine])
    fine_swap = to_peer(fine_half, fine_half_peer, last_s.at[2], last_r.at[2])
    fine_swap.start()

    down_len = down_part * halves
    fine_out[pl.ds(pl.multiple_of(core * fine_mine, 8), fine_mine), :] = fine_half[...]
    down_out[pl.ds(pl.multiple_of(core * down_len, 8), down_len), :] = down_half[...]
    mix_swap.wait()
    mix_total[...] = mix_total[...] + mix_peer[...]
    mixing_out[...] = mix_total[pl.ds(me, 1), 0:n]
    down_swap.wait()
    down_out[pl.ds(pl.multiple_of(other * down_len, 8), down_len), :] = down_half_peer[...]
    fine_swap.wait()
    fine_out[pl.ds(pl.multiple_of(other * fine_mine, 8), fine_mine), :] = fine_half_peer[...]


def put_out(*refs):
    sources, dests, done = refs[:5], refs[5:10], refs[10]
    copies = [
        pltpu.make_async_copy(source, dest, done.at[i])
        for i, (source, dest) in enumerate(zip(sources, dests))
    ]
    for copy in copies:
        copy.start()
    for copy in copies:
        copy.wait()


def fused_fits(mesh, features, w_down):
    n = mesh.shape["space"]
    batch, ny, ex, ez, ch = features.shape
    cc = w_down.shape[2]
    spots = ex * ez // 4
    return (
        batch == mesh.shape["groups"] * mesh.shape["sample"]
        and ny == 2 * n
        and mesh.shape["sample"] == 2
        and n == w_down.shape[0]
        and ch == 128
        and cc % 128 == 0
        and ez % 16 == 0
        and ex % 2 == 0
        and spots % 8 == 0
        and (spots * cc) % (n * 128 * 16) == 0
        and (27 * ch) % (n * 16) == 0
        and (8 * ch) % (n * 32) == 0
    )


def fused(mesh, features, w_fine, w_down, mixing, cotangent):
    n = lax.axis_size("space")
    _, _, ex, ez, ch = features.shape
    cc = w_down.shape[2]
    batch = lax.axis_size("sample")
    scale = float(batch * 2 * n * ex * ez) ** (-0.5)
    plane, spots, lanes = ex * ez, ex * ez // 4, 128
    rows = spots * cc // lanes // n
    fine_rows, down_rows = 27 * ch // n, 8 * ch // n
    half = fine_rows // 2
    part = -(-half // 16) * 16
    down_part = down_rows // 2
    down_len = down_part * cc // lanes
    vm = pltpu.VMEM
    dma = pltpu.SemaphoreType.DMA
    groups = n // 2
    arrays = (features, w_fine, w_down, mixing, cotangent)
    scratch = [
        *[vm(array.shape, BF16) for array in arrays], dma((5,)),
        vm((2, ex, ez, ch), BF16), vm((2, ex, ez, ch), BF16), vm((2, ex, ez, ch), BF16),
        vm((2, ex, ez + 16, ch), F32),
        vm((4, ex + 2, ez, 3 * ch), BF16), vm((4, ex + 2, ez, 3 * ch), BF16),
        vm((3, 3 * ch, 4 * plane), BF16),
        vm((plane, 2 * ch), F32),
        vm((2, ex // 2, 2, ez, ch), F32),
        vm((2, spots, 4 * ch), BF16), vm((spots, 4 * ch), BF16), vm((4 * ch, 2 * spots), BF16),
        vm((n * rows, lanes), F32),
        vm((n, rows, lanes), BF16), vm((n, rows, lanes), BF16),
        vm((n, rows, lanes), BF16), vm((2, n, rows, lanes), BF16),
        vm((2, ex // 2, 2, ez, ch), F32),
        vm((27 * ch, ch), BF16),
        vm((n, part, ch), BF16), *[vm((groups, part, ch), BF16)] * 4,
        vm((groups, down_rows, cc), BF16), *[vm((groups, down_part, cc), BF16)] * 3,
        vm((n, lanes), F32), vm((n, n, lanes), F32), vm((n, lanes), F32), vm((n, lanes), F32),
        vm((half, ch), F32), vm((half, ch), F32),
        vm((down_len, lanes), F32), vm((down_len, lanes), F32),
        dma((2,)), dma((2,)), dma((n - 1,)), dma((n - 1,)), dma((n - 1,)), dma((n - 1,)),
        dma((n - 1,)), dma((n - 1,)),
        dma((2,)), dma((2,)), dma((n,)), dma((n,)), dma, dma,
        *[dma((groups,))] * 2, dma, dma,
        *[dma((groups - 1,))] * 4, dma((3,)), dma((3,)),
    ]
    spec = pl.BlockSpec(memory_space=pltpu.VMEM)
    far = pl.BlockSpec(memory_space=pltpu.HBM)
    shapes = (
        jax.ShapeDtypeStruct(cotangent.shape, BF16),
        jax.ShapeDtypeStruct(features.shape, BF16),
        jax.ShapeDtypeStruct((fine_rows, ch), F32),
        jax.ShapeDtypeStruct((down_rows * cc // lanes, lanes), F32),
        jax.ShapeDtypeStruct((1, n), F32),
    )
    results = pl.pallas_call(
        functools.partial(fused_body, (n, ex, ez, ch, cc, scale)),
        out_shape=shapes,
        in_specs=[far] * 5,
        out_specs=tuple([spec] * 5),
        scratch_shapes=scratch,
        compiler_params=pltpu.CompilerParams(
            collective_id=0, has_side_effects=True, vmem_limit_bytes=65472 * 1024
        ),
    )(*arrays)
    a, b, c, d, e = pl.pallas_call(
        put_out,
        out_shape=shapes,
        in_specs=[spec] * 5,
        out_specs=tuple([far] * 5),
        scratch_shapes=[dma((5,))],
        compiler_params=pltpu.CompilerParams(vmem_limit_bytes=65472 * 1024),
    )(*results)
    return a, b, c.reshape(-1), d.reshape(-1), e


def with_halo(array, sides, width):
    for axis, dim in sides:
        devices, length = (lax.axis_size(axis), array.shape[dim])
        up = [(i, (i + 1) % devices) for i in range(devices - 1)]
        down = [(j, i) for i, j in up]
        last = lax.slice_in_dim(array, length - width, length, axis=dim)
        initial = lax.slice_in_dim(array, 0, width, axis=dim)
        before = lax.ppermute(last, axis, up)
        after = lax.ppermute(initial, axis, down)
        array = jnp.concatenate([before, array, after], axis=dim)
    return array


def forward_conv(padded, weight, count):
    extent_x = padded.shape[2] - 2
    extent_z = padded.shape[3] - 2
    channels = padded.shape[4]
    total = None
    for shift_y in range(3):
        for shift_x in range(3):
            pieces = [
                padded[
                    :,
                    shift_y : shift_y + count,
                    shift_x : shift_x + extent_x,
                    shift_z : shift_z + extent_z,
                    :,
                ]
                for shift_z in range(3)
            ]
            stacked = jnp.concatenate(pieces, axis=-1).reshape(-1, 3 * channels)
            first = shift_y * 9 + shift_x * 3
            kernel = weight[first : first + 3].reshape(3 * channels, weight.shape[2])
            term = jnp.dot(stacked, kernel, preferred_element_type=jnp.float32)
            total = term if total is None else total + term
    return total.reshape(padded.shape[0], count, extent_x, extent_z, weight.shape[2])


def transposed_conv(padded, weight, count):
    extent_x = padded.shape[2] - 2
    extent_z = padded.shape[3] - 2
    channels = padded.shape[4]
    total = None
    for shift_y in range(3):
        for shift_x in range(3):
            pieces = [
                padded[
                    :,
                    2 - shift_y : 2 - shift_y + count,
                    2 - shift_x : 2 - shift_x + extent_x,
                    2 - shift_z : 2 - shift_z + extent_z,
                    :,
                ]
                for shift_z in range(3)
            ]
            stacked = jnp.concatenate(pieces, axis=-1).reshape(-1, 3 * channels)
            first = shift_y * 9 + shift_x * 3
            kernel = jnp.swapaxes(weight[first : first + 3], 1, 2).reshape(
                3 * channels, weight.shape[1]
            )
            term = jnp.dot(stacked, kernel, preferred_element_type=jnp.float32)
            total = term if total is None else total + term
    return total.reshape(padded.shape[0], count, extent_x, extent_z, weight.shape[1])


def weight_terms(padded, grad, count):
    extent_x = padded.shape[2] - 2
    extent_z = padded.shape[3] - 2
    channels = padded.shape[4]
    flat_grad = grad.reshape(-1, grad.shape[4])
    blocks = []
    for shift_y in range(3):
        for shift_x in range(3):
            pieces = [
                padded[
                    :,
                    shift_y : shift_y + count,
                    shift_x : shift_x + extent_x,
                    shift_z : shift_z + extent_z,
                    :,
                ]
                for shift_z in range(3)
            ]
            stacked = jnp.concatenate(pieces, axis=-1).reshape(-1, 3 * channels)
            blocks.append(
                lax.dot_general(
                    stacked, flat_grad, (((0,), (0,)), ((), ())), preferred_element_type=jnp.float32
                )
            )
    return jnp.concatenate(blocks, axis=0).reshape(-1)


def fold_taps(hidden):
    batch, rows_here, extent_x, extent_z, channels = hidden.shape
    shaped = hidden.reshape(batch, rows_here // 2, 2, extent_x // 2, 2, extent_z // 2, 2, channels)
    return shaped.transpose(0, 1, 3, 5, 2, 4, 6, 7).reshape(-1, 8 * channels)


def unfold_taps(values, batch, rows_here, extent_x, extent_z, channels):
    shaped = values.reshape(batch, rows_here // 2, extent_x // 2, extent_z // 2, 2, 2, 2, channels)
    return shaped.transpose(0, 1, 4, 2, 5, 3, 6, 7).reshape(
        batch, rows_here, extent_x, extent_z, channels
    )


def silu_slope(value):
    sigma = jax.nn.sigmoid(value)
    return sigma * (1.0 + value * (1.0 - sigma))


def local(features, w_fine, w_down, mixing, cotangent):
    batch, rows_here, extent_x, extent_z, channels = features.shape
    coarse_ch = w_down.shape[2]
    rimmed = with_halo(features, (("space", 1),), 1)
    xpadded = jnp.pad(rimmed, ((0, 0), (0, 0), (1, 1), (1, 1), (0, 0)))
    act = forward_conv(xpadded, w_fine, rows_here)
    hidden = (features.astype(jnp.float32) + jax.nn.silu(act)).astype(jnp.bfloat16)
    folded = fold_taps(hidden)
    down_matrix = w_down.reshape(8 * channels, coarse_ch)
    coarse = jnp.dot(folded, down_matrix, preferred_element_type=jnp.float32).astype(jnp.bfloat16)
    coarse = coarse.reshape(batch, rows_here // 2, -1)
    columns = lax.all_to_all(coarse, "space", split_axis=2, concat_axis=1, tiled=True)
    mixed = jnp.stack([jnp.dot(mixing, columns[0], preferred_element_type=jnp.float32)])
    bottleneck = (columns.astype(jnp.float32) + jax.nn.silu(mixed)).astype(jnp.bfloat16)
    cot = cotangent.astype(jnp.float32)
    mixed_grad = (cot * silu_slope(mixed)).astype(jnp.bfloat16)
    term = lax.dot_general(
        mixed_grad[0], columns[0], (((1,), (1,)), ((), ())), preferred_element_type=jnp.float32
    )
    spread_list = [
        lax.dot_general(
            mixing, mixed_grad[0], (((0,), (0,)), ((), ())), preferred_element_type=jnp.float32
        )
    ]
    column_grad = (cot + jnp.stack(spread_list)).astype(jnp.bfloat16)
    coarse_grad = lax.all_to_all(column_grad, "space", split_axis=1, concat_axis=2, tiled=True)
    flat_coarse = coarse_grad.reshape(-1, coarse_ch)
    down_terms = lax.dot_general(
        folded, flat_coarse, (((0,), (0,)), ((), ())), preferred_element_type=jnp.float32
    ).reshape(-1)
    hidden_grad = unfold_taps(
        jnp.dot(flat_coarse, down_matrix.T, preferred_element_type=jnp.float32),
        batch,
        rows_here,
        extent_x,
        extent_z,
        channels,
    )
    act_grad = (hidden_grad * silu_slope(act)).astype(jnp.bfloat16)
    grad_rim = with_halo(act_grad, (("space", 1),), 1)
    gpadded = jnp.pad(grad_rim, ((0, 0), (0, 0), (1, 1), (1, 1), (0, 0)))
    spread = transposed_conv(gpadded, w_fine, rows_here)
    feature_grad = (hidden_grad + spread).astype(jnp.bfloat16)
    fine_terms = weight_terms(xpadded, act_grad, rows_here)
    scale = float(
        batch * lax.axis_size("sample") * rows_here * lax.axis_size("space") * extent_x * extent_z
    ) ** (-0.5)
    shares = (
        lax.psum_scatter(fine_terms, "space", scatter_dimension=0, tiled=True),
        lax.psum_scatter(down_terms, "space", scatter_dimension=0, tiled=True),
        lax.psum_scatter(term, "space", scatter_dimension=0, tiled=True),
    )
    totals = lax.psum((shares[0], shares[1], shares[2]), "sample")
    return (bottleneck, feature_grad, totals[0] * scale, totals[1] * scale, totals[2] * scale)


def solution(mesh):
    placed = (
        P(("groups", "sample"), "space", None, None, None),
        P(),
        P(),
        P(),
        P(("groups", "sample"), None, "space"),
    )
    out_specs = (
        P(("groups", "sample"), None, "space"),
        P(("groups", "sample"), "space", None, None, None),
        P(("groups", "space")),
        P(("groups", "space")),
        P(("groups", "space"), None),
    )

    def step(features, w_fine, w_down, mixing, cotangent):
        kernel = functools.partial(fused, mesh) if fused_fits(mesh, features, w_down) else local
        mapped = jax.shard_map(
            kernel, mesh=mesh, in_specs=placed, out_specs=out_specs, check_vma=False
        )
        return mapped(features, w_fine, w_down, mixing, cotangent)

    return step
```

```python
import functools

import jax
import jax.numpy as jnp
from jax import lax
from jax.experimental import pallas as pl
from jax.experimental.pallas import tpu as pltpu
from jax.sharding import PartitionSpec as P

MESH = pl.DeviceIdType.MESH
F32 = jnp.float32
BF16 = jnp.bfloat16
CONTRACT_LAST = (((1,), (1,)), ((), ()))
CONTRACT_FIRST = (((0,), (0,)), ((), ()))


def fused_body(
    cfg,
    features_in, w_fine_in, w_down_in, mixing_in, cotangent_in,
    bottleneck, feature_grad, fine_out, down_out, mixing_out,
    features, w_fine, w_down, mixing, cotangent, load_s,
    x_halo, g_halo, grad16, pad, x3, g3, xt, act, hid, folded, fold_met, folded_t,
    stage, fwd_send, fwd_recv, back_send, back_recv, hid_grad,
    fine16, fine_peer, fine_pair, fine_met, fine_send, fine_recv,
    down16, down_peer, down_send, down_recv,
    mix_send, mix_recv, mix_total, mix_peer,
    fine_half, fine_half_peer, down_half, down_half_peer,
    halo_s, halo_r, fwd_s, fwd_r, back_s, back_r, mix_s, mix_r,
    ghalo_s, ghalo_r, peer_s, peer_r, dpeer_s, dpeer_r,
    pair_s, pair_r, fold_s, fold_r, fine_s, fine_r, down_s, down_r, last_s, last_r,
    gate,
):
    n, ex, ez, ch, cc, scale = cfg
    plane = ex * ez
    hx, hz = ex // 2, ez // 2
    lanes = 128
    rows = hx * hz * cc // lanes // n
    halves = cc // lanes
    fine_rows = 27 * ch // n
    part = fine_send.shape[1]
    fine_step = fine_rows - part
    fine_mine = fine_rows // 2
    down_rows = 8 * ch // n
    down_part = down_rows // 2
    me = lax.axis_index("space")
    core = lax.axis_index("sample")
    other = 1 - core

    def to_space(src, dst, send, recv, who):
        return pltpu.make_async_remote_copy(
            src_ref=src, dst_ref=dst, send_sem=send, recv_sem=recv,
            device_id={"space": who}, device_id_type=MESH,
        )

    def to_peer(src, dst, send, recv):
        return pltpu.make_async_remote_copy(
            src_ref=src, dst_ref=dst, send_sem=send, recv_sem=recv,
            device_id={"sample": other}, device_id_type=MESH,
        )

    has_prev, has_next = me > 0, me < n - 1
    groups = n // 2
    group, side_of = me // 2, lax.rem(me, 2)
    partner = me + 1 - 2 * side_of

    barrier = pltpu.get_barrier_semaphore()
    greeted = 1
    for shift in (-2, -1, 1, 2):
        who = me + shift
        inside = jnp.logical_and(who >= 0, who < n)
        greeted = greeted + inside.astype(jnp.int32)

        @pl.when(inside)
        def _(who=who):
            pl.semaphore_signal(barrier, inc=1, device_id={"space": who}, device_id_type=MESH)

    pl.semaphore_signal(barrier, inc=1, device_id={"sample": other}, device_id_type=MESH)
    loads = [
        pltpu.make_async_copy(source, dest, load_s.at[i])
        for i, (source, dest) in enumerate(
            (
                (features_in, features),
                (w_fine_in, w_fine),
                (w_down_in, w_down),
                (mixing_in, mixing),
                (cotangent_in, cotangent),
            )
        )
    ]
    for load in loads:
        load.start()

    def halo_copies(first, last, halo, send, recv):
        down = to_space(first, halo.at[1], send.at[0], recv.at[1], me - 1)
        up = to_space(last, halo.at[0], send.at[1], recv.at[0], me + 1)
        return down, up

    def start_halo(copies):
        pl.when(has_prev)(copies[0].start)
        pl.when(has_next)(copies[1].start)

    def wait_halo(copies):
        def with_prev():
            copies[0].wait_send()
            copies[1].wait_recv()

        def with_next():
            copies[1].wait_send()
            copies[0].wait_recv()

        pl.when(has_prev)(with_prev)
        pl.when(has_next)(with_next)

    x_copies = halo_copies(features.at[0, 0], features.at[0, 1], x_halo, halo_s, halo_r)
    loads[0].wait()
    pl.semaphore_wait(barrier, greeted)
    start_halo(x_copies)
    gates = ((group > 0, group < groups - 1, me + 2), (group < groups - 1, group > 0, me - 2))
    ends = jnp.logical_or(group == 0, group == groups - 1)

    def await_gate(slot):
        pl.when(gates[slot][0])(lambda: pl.semaphore_wait(gate.at[slot], 1))

    for slot, (_, onward, after) in enumerate(gates):
        pl.when(jnp.logical_not(ends))(lambda slot=slot: await_gate(slot))

        @pl.when(onward)
        def _(slot=slot, after=after):
            pl.semaphore_signal(
                gate.at[slot], inc=1, device_id={"space": after}, device_id_type=MESH
            )

    @pl.when(me == 0)
    def _():
        x_halo[0] = jnp.zeros(x_halo.shape[1:], BF16)
        g_halo[0] = jnp.zeros(g_halo.shape[1:], BF16)

    @pl.when(me == n - 1)
    def _():
        x_halo[1] = jnp.zeros(x_halo.shape[1:], BF16)
        g_halo[1] = jnp.zeros(g_halo.shape[1:], BF16)

    pad[:, :, 0:8, :] = jnp.zeros((2, ex, 8, ch), F32)
    pad[:, :, 8 + ez : 16 + ez, :] = jnp.zeros((2, ex, 8, ch), F32)
    for rim in (0, ex + 1):
        x3[:, rim] = jnp.zeros((4, ez, 3 * ch), BF16)
        g3[:, rim] = jnp.zeros((4, ez, 3 * ch), BF16)

    def spread_rows(dest, index, row, slot):
        pad[slot, :, 8 : 8 + ez, :] = row.astype(F32)
        dest[index, 1 : 1 + ex, :, 0:ch] = pad[slot, :, 7 : 7 + ez, :].astype(BF16)
        dest[index, 1 : 1 + ex, :, ch : 2 * ch] = row
        dest[index, 1 : 1 + ex, :, 2 * ch : 3 * ch] = pad[slot, :, 9 : 9 + ez, :].astype(BF16)

    def window(source, index, shift):
        return source[index, shift : shift + ex].reshape(plane, 3 * ch)

    def taps(sy, sx):
        first = sy * 9 + sx * 3
        return w_fine[first : first + 3].reshape(3 * ch, ch)

    def mm(a, b):
        return jnp.dot(a, b, preferred_element_type=F32)

    spread_rows(x3, 1, features[0, 0], 0)
    spread_rows(x3, 2, features[0, 1], 1)
    loads[1].wait()
    total = None
    for sx in range(3):
        term = mm(window(x3, 1, sx), jnp.concatenate([taps(1, sx), taps(0, sx)], axis=1))
        total = term if total is None else total + term
        total = total + mm(
            window(x3, 2, sx), jnp.concatenate([taps(2, sx), taps(1, sx)], axis=1)
        )
    act[...] = total
    for slot in range(2):
        pl.when(ends)(lambda slot=slot: await_gate(slot))
    wait_halo(x_copies)
    spread_rows(x3, 0, x_halo[0], 0)
    spread_rows(x3, 3, x_halo[1], 1)
    for side in range(2):
        total = act[:, side * ch : (side + 1) * ch]
        for sx in range(3):
            total = total + mm(window(x3, 3 * side, sx), taps(2 * side, sx))
        act[:, side * ch : (side + 1) * ch] = total
        value = features[0, side].reshape(plane, ch).astype(F32) + total * jax.nn.sigmoid(total)
        hid[side] = value.astype(BF16).astype(F32).reshape(hx, 2, ez, ch)

    for t in range(8):
        i, j, k = t // 4, t // 2 % 2, t % 2
        piece = hid[i, :, j, pl.ds(k, hz, stride=2), :].reshape(hx * hz, ch)
        folded[k, :, t // 2 * ch : (t // 2 + 1) * ch] = piece.astype(BF16)
    loads[2].wait()
    coarse = mm(folded[0], jnp.concatenate([w_down[t] for t in range(0, 8, 2)], axis=0))
    coarse = coarse + mm(folded[1], jnp.concatenate([w_down[t] for t in range(1, 8, 2)], axis=0))
    coarse = coarse.astype(BF16).astype(F32)
    for h in range(halves):
        stage[pl.ds(h, hx * hz, stride=halves), :] = coarse[:, h * lanes : (h + 1) * lanes]
    fwd_send[...] = stage[...].astype(BF16).reshape(n, rows, lanes)

    def exchange(src_of, slot, send, recv):
        out = []
        for k in range(1, n):
            who = lax.rem(me + k, n)
            copy = to_space(src_of(who), slot(), send.at[k - 1], recv.at[k - 1], who)
            copy.start()
            out.append(copy)
        return out

    coarse_copies = exchange(
        lambda who: fwd_send.at[who], lambda: fwd_recv.at[me], fwd_s, fwd_r
    )
    fold_copy = to_space(folded.at[1 - side_of], fold_met, fold_s, fold_r, partner)
    fold_copy.start()
    fwd_recv[me] = fwd_send[me]

    loads[3].wait()
    loads[4].wait()
    for sx in range(3):
        for j in range(4):
            xt[sx, :, j * plane : (j + 1) * plane] = window(x3, j, sx).T

    for copy in coarse_copies:
        copy.wait()
    stage[...] = fwd_recv[...].reshape(n * rows, lanes).astype(F32)
    columns = jnp.concatenate([stage[pl.ds(r, n, stride=rows), :] for r in range(rows)], axis=1)
    columns16 = columns.astype(BF16)
    mix = mixing[...]
    mixed = mm(mix, columns16)
    sigma = jax.nn.sigmoid(mixed)
    bottleneck[0] = (columns + mixed * sigma).astype(BF16)
    cot = cotangent[0].astype(F32)
    mixed_grad = (cot * (sigma * (1.0 + mixed * (1.0 - sigma)))).astype(BF16)
    spread = lax.dot_general(mix, mixed_grad, CONTRACT_FIRST, preferred_element_type=F32)
    column_grad = cot + spread
    for r in range(rows):
        stage[pl.ds(r, n, stride=rows), :] = column_grad[:, r * lanes : (r + 1) * lanes]
    back_send[...] = stage[...].astype(BF16).reshape(n, rows, lanes)
    back_copies = exchange(
        lambda who: back_send.at[pl.ds(who // 2 * 2, 2)], lambda: back_recv.at[:, me],
        back_s, back_r,
    )
    for side in range(2):
        back_recv[side, me] = back_send[2 * group + side]
    term = lax.dot_general(mixed_grad, columns16, CONTRACT_LAST, preferred_element_type=F32)
    mix_send[...] = jnp.zeros(mix_send.shape, F32)
    mix_send[:, 0:n] = term
    mix_copies = exchange(lambda who: mix_send, lambda: mix_recv.at[me], mix_s, mix_r)
    mix_recv[me] = mix_send[...]
    value = act[...]
    sig = jax.nn.sigmoid(value)
    act[...] = sig * (1.0 + value * (1.0 - sig))

    fold_copy.wait()
    folded_t[...] = jnp.concatenate([folded[side_of], fold_met[...]], axis=0).T

    def flat_of(side):
        stage[...] = back_recv[side].reshape(n * rows, lanes).astype(F32)
        return jnp.concatenate(
            [stage[pl.ds(h, hx * hz, stride=halves), :] for h in range(halves)], axis=1
        ).astype(BF16)

    for copy in back_copies:
        copy.wait()
    flat = flat_of(side_of)

    for t in range(8):
        i, j, k = t // 4, t // 2 % 2, t % 2
        piece = lax.dot_general(flat, w_down[t], CONTRACT_LAST, preferred_element_type=F32)
        hid_grad[i, :, j, pl.ds(k, hz, stride=2), :] = piece.reshape(hx, hz, ch)
    for side in range(2):
        grad = hid_grad[side].reshape(plane, ch) * act[:, side * ch : (side + 1) * ch]
        grad16[side] = grad.astype(BF16).reshape(ex, ez, ch)
    g_copies = halo_copies(grad16.at[0], grad16.at[1], g_halo, ghalo_s, ghalo_r)

    upper = group >= groups // 2

    def owner(k):
        if k == groups - 1:
            return group
        first, last = k, groups - 1 - k
        first = first + (first >= group).astype(jnp.int32)
        last = last - (last <= group).astype(jnp.int32)
        return jnp.where(upper, first, last)

    def leave(met, outgoing, incoming, send, recv, k):
        to = owner(k)
        if k == groups - 1:
            incoming[group] = met
            return
        step = lax.rem(to - group + groups, groups) - 1
        outgoing[step] = met
        to_space(
            outgoing.at[step], incoming.at[group], send.at[step], recv.at[step], 2 * to + side_of
        ).start()

    def wait_left(outgoing, incoming, send, recv):
        for step in range(groups - 1):
            source = lax.rem(group - 1 - step + groups, groups)
            to_space(
                outgoing.at[step], incoming.at[source], send.at[step], recv.at[step], partner
            ).wait()

    flat_grad = grad16[...].reshape(2 * plane, ch)

    def fine_block(i):
        t = jnp.where(upper, i, 8 - i)
        sy, sx = t // 3, lax.rem(t, 3)
        window_t = xt[sx, :, pl.ds(pl.multiple_of(sy * plane, lanes), 2 * plane)]
        start = pl.multiple_of(t * 3 * ch, lanes)
        fine16[pl.ds(start, 3 * ch), :] = mm(window_t, flat_grad).astype(BF16)

    peer_copies = []

    def fine_to_peer(k):
        for j in range(2):
            who = 2 * owner(k) + j
            start = pl.multiple_of(who * fine_rows + other * fine_step, 16)
            copy = to_peer(
                fine16.at[pl.ds(start, part), :], fine_peer.at[who],
                peer_s.at[2 * k + j], peer_r.at[2 * k + j],
            )
            copy.start()
            peer_copies.append(copy)

    def fine_own(who):
        start = pl.multiple_of(who * fine_rows + core * fine_step, 16)
        return fine16[pl.ds(start, part), :].astype(F32) + fine_peer[who].astype(F32)

    pair_copies = []

    def fine_to_pair(k):
        peer_copies[2 * k].wait()
        peer_copies[2 * k + 1].wait()
        fine_pair[k] = fine_own(2 * owner(k) + 1 - side_of).astype(BF16)
        copy = to_space(fine_pair.at[k], fine_met.at[k], pair_s.at[k], pair_r.at[k], partner)
        copy.start()
        pair_copies.append(copy)

    def pass_on(k):
        pair_copies[k].wait()
        met = fine_own(2 * owner(k) + side_of) + fine_met[k].astype(F32)
        leave(met.astype(BF16), fine_send, fine_recv, fine_s, fine_r, k)

    ready = [-(-(k + 1) * 2 * fine_rows // (3 * ch)) if 2 * k < groups else 9 for k in range(groups)]
    sent = 0
    for i in range(9):
        fine_block(i)
        while sent < groups and ready[sent] <= i + 1:
            fine_to_peer(sent)
            if sent == 0:
                both = jnp.concatenate([flat, flat_of(1 - side_of)], axis=0)
                down16[...] = mm(folded_t[...], both).astype(BF16).reshape(groups, down_rows, cc)
                down_copy = to_peer(
                    down16.at[:, pl.ds(pl.multiple_of(other * down_part, 16), down_part), :],
                    down_peer, dpeer_s, dpeer_r,
                )
                down_copy.start()
            sent += 1
    fine_to_pair(0)
    down_copy.wait()
    for k in range(groups):
        to = owner(k)
        mine = down16[to, pl.ds(pl.multiple_of(core * down_part, 16), down_part), :]
        total = mine.astype(F32) + down_peer[to].astype(F32)
        leave(total.astype(BF16), down_send, down_recv, down_s, down_r, k)
    for k in range(1, groups):
        fine_to_pair(k)

    def turned(i, sx):
        first = i * 9 + sx * 3
        return jnp.concatenate([w_fine[first + 2 - m] for m in range(3)], axis=1)

    def mt(a, b):
        return lax.dot_general(a, b, CONTRACT_LAST, preferred_element_type=F32)

    spread_rows(g3, 1, grad16[0], 0)
    spread_rows(g3, 2, grad16[1], 1)
    total = None
    for sx in range(3):
        term = mt(window(g3, 1, 2 - sx), jnp.concatenate([turned(1, sx), turned(2, sx)], axis=0))
        total = term if total is None else total + term
        total = total + mt(
            window(g3, 2, 2 - sx), jnp.concatenate([turned(0, sx), turned(1, sx)], axis=0)
        )
    act[...] = total
    pass_on(0)
    start_halo(g_copies)
    for k in range(1, groups):
        pass_on(k)
    wait_halo(g_copies)
    spread_rows(g3, 0, g_halo[0], 0)
    spread_rows(g3, 3, g_halo[1], 1)
    for side in range(2):
        total = act[:, side * ch : (side + 1) * ch] + hid_grad[side].reshape(plane, ch)
        for sx in range(3):
            total = total + mt(window(g3, 3 * side, 2 - sx), turned(2 - 2 * side, sx))
        feature_grad[0, side] = total.astype(BF16).reshape(ex, ez, ch)

    for copy in mix_copies:
        copy.wait()
    mix_total[...] = sum(mix_recv[s] for s in range(n)) * scale
    mix_swap = to_peer(mix_total, mix_peer, last_s.at[0], last_r.at[0])
    mix_swap.start()

    wait_left(down_send, down_recv, down_s, down_r)
    value = sum(down_recv[s].astype(F32) for s in range(groups)) * scale
    for h in range(halves):
        down_half[pl.ds(h, down_part, stride=halves), :] = value[:, h * lanes : (h + 1) * lanes]
    down_swap = to_peer(down_half, down_half_peer, last_s.at[1], last_r.at[1])
    down_swap.start()

    wait_left(fine_send, fine_recv, fine_s, fine_r)
    value = sum(fine_recv[s].astype(F32) for s in range(groups)) * scale
    begin = fine_mine - fine_step
    fine_half[...] = jnp.where(core == 0, value[0:fine_mine], value[begin : begin + fine_mine])
    fine_swap = to_peer(fine_half, fine_half_peer, last_s.at[2], last_r.at[2])
    fine_swap.start()

    down_len = down_part * halves
    fine_out[pl.ds(pl.multiple_of(core * fine_mine, 8), fine_mine), :] = fine_half[...]
    down_out[pl.ds(pl.multiple_of(core * down_len, 8), down_len), :] = down_half[...]
    mix_swap.wait()
    mix_total[...] = mix_total[...] + mix_peer[...]
    mixing_out[...] = mix_total[pl.ds(me, 1), 0:n]
    down_swap.wait()
    down_out[pl.ds(pl.multiple_of(other * down_len, 8), down_len), :] = down_half_peer[...]
    fine_swap.wait()
    fine_out[pl.ds(pl.multiple_of(other * fine_mine, 8), fine_mine), :] = fine_half_peer[...]


def put_out(*refs):
    sources, dests, done = refs[:5], refs[5:10], refs[10]
    copies = [
        pltpu.make_async_copy(source, dest, done.at[i])
        for i, (source, dest) in enumerate(zip(sources, dests))
    ]
    for copy in copies:
        copy.start()
    for copy in copies:
        copy.wait()


def fused_fits(mesh, features, w_down):
    n = mesh.shape["space"]
    batch, ny, ex, ez, ch = features.shape
    cc = w_down.shape[2]
    spots = ex * ez // 4
    return (
        batch == mesh.shape["groups"] * mesh.shape["sample"]
        and ny == 2 * n
        and mesh.shape["sample"] == 2
        and n == w_down.shape[0]
        and ch == 128
        and cc % 128 == 0
        and ez % 16 == 0
        and ex % 2 == 0
        and spots % 8 == 0
        and (spots * cc) % (n * 128 * 16) == 0
        and (27 * ch) % (n * 16) == 0
        and (8 * ch) % (n * 32) == 0
    )


def fused(mesh, features, w_fine, w_down, mixing, cotangent):
    n = lax.axis_size("space")
    _, _, ex, ez, ch = features.shape
    cc = w_down.shape[2]
    batch = lax.axis_size("sample")
    scale = float(batch * 2 * n * ex * ez) ** (-0.5)
    plane, spots, lanes = ex * ez, ex * ez // 4, 128
    rows = spots * cc // lanes // n
    fine_rows, down_rows = 27 * ch // n, 8 * ch // n
    half = fine_rows // 2
    part = -(-half // 16) * 16
    down_part = down_rows // 2
    down_len = down_part * cc // lanes
    vm = pltpu.VMEM
    dma = pltpu.SemaphoreType.DMA
    groups = n // 2
    arrays = (features, w_fine, w_down, mixing, cotangent)
    scratch = [
        *[vm(array.shape, BF16) for array in arrays], dma((5,)),
        vm((2, ex, ez, ch), BF16), vm((2, ex, ez, ch), BF16), vm((2, ex, ez, ch), BF16),
        vm((2, ex, ez + 16, ch), F32),
        vm((4, ex + 2, ez, 3 * ch), BF16), vm((4, ex + 2, ez, 3 * ch), BF16),
        vm((3, 3 * ch, 4 * plane), BF16),
        vm((plane, 2 * ch), F32),
        vm((2, ex // 2, 2, ez, ch), F32),
        vm((2, spots, 4 * ch), BF16), vm((spots, 4 * ch), BF16), vm((4 * ch, 2 * spots), BF16),
        vm((n * rows, lanes), F32),
        vm((n, rows, lanes), BF16), vm((n, rows, lanes), BF16),
        vm((n, rows, lanes), BF16), vm((2, n, rows, lanes), BF16),
        vm((2, ex // 2, 2, ez, ch), F32),
        vm((27 * ch, ch), BF16),
        vm((n, part, ch), BF16), *[vm((groups, part, ch), BF16)] * 4,
        vm((groups, down_rows, cc), BF16), *[vm((groups, down_part, cc), BF16)] * 3,
        vm((n, lanes), F32), vm((n, n, lanes), F32), vm((n, lanes), F32), vm((n, lanes), F32),
        vm((half, ch), F32), vm((half, ch), F32),
        vm((down_len, lanes), F32), vm((down_len, lanes), F32),
        dma((2,)), dma((2,)), dma((n - 1,)), dma((n - 1,)), dma((n - 1,)), dma((n - 1,)),
        dma((n - 1,)), dma((n - 1,)),
        dma((2,)), dma((2,)), dma((n,)), dma((n,)), dma, dma,
        *[dma((groups,))] * 2, dma, dma,
        *[dma((groups - 1,))] * 4, dma((3,)), dma((3,)),
        pltpu.SemaphoreType.REGULAR((2,)),
    ]
    spec = pl.BlockSpec(memory_space=pltpu.VMEM)
    far = pl.BlockSpec(memory_space=pltpu.HBM)
    shapes = (
        jax.ShapeDtypeStruct(cotangent.shape, BF16),
        jax.ShapeDtypeStruct(features.shape, BF16),
        jax.ShapeDtypeStruct((fine_rows, ch), F32),
        jax.ShapeDtypeStruct((down_rows * cc // lanes, lanes), F32),
        jax.ShapeDtypeStruct((1, n), F32),
    )
    results = pl.pallas_call(
        functools.partial(fused_body, (n, ex, ez, ch, cc, scale)),
        out_shape=shapes,
        in_specs=[far] * 5,
        out_specs=tuple([spec] * 5),
        scratch_shapes=scratch,
        compiler_params=pltpu.CompilerParams(
            collective_id=0, has_side_effects=True, vmem_limit_bytes=65472 * 1024
        ),
    )(*arrays)
    a, b, c, d, e = pl.pallas_call(
        put_out,
        out_shape=shapes,
        in_specs=[spec] * 5,
        out_specs=tuple([far] * 5),
        scratch_shapes=[dma((5,))],
        compiler_params=pltpu.CompilerParams(vmem_limit_bytes=65472 * 1024),
    )(*results)
    return a, b, c.reshape(-1), d.reshape(-1), e


def with_halo(array, sides, width):
    for axis, dim in sides:
        devices, length = (lax.axis_size(axis), array.shape[dim])
        up = [(i, (i + 1) % devices) for i in range(devices - 1)]
        down = [(j, i) for i, j in up]
        last = lax.slice_in_dim(array, length - width, length, axis=dim)
        initial = lax.slice_in_dim(array, 0, width, axis=dim)
        before = lax.ppermute(last, axis, up)
        after = lax.ppermute(initial, axis, down)
        array = jnp.concatenate([before, array, after], axis=dim)
    return array


def forward_conv(padded, weight, count):
    extent_x = padded.shape[2] - 2
    extent_z = padded.shape[3] - 2
    channels = padded.shape[4]
    total = None
    for shift_y in range(3):
        for shift_x in range(3):
            pieces = [
                padded[
                    :,
                    shift_y : shift_y + count,
                    shift_x : shift_x + extent_x,
                    shift_z : shift_z + extent_z,
                    :,
                ]
                for shift_z in range(3)
            ]
            stacked = jnp.concatenate(pieces, axis=-1).reshape(-1, 3 * channels)
            first = shift_y * 9 + shift_x * 3
            kernel = weight[first : first + 3].reshape(3 * channels, weight.shape[2])
            term = jnp.dot(stacked, kernel, preferred_element_type=jnp.float32)
            total = term if total is None else total + term
    return total.reshape(padded.shape[0], count, extent_x, extent_z, weight.shape[2])


def transposed_conv(padded, weight, count):
    extent_x = padded.shape[2] - 2
    extent_z = padded.shape[3] - 2
    channels = padded.shape[4]
    total = None
    for shift_y in range(3):
        for shift_x in range(3):
            pieces = [
                padded[
                    :,
                    2 - shift_y : 2 - shift_y + count,
                    2 - shift_x : 2 - shift_x + extent_x,
                    2 - shift_z : 2 - shift_z + extent_z,
                    :,
                ]
                for shift_z in range(3)
            ]
            stacked = jnp.concatenate(pieces, axis=-1).reshape(-1, 3 * channels)
            first = shift_y * 9 + shift_x * 3
            kernel = jnp.swapaxes(weight[first : first + 3], 1, 2).reshape(
                3 * channels, weight.shape[1]
            )
            term = jnp.dot(stacked, kernel, preferred_element_type=jnp.float32)
            total = term if total is None else total + term
    return total.reshape(padded.shape[0], count, extent_x, extent_z, weight.shape[1])


def weight_terms(padded, grad, count):
    extent_x = padded.shape[2] - 2
    extent_z = padded.shape[3] - 2
    channels = padded.shape[4]
    flat_grad = grad.reshape(-1, grad.shape[4])
    blocks = []
    for shift_y in range(3):
        for shift_x in range(3):
            pieces = [
                padded[
                    :,
                    shift_y : shift_y + count,
                    shift_x : shift_x + extent_x,
                    shift_z : shift_z + extent_z,
                    :,
                ]
                for shift_z in range(3)
            ]
            stacked = jnp.concatenate(pieces, axis=-1).reshape(-1, 3 * channels)
            blocks.append(
                lax.dot_general(
                    stacked, flat_grad, (((0,), (0,)), ((), ())), preferred_element_type=jnp.float32
                )
            )
    return jnp.concatenate(blocks, axis=0).reshape(-1)


def fold_taps(hidden):
    batch, rows_here, extent_x, extent_z, channels = hidden.shape
    shaped = hidden.reshape(batch, rows_here // 2, 2, extent_x // 2, 2, extent_z // 2, 2, channels)
    return shaped.transpose(0, 1, 3, 5, 2, 4, 6, 7).reshape(-1, 8 * channels)


def unfold_taps(values, batch, rows_here, extent_x, extent_z, channels):
    shaped = values.reshape(batch, rows_here // 2, extent_x // 2, extent_z // 2, 2, 2, 2, channels)
    return shaped.transpose(0, 1, 4, 2, 5, 3, 6, 7).reshape(
        batch, rows_here, extent_x, extent_z, channels
    )


def silu_slope(value):
    sigma = jax.nn.sigmoid(value)
    return sigma * (1.0 + value * (1.0 - sigma))


def local(features, w_fine, w_down, mixing, cotangent):
    batch, rows_here, extent_x, extent_z, channels = features.shape
    coarse_ch = w_down.shape[2]
    rimmed = with_halo(features, (("space", 1),), 1)
    xpadded = jnp.pad(rimmed, ((0, 0), (0, 0), (1, 1), (1, 1), (0, 0)))
    act = forward_conv(xpadded, w_fine, rows_here)
    hidden = (features.astype(jnp.float32) + jax.nn.silu(act)).astype(jnp.bfloat16)
    folded = fold_taps(hidden)
    down_matrix = w_down.reshape(8 * channels, coarse_ch)
    coarse = jnp.dot(folded, down_matrix, preferred_element_type=jnp.float32).astype(jnp.bfloat16)
    coarse = coarse.reshape(batch, rows_here // 2, -1)
    columns = lax.all_to_all(coarse, "space", split_axis=2, concat_axis=1, tiled=True)
    mixed = jnp.stack([jnp.dot(mixing, columns[0], preferred_element_type=jnp.float32)])
    bottleneck = (columns.astype(jnp.float32) + jax.nn.silu(mixed)).astype(jnp.bfloat16)
    cot = cotangent.astype(jnp.float32)
    mixed_grad = (cot * silu_slope(mixed)).astype(jnp.bfloat16)
    term = lax.dot_general(
        mixed_grad[0], columns[0], (((1,), (1,)), ((), ())), preferred_element_type=jnp.float32
    )
    spread_list = [
        lax.dot_general(
            mixing, mixed_grad[0], (((0,), (0,)), ((), ())), preferred_element_type=jnp.float32
        )
    ]
    column_grad = (cot + jnp.stack(spread_list)).astype(jnp.bfloat16)
    coarse_grad = lax.all_to_all(column_grad, "space", split_axis=1, concat_axis=2, tiled=True)
    flat_coarse = coarse_grad.reshape(-1, coarse_ch)
    down_terms = lax.dot_general(
        folded, flat_coarse, (((0,), (0,)), ((), ())), preferred_element_type=jnp.float32
    ).reshape(-1)
    hidden_grad = unfold_taps(
        jnp.dot(flat_coarse, down_matrix.T, preferred_element_type=jnp.float32),
        batch,
        rows_here,
        extent_x,
        extent_z,
        channels,
    )
    act_grad = (hidden_grad * silu_slope(act)).astype(jnp.bfloat16)
    grad_rim = with_halo(act_grad, (("space", 1),), 1)
    gpadded = jnp.pad(grad_rim, ((0, 0), (0, 0), (1, 1), (1, 1), (0, 0)))
    spread = transposed_conv(gpadded, w_fine, rows_here)
    feature_grad = (hidden_grad + spread).astype(jnp.bfloat16)
    fine_terms = weight_terms(xpadded, act_grad, rows_here)
    scale = float(
        batch * lax.axis_size("sample") * rows_here * lax.axis_size("space") * extent_x * extent_z
    ) ** (-0.5)
    shares = (
        lax.psum_scatter(fine_terms, "space", scatter_dimension=0, tiled=True),
        lax.psum_scatter(down_terms, "space", scatter_dimension=0, tiled=True),
        lax.psum_scatter(term, "space", scatter_dimension=0, tiled=True),
    )
    totals = lax.psum((shares[0], shares[1], shares[2]), "sample")
    return (bottleneck, feature_grad, totals[0] * scale, totals[1] * scale, totals[2] * scale)


def solution(mesh):
    placed = (
        P(("groups", "sample"), "space", None, None, None),
        P(),
        P(),
        P(),
        P(("groups", "sample"), None, "space"),
    )
    out_specs = (
        P(("groups", "sample"), None, "space"),
        P(("groups", "sample"), "space", None, None, None),
        P(("groups", "space")),
        P(("groups", "space")),
        P(("groups", "space"), None),
    )

    def step(features, w_fine, w_down, mixing, cotangent):
        kernel = functools.partial(fused, mesh) if fused_fits(mesh, features, w_down) else local
        mapped = jax.shard_map(
            kernel, mesh=mesh, in_specs=placed, out_specs=out_specs, check_vma=False
        )
        return mapped(features, w_fine, w_down, mixing, cotangent)

    return step
```

```python
import functools

import jax
import jax.numpy as jnp
from jax import lax
from jax.experimental import pallas as pl
from jax.experimental.pallas import tpu as pltpu
from jax.sharding import PartitionSpec as P

MESH = pl.DeviceIdType.MESH
F32 = jnp.float32
BF16 = jnp.bfloat16
CONTRACT_LAST = (((1,), (1,)), ((), ()))
CONTRACT_FIRST = (((0,), (0,)), ((), ()))


def fused_body(
    cfg,
    features_in, w_fine_in, w_down_in, mixing_in, cotangent_in,
    bottleneck, feature_grad, fine_out, down_out, mixing_out,
    features, w_fine, w_down, mixing, cotangent, load_s,
    x_halo, x_far, g_halo, grad16, pad, x3, g3, xt, act, far, hid, folded, fold_met, folded_t,
    stage, fwd_send, fwd_recv, back_send, back_recv, hid_grad,
    fine16, fine_peer, fine_send, fine_recv, fine_keep,
    fold_peer, back_peer, down16, down_recv,
    mix_send, mix_recv, mix_total, mix_peer,
    fine_half, fine_half_peer, down_half, down_half_peer,
    halo_s, halo_r, fwd_s, fwd_r, back_s, back_r, mix_s, mix_r,
    xfar_s, xfar_r, peer_s, peer_r, dpeer_s, dpeer_r,
    fold_s, fold_r, turn_s, turn_r, fine_s, fine_r, down_s, down_r, last_s, last_r,
    gate,
):
    n, ex, ez, ch, cc, scale = cfg
    plane = ex * ez
    hx, hz = ex // 2, ez // 2
    lanes = 128
    rows = hx * hz * cc // lanes // n
    halves = cc // lanes
    fine_rows = 27 * ch // n
    part = fine_send.shape[1]
    fine_step = fine_rows - part
    fine_mine = fine_rows // 2
    down_rows = 8 * ch // n
    down_part = down_rows // 2
    me = lax.axis_index("space")
    core = lax.axis_index("sample")
    other = 1 - core

    def to_space(src, dst, send, recv, who):
        return pltpu.make_async_remote_copy(
            src_ref=src, dst_ref=dst, send_sem=send, recv_sem=recv,
            device_id={"space": who}, device_id_type=MESH,
        )

    def to_peer(src, dst, send, recv):
        return pltpu.make_async_remote_copy(
            src_ref=src, dst_ref=dst, send_sem=send, recv_sem=recv,
            device_id={"sample": other}, device_id_type=MESH,
        )

    has_prev, has_next = me > 0, me < n - 1
    groups = n // 2
    group, side_of = me // 2, lax.rem(me, 2)
    partner = me + 1 - 2 * side_of

    barrier = pltpu.get_barrier_semaphore()
    greeted = 1
    for shift in (-2, -1, 1, 2):
        who = me + shift
        inside = jnp.logical_and(who >= 0, who < n)
        greeted = greeted + inside.astype(jnp.int32)

        @pl.when(inside)
        def _(who=who):
            pl.semaphore_signal(barrier, inc=1, device_id={"space": who}, device_id_type=MESH)

    pl.semaphore_signal(barrier, inc=1, device_id={"sample": other}, device_id_type=MESH)
    loads = [
        pltpu.make_async_copy(source, dest, load_s.at[i])
        for i, (source, dest) in enumerate(
            (
                (features_in, features),
                (w_fine_in, w_fine),
                (w_down_in, w_down),
                (mixing_in, mixing),
                (cotangent_in, cotangent),
            )
        )
    ]
    for load in loads:
        load.start()

    def halo_copies(first, last, halo, send, recv):
        down = to_space(first, halo.at[1], send.at[0], recv.at[1], me - 1)
        up = to_space(last, halo.at[0], send.at[1], recv.at[0], me + 1)
        return down, up

    def start_halo(copies):
        pl.when(has_prev)(copies[0].start)
        pl.when(has_next)(copies[1].start)

    def wait_halo(copies):
        def with_prev():
            copies[0].wait_send()
            copies[1].wait_recv()

        def with_next():
            copies[1].wait_send()
            copies[0].wait_recv()

        pl.when(has_prev)(with_prev)
        pl.when(has_next)(with_next)

    x_copies = halo_copies(features.at[0, 0], features.at[0, 1], x_halo, halo_s, halo_r)
    loads[0].wait()
    pl.semaphore_wait(barrier, greeted)
    start_halo(x_copies)
    gates = ((group > 0, group < groups - 1, me + 2), (group < groups - 1, group > 0, me - 2))
    ends = jnp.logical_or(group == 0, group == groups - 1)

    def await_gate(slot):
        pl.when(gates[slot][0])(lambda: pl.semaphore_wait(gate.at[slot], 1))

    for slot, (_, onward, after) in enumerate(gates):
        pl.when(jnp.logical_not(ends))(lambda slot=slot: await_gate(slot))

        @pl.when(onward)
        def _(slot=slot, after=after):
            pl.semaphore_signal(
                gate.at[slot], inc=1, device_id={"space": after}, device_id_type=MESH
            )

    @pl.when(me == 0)
    def _():
        x_halo[0] = jnp.zeros(x_halo.shape[1:], BF16)
        x_far[0] = jnp.zeros(x_far.shape[1:], BF16)
        g_halo[0] = jnp.zeros(g_halo.shape[1:], BF16)

    @pl.when(me == n - 1)
    def _():
        x_halo[1] = jnp.zeros(x_halo.shape[1:], BF16)
        x_far[1] = jnp.zeros(x_far.shape[1:], BF16)
        g_halo[1] = jnp.zeros(g_halo.shape[1:], BF16)

    pad[:, :, 0:8, :] = jnp.zeros((2, ex, 8, ch), F32)
    pad[:, :, 8 + ez : 16 + ez, :] = jnp.zeros((2, ex, 8, ch), F32)
    for rim in (0, ex + 1):
        x3[:, rim] = jnp.zeros((6, ez, 3 * ch), BF16)
        g3[:, rim] = jnp.zeros((4, ez, 3 * ch), BF16)

    def spread_rows(dest, index, row, slot):
        pad[slot, :, 8 : 8 + ez, :] = row.astype(F32)
        dest[index, 1 : 1 + ex, :, 0:ch] = pad[slot, :, 7 : 7 + ez, :].astype(BF16)
        dest[index, 1 : 1 + ex, :, ch : 2 * ch] = row
        dest[index, 1 : 1 + ex, :, 2 * ch : 3 * ch] = pad[slot, :, 9 : 9 + ez, :].astype(BF16)

    def window(source, index, shift):
        return source[index, shift : shift + ex].reshape(plane, 3 * ch)

    def taps(sy, sx):
        first = sy * 9 + sx * 3
        return w_fine[first : first + 3].reshape(3 * ch, ch)

    def mm(a, b):
        return jnp.dot(a, b, preferred_element_type=F32)

    spread_rows(x3, 1, features[0, 0], 0)
    spread_rows(x3, 2, features[0, 1], 1)
    loads[1].wait()
    total = None
    for sx in range(3):
        term = mm(window(x3, 1, sx), jnp.concatenate([taps(1, sx), taps(0, sx)], axis=1))
        total = term if total is None else total + term
        total = total + mm(
            window(x3, 2, sx), jnp.concatenate([taps(2, sx), taps(1, sx)], axis=1)
        )
    act[...] = total
    for slot in range(2):
        pl.when(ends)(lambda slot=slot: await_gate(slot))
    wait_halo(x_copies)
    spread_rows(x3, 0, x_halo[0], 0)
    spread_rows(x3, 3, x_halo[1], 1)
    for side in range(2):
        total = act[:, side * ch : (side + 1) * ch]
        for sx in range(3):
            total = total + mm(window(x3, 3 * side, sx), taps(2 * side, sx))
        act[:, side * ch : (side + 1) * ch] = total
        value = features[0, side].reshape(plane, ch).astype(F32) + total * jax.nn.sigmoid(total)
        hid[side] = value.astype(BF16).astype(F32).reshape(hx, 2, ez, ch)

    for t in range(8):
        i, j, k = t // 4, t // 2 % 2, t % 2
        piece = hid[i, :, j, pl.ds(k, hz, stride=2), :].reshape(hx * hz, ch)
        folded[k, :, t // 2 * ch : (t // 2 + 1) * ch] = piece.astype(BF16)
    loads[2].wait()
    coarse = mm(folded[0], jnp.concatenate([w_down[t] for t in range(0, 8, 2)], axis=0))
    coarse = coarse + mm(folded[1], jnp.concatenate([w_down[t] for t in range(1, 8, 2)], axis=0))
    coarse = coarse.astype(BF16).astype(F32)
    for h in range(halves):
        stage[pl.ds(h, hx * hz, stride=halves), :] = coarse[:, h * lanes : (h + 1) * lanes]
    fwd_send[...] = stage[...].astype(BF16).reshape(n, rows, lanes)

    def exchange(src_of, slot, send, recv):
        out = []
        for k in range(1, n):
            who = lax.rem(me + k, n)
            copy = to_space(src_of(who), slot(), send.at[k - 1], recv.at[k - 1], who)
            copy.start()
            out.append(copy)
        return out

    def first_row(who):
        return jnp.clip(who - 1, 0, n - 3)

    coarse_copies = exchange(
        lambda who: fwd_send.at[who], lambda: fwd_recv.at[me], fwd_s, fwd_r
    )
    fold_copy = to_space(folded.at[1 - side_of], fold_met, fold_s, fold_r, partner)
    fold_copy.start()
    rim_copies = halo_copies(features.at[0, 1], features.at[0, 0], x_far, xfar_s, xfar_r)
    start_halo(rim_copies)
    fwd_recv[me] = fwd_send[me]

    loads[3].wait()
    loads[4].wait()
    for sx in range(3):
        for j in range(4):
            xt[sx, :, j * plane : (j + 1) * plane] = window(x3, j, sx).T

    for copy in coarse_copies:
        copy.wait()
    stage[...] = fwd_recv[...].reshape(n * rows, lanes).astype(F32)
    columns = jnp.concatenate([stage[pl.ds(r, n, stride=rows), :] for r in range(rows)], axis=1)
    columns16 = columns.astype(BF16)
    mix = mixing[...]
    mixed = mm(mix, columns16)
    sigma = jax.nn.sigmoid(mixed)
    bottleneck[0] = (columns + mixed * sigma).astype(BF16)
    cot = cotangent[0].astype(F32)
    mixed_grad = (cot * (sigma * (1.0 + mixed * (1.0 - sigma)))).astype(BF16)
    spread = lax.dot_general(mix, mixed_grad, CONTRACT_FIRST, preferred_element_type=F32)
    column_grad = cot + spread
    for r in range(rows):
        stage[pl.ds(r, n, stride=rows), :] = column_grad[:, r * lanes : (r + 1) * lanes]
    back_send[...] = stage[...].astype(BF16).reshape(n, rows, lanes)
    back_copies = exchange(
        lambda who: back_send.at[pl.ds(first_row(who), 3)], lambda: back_recv.at[:, me],
        back_s, back_r,
    )
    base = first_row(me)
    for row in range(3):
        back_recv[row, me] = back_send[base + row]
    term = lax.dot_general(mixed_grad, columns16, CONTRACT_LAST, preferred_element_type=F32)
    mix_send[...] = jnp.zeros(mix_send.shape, F32)
    mix_send[:, 0:n] = term
    mix_copies = exchange(lambda who: mix_send, lambda: mix_recv.at[me], mix_s, mix_r)
    mix_recv[me] = mix_send[...]
    value = act[...]
    sig = jax.nn.sigmoid(value)
    act[...] = sig * (1.0 + value * (1.0 - sig))

    wait_halo(rim_copies)
    spread_rows(x3, 4, x_far[0], 0)
    spread_rows(x3, 5, x_far[1], 1)
    for side, near_rows in enumerate(((4, 0, 1), (2, 3, 5))):
        total = None
        for sy, index in enumerate(near_rows):
            for sx in range(3):
                term = mm(window(x3, index, sx), taps(sy, sx))
                total = term if total is None else total + term
        sig = jax.nn.sigmoid(total)
        far[:, side * ch : (side + 1) * ch] = sig * (1.0 + total * (1.0 - sig))

    fold_copy.wait()
    turned_taps = jnp.concatenate([folded[side_of], fold_met[...]], axis=0).T
    folded_t[...] = turned_taps.reshape(groups, ch, 2 * hx * hz)
    turn_copy = to_peer(
        folded_t.at[:, pl.ds(pl.multiple_of(other * down_part, 16), down_part), :],
        fold_peer, turn_s, turn_r,
    )
    turn_copy.start()

    def flat_of(source, side):
        stage[...] = source[side].reshape(n * rows, lanes).astype(F32)
        return jnp.concatenate(
            [stage[pl.ds(h, hx * hz, stride=halves), :] for h in range(halves)], axis=1
        ).astype(BF16)

    for copy in back_copies:
        copy.wait()
    flat_copy = to_peer(
        back_recv.at[pl.ds(2 * group - base, 2)], back_peer, dpeer_s, dpeer_r
    )
    flat_copy.start()
    flat = flat_of(back_recv, me - base)

    for t in range(8):
        i, j, k = t // 4, t // 2 % 2, t % 2
        piece = lax.dot_general(flat, w_down[t], CONTRACT_LAST, preferred_element_type=F32)
        hid_grad[i, :, j, pl.ds(k, hz, stride=2), :] = piece.reshape(hx, hz, ch)
    for side in range(2):
        grad = hid_grad[side].reshape(plane, ch) * act[:, side * ch : (side + 1) * ch]
        grad16[side] = grad.astype(BF16).reshape(ex, ez, ch)
    def send_down():
        turn_copy.wait()
        flat_copy.wait()
        taps_here = folded_t[:, pl.ds(pl.multiple_of(core * down_part, 16), down_part), :]
        left = jnp.concatenate([taps_here, fold_peer[...]], axis=2)
        right = jnp.concatenate(
            [
                flat, flat_of(back_recv, partner - base),
                flat_of(back_peer, side_of), flat_of(back_peer, 1 - side_of),
            ],
            axis=0,
        )
        total = mm(left.reshape(groups * down_part, 4 * hx * hz), right)
        down16[...] = total.astype(BF16).reshape(groups, down_part, cc)

    def start_down():
        for step in range(groups - 1):
            to = lax.rem(group + step + 1, groups)
            to_space(
                down16.at[to], down_recv.at[group], down_s.at[step], down_r.at[step],
                2 * to + side_of,
            ).start()
        down_recv[group] = down16[group]

    def wait_down():
        for step in range(groups - 1):
            source = lax.rem(group - 1 - step + groups, groups)
            to_space(
                down16.at[source], down_recv.at[source], down_s.at[step], down_r.at[step], partner
            ).wait()

    flip = group + 1 - 2 * lax.rem(group, 2)
    across = lax.rem(group + 2, groups)
    owners = (lax.rem(flip + 2, groups), across, flip, group)
    orders = ((8, 7, 6, 5, 4, 3, 2, 1, 0), (6, 5, 4, 8, 7, 2, 1, 0, 3))
    orders = orders + tuple(tuple(8 - t for t in order) for order in orders[::-1])

    flat_grad = grad16[...].reshape(2 * plane, ch)

    def fine_block(i):
        t = orders[0][i]
        for g in range(1, groups):
            t = jnp.where(group == g, orders[g][i], t)
        sy, sx = t // 3, lax.rem(t, 3)
        window_t = xt[sx, :, pl.ds(pl.multiple_of(sy * plane, lanes), 2 * plane)]
        start = pl.multiple_of(t * 3 * ch, lanes)
        fine16[pl.ds(start, 3 * ch), :] = mm(window_t, flat_grad).astype(BF16)

    peer_copies = []

    def fine_to_peer(k):
        for j in range(2):
            who = 2 * owners[k] + j
            start = pl.multiple_of(who * fine_rows + other * fine_step, 16)
            copy = to_peer(
                fine16.at[pl.ds(start, part), :], fine_peer.at[who],
                peer_s.at[2 * k + j], peer_r.at[2 * k + j],
            )
            copy.start()
            peer_copies.append(copy)

    def fine_own(who):
        start = pl.multiple_of(who * fine_rows + core * fine_step, 16)
        return fine16[pl.ds(start, part), :].astype(F32) + fine_peer[who].astype(F32)

    pieces = 2
    height = part // pieces

    def own_rows(who, first, count):
        start = pl.multiple_of(who * fine_rows + core * fine_step + first, 16)
        mine = fine16[pl.ds(start, count), :].astype(F32)
        return mine + fine_peer[who, first : first + count].astype(F32)

    def slot_copy(slot, piece, who):
        rows_of = pl.ds(piece * height, height)
        index = slot * pieces + piece
        return to_space(
            fine_send.at[slot, rows_of], fine_recv.at[slot, rows_of],
            fine_s.at[index], fine_r.at[index], who,
        )

    def whole_copy(slot, who):
        return to_space(
            fine_send.at[slot], fine_recv.at[slot],
            fine_s.at[slot * pieces], fine_r.at[slot * pieces], who,
        )

    far_copies = [[None] * 3 for _ in range(pieces)]

    def met_peer(k):
        peer_copies[2 * k].wait()
        peer_copies[2 * k + 1].wait()

    def far_piece(piece, first, k):
        to = 2 * owners[k]
        targets = ((2, 1 - side_of), (1, side_of)) if k == 0 else ((0, 1 - side_of),)
        for slot, side in targets:
            fine_send[slot, first : first + height] = own_rows(to + side, first, height).astype(BF16)
            at = (partner, 2 * flip + side_of, 2 * flip + 1 - side_of)[slot]
            copy = slot_copy(slot, piece, at)
            copy.start()
            far_copies[piece][slot] = copy
        if k == 1:
            fine_keep[0, first : first + height] = own_rows(to + side_of, first, height)

    near_copies = {}

    def near_piece(k):
        met_peer(k)
        fine_send[k + 1] = fine_own(2 * owners[k] + 1 - side_of).astype(BF16)
        near_copies[k + 1] = whole_copy(k + 1, partner)
        near_copies[k + 1].start()
        fine_keep[k - 1] = fine_own(2 * owners[k] + side_of)

    def near_on():
        near_copies[3].wait()
        fine_send[5] = (fine_keep[1] + fine_recv[3].astype(F32)).astype(BF16)
        near_copies[5] = whole_copy(5, 2 * flip + side_of)
        near_copies[5].start()

    cross_copies = []

    def cross_piece(piece):
        for copy in far_copies[piece]:
            copy.wait_recv()
        first = piece * height
        rows_of = slice(first, first + height)
        total = fine_keep[0, rows_of] + sum(fine_recv[j, rows_of].astype(F32) for j in range(3))
        fine_send[6, rows_of] = total.astype(BF16)
        copy = slot_copy(6, piece, 2 * across + side_of)
        copy.start()
        cross_copies.append(copy)

    ready = {3: 0, 5: 1, 8: 2, 9: 3}
    for i in range(9):
        fine_block(i)
        if i + 1 in ready:
            fine_to_peer(ready[i + 1])
    met_peer(0)
    far_piece(0, 0, 0)
    met_peer(1)
    far_piece(0, 0, 1)
    for piece in range(1, pieces):
        far_piece(piece, piece * height, 0)
        far_piece(piece, piece * height, 1)
    near_piece(2)
    send_down()
    start_down()

    def turned(i, sx):
        first = i * 9 + sx * 3
        return jnp.concatenate([w_fine[first + 2 - m] for m in range(3)], axis=1)

    def mt(a, b):
        return lax.dot_general(a, b, CONTRACT_LAST, preferred_element_type=F32)

    spread_rows(g3, 1, grad16[0], 0)
    spread_rows(g3, 2, grad16[1], 1)
    total = None
    for sx in range(3):
        term = mt(window(g3, 1, 2 - sx), jnp.concatenate([turned(1, sx), turned(2, sx)], axis=0))
        total = term if total is None else total + term
        total = total + mt(
            window(g3, 2, 2 - sx), jnp.concatenate([turned(0, sx), turned(1, sx)], axis=0)
        )
    act[...] = total
    for side, inside in enumerate((has_prev, has_next)):
        index = me - base + 2 * side - 1
        flat_far = flat_of(back_recv, jnp.clip(index, 0, 2))
        for t in range(4):
            j, k = t // 2, t % 2
            piece = lax.dot_general(
                flat_far, w_down[4 * (1 - side) + t], CONTRACT_LAST, preferred_element_type=F32
            )
            hid[side, :, j, pl.ds(k, hz, stride=2), :] = piece.reshape(hx, hz, ch)
        grad = hid[side].reshape(plane, ch) * far[:, side * ch : (side + 1) * ch]

        @pl.when(inside)
        def _(side=side, grad=grad):
            g_halo[side] = grad.astype(BF16).reshape(ex, ez, ch)

        spread_rows(g3, 3 * side, g_halo[side], side)
    for side in range(2):
        total = act[:, side * ch : (side + 1) * ch] + hid_grad[side].reshape(plane, ch)
        for sx in range(3):
            total = total + mt(window(g3, 3 * side, 2 - sx), turned(2 - 2 * side, sx))
        feature_grad[0, side] = total.astype(BF16).reshape(ex, ez, ch)
    for piece in range(pieces):
        cross_piece(piece)
        if piece == 0:
            near_piece(3)
    for copies in far_copies:
        for copy in copies:
            copy.wait_send()
    near_on()

    for copy in mix_copies:
        copy.wait()
    mix_total[...] = sum(mix_recv[s] for s in range(n)) * scale
    mix_swap = to_peer(mix_total, mix_peer, last_s.at[0], last_r.at[0])
    mix_swap.start()

    wait_down()
    value = sum(down_recv[s].astype(F32) for s in range(groups)) * scale
    for h in range(halves):
        down_half[pl.ds(h, down_part, stride=halves), :] = value[:, h * lanes : (h + 1) * lanes]
    down_swap = to_peer(down_half, down_half_peer, last_s.at[1], last_r.at[1])
    down_swap.start()

    near_copies[4].wait()
    near_copies[5].wait()
    fine_swaps = []
    for piece, copy in enumerate(cross_copies):
        rows_of = slice(piece * height, (piece + 1) * height)
        value = fine_keep[2, rows_of] + sum(fine_recv[j, rows_of].astype(F32) for j in (4, 5))
        copy.wait()
        fine_half[rows_of] = (value + fine_recv[6, rows_of].astype(F32)) * scale
        swap = to_peer(
            fine_half.at[pl.ds(piece * height, height)],
            fine_half_peer.at[pl.ds(piece * height, height)],
            last_s.at[2 + piece], last_r.at[2 + piece],
        )
        swap.start()
        fine_swaps.append(swap)

    skew = fine_mine - fine_step

    def put_fine(source, whose):
        fine_out[pl.ds(pl.multiple_of(whose * fine_mine, 8), fine_mine), :] = source[
            pl.ds(pl.multiple_of(whose * skew, 8), fine_mine), :
        ]

    down_len = down_part * halves
    put_fine(fine_half, core)
    down_out[pl.ds(pl.multiple_of(core * down_len, 8), down_len), :] = down_half[...]
    mix_swap.wait()
    mix_total[...] = mix_total[...] + mix_peer[...]
    mixing_out[...] = mix_total[pl.ds(me, 1), 0:n]
    down_swap.wait()
    down_out[pl.ds(pl.multiple_of(other * down_len, 8), down_len), :] = down_half_peer[...]
    for swap in fine_swaps:
        swap.wait()
    put_fine(fine_half_peer, other)


def put_out(*refs):
    sources, dests, done = refs[:5], refs[5:10], refs[10]
    copies = [
        pltpu.make_async_copy(source, dest, done.at[i])
        for i, (source, dest) in enumerate(zip(sources, dests))
    ]
    for copy in copies:
        copy.start()
    for copy in copies:
        copy.wait()


def fused_fits(mesh, features, w_down):
    n = mesh.shape["space"]
    batch, ny, ex, ez, ch = features.shape
    cc = w_down.shape[2]
    spots = ex * ez // 4
    return (
        batch == mesh.shape["groups"] * mesh.shape["sample"]
        and ny == 2 * n
        and mesh.shape["sample"] == 2
        and n == 8
        and w_down.shape[0] == 8
        and -(27 * ch // n // 2) // 16 % 2 == 0
        and ch == 128
        and cc % 128 == 0
        and ez % 16 == 0
        and ex % 2 == 0
        and spots % 8 == 0
        and (spots * cc) % (n * 128 * 16) == 0
        and (27 * ch) % (n * 16) == 0
        and (8 * ch) % (n * 32) == 0
    )


def fused(mesh, features, w_fine, w_down, mixing, cotangent):
    n = lax.axis_size("space")
    _, _, ex, ez, ch = features.shape
    cc = w_down.shape[2]
    batch = lax.axis_size("sample")
    scale = float(batch * 2 * n * ex * ez) ** (-0.5)
    plane, spots, lanes = ex * ez, ex * ez // 4, 128
    rows = spots * cc // lanes // n
    fine_rows, down_rows = 27 * ch // n, 8 * ch // n
    half = fine_rows // 2
    part = -(-half // 16) * 16
    down_part = down_rows // 2
    down_len = down_part * cc // lanes
    vm = pltpu.VMEM
    dma = pltpu.SemaphoreType.DMA
    groups = n // 2
    arrays = (features, w_fine, w_down, mixing, cotangent)
    scratch = [
        *[vm(array.shape, BF16) for array in arrays], dma((5,)),
        *[vm((2, ex, ez, ch), BF16)] * 4,
        vm((2, ex, ez + 16, ch), F32),
        vm((6, ex + 2, ez, 3 * ch), BF16), vm((4, ex + 2, ez, 3 * ch), BF16),
        vm((3, 3 * ch, 4 * plane), BF16),
        vm((plane, 2 * ch), F32), vm((plane, 2 * ch), F32),
        vm((2, ex // 2, 2, ez, ch), F32),
        vm((2, spots, 4 * ch), BF16), vm((spots, 4 * ch), BF16),
        vm((groups, ch, 2 * spots), BF16),
        vm((n * rows, lanes), F32),
        vm((n, rows, lanes), BF16), vm((n, rows, lanes), BF16),
        vm((n, rows, lanes), BF16), vm((3, n, rows, lanes), BF16),
        vm((2, ex // 2, 2, ez, ch), F32),
        vm((27 * ch, ch), BF16),
        vm((n, part, ch), BF16), *[vm((7, part, ch), BF16)] * 2, vm((3, part, ch), F32),
        vm((groups, down_part, 2 * spots), BF16), vm((2, n, rows, lanes), BF16),
        *[vm((groups, down_part, cc), BF16)] * 2,
        vm((n, lanes), F32), vm((n, n, lanes), F32), vm((n, lanes), F32), vm((n, lanes), F32),
        vm((part, ch), F32), vm((part, ch), F32),
        vm((down_len, lanes), F32), vm((down_len, lanes), F32),
        dma((2,)), dma((2,)), dma((n - 1,)), dma((n - 1,)), dma((n - 1,)), dma((n - 1,)),
        dma((n - 1,)), dma((n - 1,)),
        dma((2,)), dma((2,)), dma((n,)), dma((n,)), dma, dma,
        *[dma] * 4,
        *[dma((14,))] * 2, *[dma((groups - 1,))] * 2, dma((4,)), dma((4,)),
        pltpu.SemaphoreType.REGULAR((2,)),
    ]
    spec = pl.BlockSpec(memory_space=pltpu.VMEM)
    far = pl.BlockSpec(memory_space=pltpu.HBM)
    shapes = (
        jax.ShapeDtypeStruct(cotangent.shape, BF16),
        jax.ShapeDtypeStruct(features.shape, BF16),
        jax.ShapeDtypeStruct((fine_rows, ch), F32),
        jax.ShapeDtypeStruct((down_rows * cc // lanes, lanes), F32),
        jax.ShapeDtypeStruct((1, n), F32),
    )
    results = pl.pallas_call(
        functools.partial(fused_body, (n, ex, ez, ch, cc, scale)),
        out_shape=shapes,
        in_specs=[far] * 5,
        out_specs=tuple([spec] * 5),
        scratch_shapes=scratch,
        compiler_params=pltpu.CompilerParams(
            collective_id=0, has_side_effects=True, vmem_limit_bytes=65472 * 1024
        ),
    )(*arrays)
    a, b, c, d, e = pl.pallas_call(
        put_out,
        out_shape=shapes,
        in_specs=[spec] * 5,
        out_specs=tuple([far] * 5),
        scratch_shapes=[dma((5,))],
        compiler_params=pltpu.CompilerParams(vmem_limit_bytes=65472 * 1024),
    )(*results)
    return a, b, c.reshape(-1), d.reshape(-1), e


def with_halo(array, sides, width):
    for axis, dim in sides:
        devices, length = (lax.axis_size(axis), array.shape[dim])
        up = [(i, (i + 1) % devices) for i in range(devices - 1)]
        down = [(j, i) for i, j in up]
        last = lax.slice_in_dim(array, length - width, length, axis=dim)
        initial = lax.slice_in_dim(array, 0, width, axis=dim)
        before = lax.ppermute(last, axis, up)
        after = lax.ppermute(initial, axis, down)
        array = jnp.concatenate([before, array, after], axis=dim)
    return array


def forward_conv(padded, weight, count):
    extent_x = padded.shape[2] - 2
    extent_z = padded.shape[3] - 2
    channels = padded.shape[4]
    total = None
    for shift_y in range(3):
        for shift_x in range(3):
            pieces = [
                padded[
                    :,
                    shift_y : shift_y + count,
                    shift_x : shift_x + extent_x,
                    shift_z : shift_z + extent_z,
                    :,
                ]
                for shift_z in range(3)
            ]
            stacked = jnp.concatenate(pieces, axis=-1).reshape(-1, 3 * channels)
            first = shift_y * 9 + shift_x * 3
            kernel = weight[first : first + 3].reshape(3 * channels, weight.shape[2])
            term = jnp.dot(stacked, kernel, preferred_element_type=jnp.float32)
            total = term if total is None else total + term
    return total.reshape(padded.shape[0], count, extent_x, extent_z, weight.shape[2])


def transposed_conv(padded, weight, count):
    extent_x = padded.shape[2] - 2
    extent_z = padded.shape[3] - 2
    channels = padded.shape[4]
    total = None
    for shift_y in range(3):
        for shift_x in range(3):
            pieces = [
                padded[
                    :,
                    2 - shift_y : 2 - shift_y + count,
                    2 - shift_x : 2 - shift_x + extent_x,
                    2 - shift_z : 2 - shift_z + extent_z,
                    :,
                ]
                for shift_z in range(3)
            ]
            stacked = jnp.concatenate(pieces, axis=-1).reshape(-1, 3 * channels)
            first = shift_y * 9 + shift_x * 3
            kernel = jnp.swapaxes(weight[first : first + 3], 1, 2).reshape(
                3 * channels, weight.shape[1]
            )
            term = jnp.dot(stacked, kernel, preferred_element_type=jnp.float32)
            total = term if total is None else total + term
    return total.reshape(padded.shape[0], count, extent_x, extent_z, weight.shape[1])


def weight_terms(padded, grad, count):
    extent_x = padded.shape[2] - 2
    extent_z = padded.shape[3] - 2
    channels = padded.shape[4]
    flat_grad = grad.reshape(-1, grad.shape[4])
    blocks = []
    for shift_y in range(3):
        for shift_x in range(3):
            pieces = [
                padded[
                    :,
                    shift_y : shift_y + count,
                    shift_x : shift_x + extent_x,
                    shift_z : shift_z + extent_z,
                    :,
                ]
                for shift_z in range(3)
            ]
            stacked = jnp.concatenate(pieces, axis=-1).reshape(-1, 3 * channels)
            blocks.append(
                lax.dot_general(
                    stacked, flat_grad, (((0,), (0,)), ((), ())), preferred_element_type=jnp.float32
                )
            )
    return jnp.concatenate(blocks, axis=0).reshape(-1)


def fold_taps(hidden):
    batch, rows_here, extent_x, extent_z, channels = hidden.shape
    shaped = hidden.reshape(batch, rows_here // 2, 2, extent_x // 2, 2, extent_z // 2, 2, channels)
    return shaped.transpose(0, 1, 3, 5, 2, 4, 6, 7).reshape(-1, 8 * channels)


def unfold_taps(values, batch, rows_here, extent_x, extent_z, channels):
    shaped = values.reshape(batch, rows_here // 2, extent_x // 2, extent_z // 2, 2, 2, 2, channels)
    return shaped.transpose(0, 1, 4, 2, 5, 3, 6, 7).reshape(
        batch, rows_here, extent_x, extent_z, channels
    )


def silu_slope(value):
    sigma = jax.nn.sigmoid(value)
    return sigma * (1.0 + value * (1.0 - sigma))


def local(features, w_fine, w_down, mixing, cotangent):
    batch, rows_here, extent_x, extent_z, channels = features.shape
    coarse_ch = w_down.shape[2]
    rimmed = with_halo(features, (("space", 1),), 1)
    xpadded = jnp.pad(rimmed, ((0, 0), (0, 0), (1, 1), (1, 1), (0, 0)))
    act = forward_conv(xpadded, w_fine, rows_here)
    hidden = (features.astype(jnp.float32) + jax.nn.silu(act)).astype(jnp.bfloat16)
    folded = fold_taps(hidden)
    down_matrix = w_down.reshape(8 * channels, coarse_ch)
    coarse = jnp.dot(folded, down_matrix, preferred_element_type=jnp.float32).astype(jnp.bfloat16)
    coarse = coarse.reshape(batch, rows_here // 2, -1)
    columns = lax.all_to_all(coarse, "space", split_axis=2, concat_axis=1, tiled=True)
    mixed = jnp.stack([jnp.dot(mixing, columns[0], preferred_element_type=jnp.float32)])
    bottleneck = (columns.astype(jnp.float32) + jax.nn.silu(mixed)).astype(jnp.bfloat16)
    cot = cotangent.astype(jnp.float32)
    mixed_grad = (cot * silu_slope(mixed)).astype(jnp.bfloat16)
    term = lax.dot_general(
        mixed_grad[0], columns[0], (((1,), (1,)), ((), ())), preferred_element_type=jnp.float32
    )
    spread_list = [
        lax.dot_general(
            mixing, mixed_grad[0], (((0,), (0,)), ((), ())), preferred_element_type=jnp.float32
        )
    ]
    column_grad = (cot + jnp.stack(spread_list)).astype(jnp.bfloat16)
    coarse_grad = lax.all_to_all(column_grad, "space", split_axis=1, concat_axis=2, tiled=True)
    flat_coarse = coarse_grad.reshape(-1, coarse_ch)
    down_terms = lax.dot_general(
        folded, flat_coarse, (((0,), (0,)), ((), ())), preferred_element_type=jnp.float32
    ).reshape(-1)
    hidden_grad = unfold_taps(
        jnp.dot(flat_coarse, down_matrix.T, preferred_element_type=jnp.float32),
        batch,
        rows_here,
        extent_x,
        extent_z,
        channels,
    )
    act_grad = (hidden_grad * silu_slope(act)).astype(jnp.bfloat16)
    grad_rim = with_halo(act_grad, (("space", 1),), 1)
    gpadded = jnp.pad(grad_rim, ((0, 0), (0, 0), (1, 1), (1, 1), (0, 0)))
    spread = transposed_conv(gpadded, w_fine, rows_here)
    feature_grad = (hidden_grad + spread).astype(jnp.bfloat16)
    fine_terms = weight_terms(xpadded, act_grad, rows_here)
    scale = float(
        batch * lax.axis_size("sample") * rows_here * lax.axis_size("space") * extent_x * extent_z
    ) ** (-0.5)
    shares = (
        lax.psum_scatter(fine_terms, "space", scatter_dimension=0, tiled=True),
        lax.psum_scatter(down_terms, "space", scatter_dimension=0, tiled=True),
        lax.psum_scatter(term, "space", scatter_dimension=0, tiled=True),
    )
    totals = lax.psum((shares[0], shares[1], shares[2]), "sample")
    return (bottleneck, feature_grad, totals[0] * scale, totals[1] * scale, totals[2] * scale)


def solution(mesh):
    placed = (
        P(("groups", "sample"), "space", None, None, None),
        P(),
        P(),
        P(),
        P(("groups", "sample"), None, "space"),
    )
    out_specs = (
        P(("groups", "sample"), None, "space"),
        P(("groups", "sample"), "space", None, None, None),
        P(("groups", "space")),
        P(("groups", "space")),
        P(("groups", "space"), None),
    )

    def step(features, w_fine, w_down, mixing, cotangent):
        kernel = functools.partial(fused, mesh) if fused_fits(mesh, features, w_down) else local
        mapped = jax.shard_map(
            kernel, mesh=mesh, in_specs=placed, out_specs=out_specs, check_vma=False
        )
        return mapped(features, w_fine, w_down, mixing, cotangent)

    return step
```

```python
import functools

import jax
import jax.numpy as jnp
from jax import lax
from jax.experimental import pallas as pl
from jax.experimental.pallas import tpu as pltpu
from jax.sharding import PartitionSpec as P

MESH = pl.DeviceIdType.MESH
F32 = jnp.float32
BF16 = jnp.bfloat16
CONTRACT_LAST = (((1,), (1,)), ((), ()))
CONTRACT_FIRST = (((0,), (0,)), ((), ()))


def fused_body(
    cfg,
    features_in, w_fine_in, w_down_in, mixing_in, cotangent_in,
    bottleneck, feature_grad, fine_out, down_out, mixing_out,
    features, w_fine, w_down, mixing, cotangent, load_s,
    x_halo, g_halo, grad16, pad, x3, g3, xt, act, hid, folded, fold_met, folded_t,
    stage, fwd_send, fwd_recv, back_send, back_recv, hid_grad,
    fine16, fine_peer, fine_send, fine_recv, fine_keep,
    fold_peer, back_peer, down16, down_recv,
    mix_send, mix_recv, mix_total, mix_peer,
    fine_half, fine_half_peer, down_half, down_half_peer,
    halo_s, halo_r, fwd_s, fwd_r, back_s, back_r, mix_s, mix_r,
    ghalo_s, ghalo_r, peer_s, peer_r, dpeer_s, dpeer_r,
    fold_s, fold_r, turn_s, turn_r, fine_s, fine_r, down_s, down_r, last_s, last_r,
    gate,
):
    n, ex, ez, ch, cc, scale = cfg
    plane = ex * ez
    hx, hz = ex // 2, ez // 2
    lanes = 128
    rows = hx * hz * cc // lanes // n
    halves = cc // lanes
    fine_rows = 27 * ch // n
    part = fine_send.shape[1]
    fine_step = fine_rows - part
    fine_mine = fine_rows // 2
    down_rows = 8 * ch // n
    down_part = down_rows // 2
    me = lax.axis_index("space")
    core = lax.axis_index("sample")
    other = 1 - core

    def to_space(src, dst, send, recv, who):
        return pltpu.make_async_remote_copy(
            src_ref=src, dst_ref=dst, send_sem=send, recv_sem=recv,
            device_id={"space": who}, device_id_type=MESH,
        )

    def to_peer(src, dst, send, recv):
        return pltpu.make_async_remote_copy(
            src_ref=src, dst_ref=dst, send_sem=send, recv_sem=recv,
            device_id={"sample": other}, device_id_type=MESH,
        )

    has_prev, has_next = me > 0, me < n - 1
    groups = n // 2
    group, side_of = me // 2, lax.rem(me, 2)
    partner = me + 1 - 2 * side_of

    barrier = pltpu.get_barrier_semaphore()
    greeted = 1
    for shift in (-2, -1, 1, 2):
        who = me + shift
        inside = jnp.logical_and(who >= 0, who < n)
        greeted = greeted + inside.astype(jnp.int32)

        @pl.when(inside)
        def _(who=who):
            pl.semaphore_signal(barrier, inc=1, device_id={"space": who}, device_id_type=MESH)

    pl.semaphore_signal(barrier, inc=1, device_id={"sample": other}, device_id_type=MESH)
    loads = [
        pltpu.make_async_copy(source, dest, load_s.at[i])
        for i, (source, dest) in enumerate(
            (
                (features_in, features),
                (w_fine_in, w_fine),
                (w_down_in, w_down),
                (mixing_in, mixing),
                (cotangent_in, cotangent),
            )
        )
    ]
    for load in loads:
        load.start()

    def halo_copies(first, last, halo, send, recv):
        down = to_space(first, halo.at[1], send.at[0], recv.at[1], me - 1)
        up = to_space(last, halo.at[0], send.at[1], recv.at[0], me + 1)
        return down, up

    def start_halo(copies):
        pl.when(has_prev)(copies[0].start)
        pl.when(has_next)(copies[1].start)

    def wait_halo(copies):
        def with_prev():
            copies[0].wait_send()
            copies[1].wait_recv()

        def with_next():
            copies[1].wait_send()
            copies[0].wait_recv()

        pl.when(has_prev)(with_prev)
        pl.when(has_next)(with_next)

    x_copies = halo_copies(features.at[0, 0], features.at[0, 1], x_halo, halo_s, halo_r)
    loads[0].wait()
    pl.semaphore_wait(barrier, greeted)
    start_halo(x_copies)
    gates = ((group > 0, group < groups - 1, me + 2), (group < groups - 1, group > 0, me - 2))
    ends = jnp.logical_or(group == 0, group == groups - 1)

    def await_gate(slot):
        pl.when(gates[slot][0])(lambda: pl.semaphore_wait(gate.at[slot], 1))

    for slot, (_, onward, after) in enumerate(gates):
        pl.when(jnp.logical_not(ends))(lambda slot=slot: await_gate(slot))

        @pl.when(onward)
        def _(slot=slot, after=after):
            pl.semaphore_signal(
                gate.at[slot], inc=1, device_id={"space": after}, device_id_type=MESH
            )

    @pl.when(me == 0)
    def _():
        x_halo[0] = jnp.zeros(x_halo.shape[1:], BF16)
        g_halo[0] = jnp.zeros(g_halo.shape[1:], BF16)

    @pl.when(me == n - 1)
    def _():
        x_halo[1] = jnp.zeros(x_halo.shape[1:], BF16)
        g_halo[1] = jnp.zeros(g_halo.shape[1:], BF16)

    pad[:, :, 0:8, :] = jnp.zeros((2, ex, 8, ch), F32)
    pad[:, :, 8 + ez : 16 + ez, :] = jnp.zeros((2, ex, 8, ch), F32)
    for rim in (0, ex + 1):
        x3[:, rim] = jnp.zeros((4, ez, 3 * ch), BF16)
        g3[:, rim] = jnp.zeros((4, ez, 3 * ch), BF16)

    def spread_rows(dest, index, row, slot):
        pad[slot, :, 8 : 8 + ez, :] = row.astype(F32)
        dest[index, 1 : 1 + ex, :, 0:ch] = pad[slot, :, 7 : 7 + ez, :].astype(BF16)
        dest[index, 1 : 1 + ex, :, ch : 2 * ch] = row
        dest[index, 1 : 1 + ex, :, 2 * ch : 3 * ch] = pad[slot, :, 9 : 9 + ez, :].astype(BF16)

    def window(source, index, shift):
        return source[index, shift : shift + ex].reshape(plane, 3 * ch)

    def taps(sy, sx):
        first = sy * 9 + sx * 3
        return w_fine[first : first + 3].reshape(3 * ch, ch)

    def mm(a, b):
        return jnp.dot(a, b, preferred_element_type=F32)

    spread_rows(x3, 1, features[0, 0], 0)
    spread_rows(x3, 2, features[0, 1], 1)
    loads[1].wait()
    total = None
    for sx in range(3):
        term = mm(window(x3, 1, sx), jnp.concatenate([taps(1, sx), taps(0, sx)], axis=1))
        total = term if total is None else total + term
        total = total + mm(
            window(x3, 2, sx), jnp.concatenate([taps(2, sx), taps(1, sx)], axis=1)
        )
    act[...] = total
    for slot in range(2):
        pl.when(ends)(lambda slot=slot: await_gate(slot))
    wait_halo(x_copies)
    spread_rows(x3, 0, x_halo[0], 0)
    spread_rows(x3, 3, x_halo[1], 1)
    for side in range(2):
        total = act[:, side * ch : (side + 1) * ch]
        for sx in range(3):
            total = total + mm(window(x3, 3 * side, sx), taps(2 * side, sx))
        act[:, side * ch : (side + 1) * ch] = total
        value = features[0, side].reshape(plane, ch).astype(F32) + total * jax.nn.sigmoid(total)
        hid[side] = value.astype(BF16).astype(F32).reshape(hx, 2, ez, ch)

    for t in range(8):
        i, j, k = t // 4, t // 2 % 2, t % 2
        piece = hid[i, :, j, pl.ds(k, hz, stride=2), :].reshape(hx * hz, ch)
        folded[k, :, t // 2 * ch : (t // 2 + 1) * ch] = piece.astype(BF16)
    loads[2].wait()
    coarse = mm(folded[0], jnp.concatenate([w_down[t] for t in range(0, 8, 2)], axis=0))
    coarse = coarse + mm(folded[1], jnp.concatenate([w_down[t] for t in range(1, 8, 2)], axis=0))
    coarse = coarse.astype(BF16).astype(F32)
    for h in range(halves):
        stage[pl.ds(h, hx * hz, stride=halves), :] = coarse[:, h * lanes : (h + 1) * lanes]
    fwd_send[...] = stage[...].astype(BF16).reshape(n, rows, lanes)

    def exchange(src_of, slot, send, recv):
        out = []
        for k in range(1, n):
            who = lax.rem(me + k, n)
            copy = to_space(src_of(who), slot(), send.at[k - 1], recv.at[k - 1], who)
            copy.start()
            out.append(copy)
        return out

    coarse_copies = exchange(
        lambda who: fwd_send.at[who], lambda: fwd_recv.at[me], fwd_s, fwd_r
    )
    fold_copy = to_space(folded.at[1 - side_of], fold_met, fold_s, fold_r, partner)
    fold_copy.start()
    fwd_recv[me] = fwd_send[me]

    loads[3].wait()
    loads[4].wait()
    for sx in range(3):
        for j in range(4):
            xt[sx, :, j * plane : (j + 1) * plane] = window(x3, j, sx).T

    for copy in coarse_copies:
        copy.wait()
    stage[...] = fwd_recv[...].reshape(n * rows, lanes).astype(F32)
    columns = jnp.concatenate([stage[pl.ds(r, n, stride=rows), :] for r in range(rows)], axis=1)
    columns16 = columns.astype(BF16)
    mix = mixing[...]
    mixed = mm(mix, columns16)
    sigma = jax.nn.sigmoid(mixed)
    bottleneck[0] = (columns + mixed * sigma).astype(BF16)
    cot = cotangent[0].astype(F32)
    mixed_grad = (cot * (sigma * (1.0 + mixed * (1.0 - sigma)))).astype(BF16)
    spread = lax.dot_general(mix, mixed_grad, CONTRACT_FIRST, preferred_element_type=F32)
    column_grad = cot + spread
    for r in range(rows):
        stage[pl.ds(r, n, stride=rows), :] = column_grad[:, r * lanes : (r + 1) * lanes]
    back_send[...] = stage[...].astype(BF16).reshape(n, rows, lanes)
    back_copies = exchange(
        lambda who: back_send.at[pl.ds(who // 2 * 2, 2)], lambda: back_recv.at[:, me],
        back_s, back_r,
    )
    for side in range(2):
        back_recv[side, me] = back_send[2 * group + side]
    term = lax.dot_general(mixed_grad, columns16, CONTRACT_LAST, preferred_element_type=F32)
    mix_send[...] = jnp.zeros(mix_send.shape, F32)
    mix_send[:, 0:n] = term
    mix_copies = exchange(lambda who: mix_send, lambda: mix_recv.at[me], mix_s, mix_r)
    mix_recv[me] = mix_send[...]
    value = act[...]
    sig = jax.nn.sigmoid(value)
    act[...] = sig * (1.0 + value * (1.0 - sig))

    fold_copy.wait()
    turned_taps = jnp.concatenate([folded[side_of], fold_met[...]], axis=0).T
    folded_t[...] = turned_taps.reshape(groups, ch, 2 * hx * hz)
    turn_copy = to_peer(
        folded_t.at[:, pl.ds(pl.multiple_of(other * down_part, 16), down_part), :],
        fold_peer, turn_s, turn_r,
    )
    turn_copy.start()

    def flat_of(source, side):
        stage[...] = source[side].reshape(n * rows, lanes).astype(F32)
        return jnp.concatenate(
            [stage[pl.ds(h, hx * hz, stride=halves), :] for h in range(halves)], axis=1
        ).astype(BF16)

    for copy in back_copies:
        copy.wait()
    flat_copy = to_peer(back_recv, back_peer, dpeer_s, dpeer_r)
    flat_copy.start()
    flat = flat_of(back_recv, side_of)

    for t in range(8):
        i, j, k = t // 4, t // 2 % 2, t % 2
        piece = lax.dot_general(flat, w_down[t], CONTRACT_LAST, preferred_element_type=F32)
        hid_grad[i, :, j, pl.ds(k, hz, stride=2), :] = piece.reshape(hx, hz, ch)
    for side in range(2):
        grad = hid_grad[side].reshape(plane, ch) * act[:, side * ch : (side + 1) * ch]
        grad16[side] = grad.astype(BF16).reshape(ex, ez, ch)
    g_copies = halo_copies(grad16.at[0], grad16.at[1], g_halo, ghalo_s, ghalo_r)

    near = (side_of == 1, side_of == 0)
    away = (
        jnp.logical_and(side_of == 0, has_prev), jnp.logical_and(side_of == 1, has_next)
    )

    def start_some(conditions):
        for condition, copy in zip(conditions, g_copies):
            pl.when(condition)(copy.start)

    start_some(away)
    def send_down():
        turn_copy.wait()
        flat_copy.wait()
        taps_here = folded_t[:, pl.ds(pl.multiple_of(core * down_part, 16), down_part), :]
        left = jnp.concatenate([taps_here, fold_peer[...]], axis=2)
        right = jnp.concatenate(
            [
                flat, flat_of(back_recv, 1 - side_of),
                flat_of(back_peer, side_of), flat_of(back_peer, 1 - side_of),
            ],
            axis=0,
        )
        total = mm(left.reshape(groups * down_part, 4 * hx * hz), right)
        down16[...] = total.astype(BF16).reshape(groups, down_part, cc)

    def start_down():
        for step in range(groups - 1):
            to = lax.rem(group + step + 1, groups)
            to_space(
                down16.at[to], down_recv.at[group], down_s.at[step], down_r.at[step],
                2 * to + side_of,
            ).start()
        down_recv[group] = down16[group]

    def wait_down():
        for step in range(groups - 1):
            source = lax.rem(group - 1 - step + groups, groups)
            to_space(
                down16.at[source], down_recv.at[source], down_s.at[step], down_r.at[step], partner
            ).wait()

    flip = group + 1 - 2 * lax.rem(group, 2)
    across = lax.rem(group + 2, groups)
    owners = (lax.rem(flip + 2, groups), across, flip, group)
    orders = ((8, 7, 6, 5, 4, 3, 2, 1, 0), (6, 5, 4, 8, 7, 2, 1, 0, 3))
    orders = orders + tuple(tuple(8 - t for t in order) for order in orders[::-1])

    flat_grad = grad16[...].reshape(2 * plane, ch)

    def fine_block(i):
        t = orders[0][i]
        for g in range(1, groups):
            t = jnp.where(group == g, orders[g][i], t)
        sy, sx = t // 3, lax.rem(t, 3)
        window_t = xt[sx, :, pl.ds(pl.multiple_of(sy * plane, lanes), 2 * plane)]
        start = pl.multiple_of(t * 3 * ch, lanes)
        fine16[pl.ds(start, 3 * ch), :] = mm(window_t, flat_grad).astype(BF16)

    peer_copies = []

    def fine_to_peer(k):
        for j in range(2):
            who = 2 * owners[k] + j
            start = pl.multiple_of(who * fine_rows + other * fine_step, 16)
            copy = to_peer(
                fine16.at[pl.ds(start, part), :], fine_peer.at[who],
                peer_s.at[2 * k + j], peer_r.at[2 * k + j],
            )
            copy.start()
            peer_copies.append(copy)

    def fine_own(who):
        start = pl.multiple_of(who * fine_rows + core * fine_step, 16)
        return fine16[pl.ds(start, part), :].astype(F32) + fine_peer[who].astype(F32)

    pieces = 2
    height = part // pieces

    def own_rows(who, first, count):
        start = pl.multiple_of(who * fine_rows + core * fine_step + first, 16)
        mine = fine16[pl.ds(start, count), :].astype(F32)
        return mine + fine_peer[who, first : first + count].astype(F32)

    def slot_copy(slot, piece, who):
        rows_of = pl.ds(piece * height, height)
        index = slot * pieces + piece
        return to_space(
            fine_send.at[slot, rows_of], fine_recv.at[slot, rows_of],
            fine_s.at[index], fine_r.at[index], who,
        )

    def whole_copy(slot, who):
        return to_space(
            fine_send.at[slot], fine_recv.at[slot],
            fine_s.at[slot * pieces], fine_r.at[slot * pieces], who,
        )

    far_copies = [[None] * 3 for _ in range(pieces)]

    def met_peer(k):
        peer_copies[2 * k].wait()
        peer_copies[2 * k + 1].wait()

    def far_piece(piece, first, k):
        to = 2 * owners[k]
        targets = ((2, 1 - side_of), (1, side_of)) if k == 0 else ((0, 1 - side_of),)
        for slot, side in targets:
            fine_send[slot, first : first + height] = own_rows(to + side, first, height).astype(BF16)
            at = (partner, 2 * flip + side_of, 2 * flip + 1 - side_of)[slot]
            copy = slot_copy(slot, piece, at)
            copy.start()
            far_copies[piece][slot] = copy
        if k == 1:
            fine_keep[0, first : first + height] = own_rows(to + side_of, first, height)

    near_copies = {}

    def near_piece(k):
        met_peer(k)
        fine_send[k + 1] = fine_own(2 * owners[k] + 1 - side_of).astype(BF16)
        near_copies[k + 1] = whole_copy(k + 1, partner)
        near_copies[k + 1].start()
        fine_keep[k - 1] = fine_own(2 * owners[k] + side_of)

    def near_on():
        near_copies[3].wait()
        fine_send[5] = (fine_keep[1] + fine_recv[3].astype(F32)).astype(BF16)
        near_copies[5] = whole_copy(5, 2 * flip + side_of)
        near_copies[5].start()

    cross_copies = []

    def cross_piece(piece):
        for copy in far_copies[piece]:
            copy.wait_recv()
        first = piece * height
        rows_of = slice(first, first + height)
        total = fine_keep[0, rows_of] + sum(fine_recv[j, rows_of].astype(F32) for j in range(3))
        fine_send[6, rows_of] = total.astype(BF16)
        copy = slot_copy(6, piece, 2 * across + side_of)
        copy.start()
        cross_copies.append(copy)

    ready = {3: 0, 5: 1, 8: 2, 9: 3}
    for i in range(9):
        fine_block(i)
        if i + 1 in ready:
            fine_to_peer(ready[i + 1])
    met_peer(0)
    far_piece(0, 0, 0)
    met_peer(1)
    far_piece(0, 0, 1)
    for piece in range(1, pieces):
        far_piece(piece, piece * height, 0)
        far_piece(piece, piece * height, 1)
    near_piece(2)
    near_piece(3)
    send_down()
    start_down()

    def turned(i, sx):
        first = i * 9 + sx * 3
        return jnp.concatenate([w_fine[first + 2 - m] for m in range(3)], axis=1)

    def mt(a, b):
        return lax.dot_general(a, b, CONTRACT_LAST, preferred_element_type=F32)

    spread_rows(g3, 1, grad16[0], 0)
    spread_rows(g3, 2, grad16[1], 1)
    total = None
    for sx in range(3):
        term = mt(window(g3, 1, 2 - sx), jnp.concatenate([turned(1, sx), turned(2, sx)], axis=0))
        total = term if total is None else total + term
        total = total + mt(
            window(g3, 2, 2 - sx), jnp.concatenate([turned(0, sx), turned(1, sx)], axis=0)
        )
    act[...] = total
    start_some(near)
    for piece in range(pieces):
        cross_piece(piece)
    for copies in far_copies:
        for copy in copies:
            copy.wait_send()
    near_on()
    wait_halo(g_copies)
    spread_rows(g3, 0, g_halo[0], 0)
    spread_rows(g3, 3, g_halo[1], 1)
    for side in range(2):
        total = act[:, side * ch : (side + 1) * ch] + hid_grad[side].reshape(plane, ch)
        for sx in range(3):
            total = total + mt(window(g3, 3 * side, 2 - sx), turned(2 - 2 * side, sx))
        feature_grad[0, side] = total.astype(BF16).reshape(ex, ez, ch)


    for copy in mix_copies:
        copy.wait()
    mix_total[...] = sum(mix_recv[s] for s in range(n)) * scale
    mix_swap = to_peer(mix_total, mix_peer, last_s.at[0], last_r.at[0])
    mix_swap.start()

    wait_down()
    value = sum(down_recv[s].astype(F32) for s in range(groups)) * scale
    for h in range(halves):
        down_half[pl.ds(h, down_part, stride=halves), :] = value[:, h * lanes : (h + 1) * lanes]
    down_swap = to_peer(down_half, down_half_peer, last_s.at[1], last_r.at[1])
    down_swap.start()

    near_copies[4].wait()
    near_copies[5].wait()
    fine_swaps = []
    for piece, copy in enumerate(cross_copies):
        rows_of = slice(piece * height, (piece + 1) * height)
        value = fine_keep[2, rows_of] + sum(fine_recv[j, rows_of].astype(F32) for j in (4, 5))
        copy.wait()
        fine_half[rows_of] = (value + fine_recv[6, rows_of].astype(F32)) * scale
        swap = to_peer(
            fine_half.at[pl.ds(piece * height, height)],
            fine_half_peer.at[pl.ds(piece * height, height)],
            last_s.at[2 + piece], last_r.at[2 + piece],
        )
        swap.start()
        fine_swaps.append(swap)

    skew = fine_mine - fine_step

    def put_fine(source, whose):
        fine_out[pl.ds(pl.multiple_of(whose * fine_mine, 8), fine_mine), :] = source[
            pl.ds(pl.multiple_of(whose * skew, 8), fine_mine), :
        ]

    down_len = down_part * halves
    put_fine(fine_half, core)
    down_out[pl.ds(pl.multiple_of(core * down_len, 8), down_len), :] = down_half[...]
    mix_swap.wait()
    mix_total[...] = mix_total[...] + mix_peer[...]
    mixing_out[...] = mix_total[pl.ds(me, 1), 0:n]
    down_swap.wait()
    down_out[pl.ds(pl.multiple_of(other * down_len, 8), down_len), :] = down_half_peer[...]
    for swap in fine_swaps:
        swap.wait()
    put_fine(fine_half_peer, other)


def put_out(*refs):
    sources, dests, done = refs[:5], refs[5:10], refs[10]
    copies = [
        pltpu.make_async_copy(source, dest, done.at[i])
        for i, (source, dest) in enumerate(zip(sources, dests))
    ]
    for copy in copies:
        copy.start()
    for copy in copies:
        copy.wait()


def fused_fits(mesh, features, w_down):
    n = mesh.shape["space"]
    batch, ny, ex, ez, ch = features.shape
    cc = w_down.shape[2]
    spots = ex * ez // 4
    return (
        batch == mesh.shape["groups"] * mesh.shape["sample"]
        and ny == 2 * n
        and mesh.shape["sample"] == 2
        and n == 8
        and w_down.shape[0] == 8
        and -(27 * ch // n // 2) // 16 % 2 == 0
        and ch == 128
        and cc % 128 == 0
        and ez % 16 == 0
        and ex % 2 == 0
        and spots % 8 == 0
        and (spots * cc) % (n * 128 * 16) == 0
        and (27 * ch) % (n * 16) == 0
        and (8 * ch) % (n * 32) == 0
    )


def fused(mesh, features, w_fine, w_down, mixing, cotangent):
    n = lax.axis_size("space")
    _, _, ex, ez, ch = features.shape
    cc = w_down.shape[2]
    batch = lax.axis_size("sample")
    scale = float(batch * 2 * n * ex * ez) ** (-0.5)
    plane, spots, lanes = ex * ez, ex * ez // 4, 128
    rows = spots * cc // lanes // n
    fine_rows, down_rows = 27 * ch // n, 8 * ch // n
    half = fine_rows // 2
    part = -(-half // 16) * 16
    down_part = down_rows // 2
    down_len = down_part * cc // lanes
    vm = pltpu.VMEM
    dma = pltpu.SemaphoreType.DMA
    groups = n // 2
    arrays = (features, w_fine, w_down, mixing, cotangent)
    scratch = [
        *[vm(array.shape, BF16) for array in arrays], dma((5,)),
        vm((2, ex, ez, ch), BF16), vm((2, ex, ez, ch), BF16), vm((2, ex, ez, ch), BF16),
        vm((2, ex, ez + 16, ch), F32),
        vm((4, ex + 2, ez, 3 * ch), BF16), vm((4, ex + 2, ez, 3 * ch), BF16),
        vm((3, 3 * ch, 4 * plane), BF16),
        vm((plane, 2 * ch), F32),
        vm((2, ex // 2, 2, ez, ch), F32),
        vm((2, spots, 4 * ch), BF16), vm((spots, 4 * ch), BF16),
        vm((groups, ch, 2 * spots), BF16),
        vm((n * rows, lanes), F32),
        vm((n, rows, lanes), BF16), vm((n, rows, lanes), BF16),
        vm((n, rows, lanes), BF16), vm((2, n, rows, lanes), BF16),
        vm((2, ex // 2, 2, ez, ch), F32),
        vm((27 * ch, ch), BF16),
        vm((n, part, ch), BF16), *[vm((7, part, ch), BF16)] * 2, vm((3, part, ch), F32),
        vm((groups, down_part, 2 * spots), BF16), vm((2, n, rows, lanes), BF16),
        *[vm((groups, down_part, cc), BF16)] * 2,
        vm((n, lanes), F32), vm((n, n, lanes), F32), vm((n, lanes), F32), vm((n, lanes), F32),
        vm((part, ch), F32), vm((part, ch), F32),
        vm((down_len, lanes), F32), vm((down_len, lanes), F32),
        dma((2,)), dma((2,)), dma((n - 1,)), dma((n - 1,)), dma((n - 1,)), dma((n - 1,)),
        dma((n - 1,)), dma((n - 1,)),
        dma((2,)), dma((2,)), dma((n,)), dma((n,)), dma, dma,
        *[dma] * 4,
        *[dma((7 * 2,))] * 2, *[dma((groups - 1,))] * 2, dma((4,)), dma((4,)),
        pltpu.SemaphoreType.REGULAR((2,)),
    ]
    spec = pl.BlockSpec(memory_space=pltpu.VMEM)
    far = pl.BlockSpec(memory_space=pltpu.HBM)
    shapes = (
        jax.ShapeDtypeStruct(cotangent.shape, BF16),
        jax.ShapeDtypeStruct(features.shape, BF16),
        jax.ShapeDtypeStruct((fine_rows, ch), F32),
        jax.ShapeDtypeStruct((down_rows * cc // lanes, lanes), F32),
        jax.ShapeDtypeStruct((1, n), F32),
    )
    results = pl.pallas_call(
        functools.partial(fused_body, (n, ex, ez, ch, cc, scale)),
        out_shape=shapes,
        in_specs=[far] * 5,
        out_specs=tuple([spec] * 5),
        scratch_shapes=scratch,
        compiler_params=pltpu.CompilerParams(
            collective_id=0, has_side_effects=True, vmem_limit_bytes=65472 * 1024
        ),
    )(*arrays)
    a, b, c, d, e = pl.pallas_call(
        put_out,
        out_shape=shapes,
        in_specs=[spec] * 5,
        out_specs=tuple([far] * 5),
        scratch_shapes=[dma((5,))],
        compiler_params=pltpu.CompilerParams(vmem_limit_bytes=65472 * 1024),
    )(*results)
    return a, b, c.reshape(-1), d.reshape(-1), e


def with_halo(array, sides, width):
    for axis, dim in sides:
        devices, length = (lax.axis_size(axis), array.shape[dim])
        up = [(i, (i + 1) % devices) for i in range(devices - 1)]
        down = [(j, i) for i, j in up]
        last = lax.slice_in_dim(array, length - width, length, axis=dim)
        initial = lax.slice_in_dim(array, 0, width, axis=dim)
        before = lax.ppermute(last, axis, up)
        after = lax.ppermute(initial, axis, down)
        array = jnp.concatenate([before, array, after], axis=dim)
    return array


def forward_conv(padded, weight, count):
    extent_x = padded.shape[2] - 2
    extent_z = padded.shape[3] - 2
    channels = padded.shape[4]
    total = None
    for shift_y in range(3):
        for shift_x in range(3):
            pieces = [
                padded[
                    :,
                    shift_y : shift_y + count,
                    shift_x : shift_x + extent_x,
                    shift_z : shift_z + extent_z,
                    :,
                ]
                for shift_z in range(3)
            ]
            stacked = jnp.concatenate(pieces, axis=-1).reshape(-1, 3 * channels)
            first = shift_y * 9 + shift_x * 3
            kernel = weight[first : first + 3].reshape(3 * channels, weight.shape[2])
            term = jnp.dot(stacked, kernel, preferred_element_type=jnp.float32)
            total = term if total is None else total + term
    return total.reshape(padded.shape[0], count, extent_x, extent_z, weight.shape[2])


def transposed_conv(padded, weight, count):
    extent_x = padded.shape[2] - 2
    extent_z = padded.shape[3] - 2
    channels = padded.shape[4]
    total = None
    for shift_y in range(3):
        for shift_x in range(3):
            pieces = [
                padded[
                    :,
                    2 - shift_y : 2 - shift_y + count,
                    2 - shift_x : 2 - shift_x + extent_x,
                    2 - shift_z : 2 - shift_z + extent_z,
                    :,
                ]
                for shift_z in range(3)
            ]
            stacked = jnp.concatenate(pieces, axis=-1).reshape(-1, 3 * channels)
            first = shift_y * 9 + shift_x * 3
            kernel = jnp.swapaxes(weight[first : first + 3], 1, 2).reshape(
                3 * channels, weight.shape[1]
            )
            term = jnp.dot(stacked, kernel, preferred_element_type=jnp.float32)
            total = term if total is None else total + term
    return total.reshape(padded.shape[0], count, extent_x, extent_z, weight.shape[1])


def weight_terms(padded, grad, count):
    extent_x = padded.shape[2] - 2
    extent_z = padded.shape[3] - 2
    channels = padded.shape[4]
    flat_grad = grad.reshape(-1, grad.shape[4])
    blocks = []
    for shift_y in range(3):
        for shift_x in range(3):
            pieces = [
                padded[
                    :,
                    shift_y : shift_y + count,
                    shift_x : shift_x + extent_x,
                    shift_z : shift_z + extent_z,
                    :,
                ]
                for shift_z in range(3)
            ]
            stacked = jnp.concatenate(pieces, axis=-1).reshape(-1, 3 * channels)
            blocks.append(
                lax.dot_general(
                    stacked, flat_grad, (((0,), (0,)), ((), ())), preferred_element_type=jnp.float32
                )
            )
    return jnp.concatenate(blocks, axis=0).reshape(-1)


def fold_taps(hidden):
    batch, rows_here, extent_x, extent_z, channels = hidden.shape
    shaped = hidden.reshape(batch, rows_here // 2, 2, extent_x // 2, 2, extent_z // 2, 2, channels)
    return shaped.transpose(0, 1, 3, 5, 2, 4, 6, 7).reshape(-1, 8 * channels)


def unfold_taps(values, batch, rows_here, extent_x, extent_z, channels):
    shaped = values.reshape(batch, rows_here // 2, extent_x // 2, extent_z // 2, 2, 2, 2, channels)
    return shaped.transpose(0, 1, 4, 2, 5, 3, 6, 7).reshape(
        batch, rows_here, extent_x, extent_z, channels
    )


def silu_slope(value):
    sigma = jax.nn.sigmoid(value)
    return sigma * (1.0 + value * (1.0 - sigma))


def local(features, w_fine, w_down, mixing, cotangent):
    batch, rows_here, extent_x, extent_z, channels = features.shape
    coarse_ch = w_down.shape[2]
    rimmed = with_halo(features, (("space", 1),), 1)
    xpadded = jnp.pad(rimmed, ((0, 0), (0, 0), (1, 1), (1, 1), (0, 0)))
    act = forward_conv(xpadded, w_fine, rows_here)
    hidden = (features.astype(jnp.float32) + jax.nn.silu(act)).astype(jnp.bfloat16)
    folded = fold_taps(hidden)
    down_matrix = w_down.reshape(8 * channels, coarse_ch)
    coarse = jnp.dot(folded, down_matrix, preferred_element_type=jnp.float32).astype(jnp.bfloat16)
    coarse = coarse.reshape(batch, rows_here // 2, -1)
    columns = lax.all_to_all(coarse, "space", split_axis=2, concat_axis=1, tiled=True)
    mixed = jnp.stack([jnp.dot(mixing, columns[0], preferred_element_type=jnp.float32)])
    bottleneck = (columns.astype(jnp.float32) + jax.nn.silu(mixed)).astype(jnp.bfloat16)
    cot = cotangent.astype(jnp.float32)
    mixed_grad = (cot * silu_slope(mixed)).astype(jnp.bfloat16)
    term = lax.dot_general(
        mixed_grad[0], columns[0], (((1,), (1,)), ((), ())), preferred_element_type=jnp.float32
    )
    spread_list = [
        lax.dot_general(
            mixing, mixed_grad[0], (((0,), (0,)), ((), ())), preferred_element_type=jnp.float32
        )
    ]
    column_grad = (cot + jnp.stack(spread_list)).astype(jnp.bfloat16)
    coarse_grad = lax.all_to_all(column_grad, "space", split_axis=1, concat_axis=2, tiled=True)
    flat_coarse = coarse_grad.reshape(-1, coarse_ch)
    down_terms = lax.dot_general(
        folded, flat_coarse, (((0,), (0,)), ((), ())), preferred_element_type=jnp.float32
    ).reshape(-1)
    hidden_grad = unfold_taps(
        jnp.dot(flat_coarse, down_matrix.T, preferred_element_type=jnp.float32),
        batch,
        rows_here,
        extent_x,
        extent_z,
        channels,
    )
    act_grad = (hidden_grad * silu_slope(act)).astype(jnp.bfloat16)
    grad_rim = with_halo(act_grad, (("space", 1),), 1)
    gpadded = jnp.pad(grad_rim, ((0, 0), (0, 0), (1, 1), (1, 1), (0, 0)))
    spread = transposed_conv(gpadded, w_fine, rows_here)
    feature_grad = (hidden_grad + spread).astype(jnp.bfloat16)
    fine_terms = weight_terms(xpadded, act_grad, rows_here)
    scale = float(
        batch * lax.axis_size("sample") * rows_here * lax.axis_size("space") * extent_x * extent_z
    ) ** (-0.5)
    shares = (
        lax.psum_scatter(fine_terms, "space", scatter_dimension=0, tiled=True),
        lax.psum_scatter(down_terms, "space", scatter_dimension=0, tiled=True),
        lax.psum_scatter(term, "space", scatter_dimension=0, tiled=True),
    )
    totals = lax.psum((shares[0], shares[1], shares[2]), "sample")
    return (bottleneck, feature_grad, totals[0] * scale, totals[1] * scale, totals[2] * scale)


def solution(mesh):
    placed = (
        P(("groups", "sample"), "space", None, None, None),
        P(),
        P(),
        P(),
        P(("groups", "sample"), None, "space"),
    )
    out_specs = (
        P(("groups", "sample"), None, "space"),
        P(("groups", "sample"), "space", None, None, None),
        P(("groups", "space")),
        P(("groups", "space")),
        P(("groups", "space"), None),
    )

    def step(features, w_fine, w_down, mixing, cotangent):
        kernel = functools.partial(fused, mesh) if fused_fits(mesh, features, w_down) else local
        mapped = jax.shard_map(
            kernel, mesh=mesh, in_specs=placed, out_specs=out_specs, check_vma=False
        )
        return mapped(features, w_fine, w_down, mixing, cotangent)

    return step
```

```python
import functools

import jax
import jax.numpy as jnp
from jax import lax
from jax.experimental import pallas as pl
from jax.experimental.pallas import tpu as pltpu
from jax.sharding import PartitionSpec as P

MESH = pl.DeviceIdType.MESH
F32 = jnp.float32
BF16 = jnp.bfloat16
CONTRACT_LAST = (((1,), (1,)), ((), ()))
CONTRACT_FIRST = (((0,), (0,)), ((), ()))


def fused_body(
    cfg,
    features_in, w_fine_in, w_down_in, mixing_in, cotangent_in,
    bottleneck, feature_grad, fine_out, down_out, mixing_out,
    features, w_fine, w_down, mixing, cotangent, load_s,
    x_halo, g_halo, grad16, pad, x3, g3, xt, act, hid, folded, fold_met, folded_t,
    stage, fwd_send, fwd_recv, back_send, back_recv, hid_grad,
    fine16, fine_peer, fine_send, fine_recv, fine_keep,
    fold_peer, back_peer, down16, down_recv,
    mix_send, mix_recv, mix_total, mix_peer,
    fine_half, fine_half_peer, down_half, down_half_peer,
    halo_s, halo_r, fwd_s, fwd_r, back_s, back_r, mix_s, mix_r,
    ghalo_s, ghalo_r, peer_s, peer_r, dpeer_s, dpeer_r,
    fold_s, fold_r, turn_s, turn_r, fine_s, fine_r, down_s, down_r, last_s, last_r,
    gate,
):
    n, ex, ez, ch, cc, scale = cfg
    plane = ex * ez
    hx, hz = ex // 2, ez // 2
    lanes = 128
    rows = hx * hz * cc // lanes // n
    halves = cc // lanes
    fine_rows = 27 * ch // n
    part = fine_send.shape[1]
    fine_step = fine_rows - part
    fine_mine = fine_rows // 2
    down_rows = 8 * ch // n
    down_part = down_rows // 2
    me = lax.axis_index("space")
    core = lax.axis_index("sample")
    other = 1 - core

    def to_space(src, dst, send, recv, who):
        return pltpu.make_async_remote_copy(
            src_ref=src, dst_ref=dst, send_sem=send, recv_sem=recv,
            device_id={"space": who}, device_id_type=MESH,
        )

    def to_peer(src, dst, send, recv):
        return pltpu.make_async_remote_copy(
            src_ref=src, dst_ref=dst, send_sem=send, recv_sem=recv,
            device_id={"sample": other}, device_id_type=MESH,
        )

    has_prev, has_next = me > 0, me < n - 1
    groups = n // 2
    group, side_of = me // 2, lax.rem(me, 2)
    partner = me + 1 - 2 * side_of

    barrier = pltpu.get_barrier_semaphore()
    greeted = 1
    for shift in (-2, -1, 1, 2):
        who = me + shift
        inside = jnp.logical_and(who >= 0, who < n)
        greeted = greeted + inside.astype(jnp.int32)

        @pl.when(inside)
        def _(who=who):
            pl.semaphore_signal(barrier, inc=1, device_id={"space": who}, device_id_type=MESH)

    pl.semaphore_signal(barrier, inc=1, device_id={"sample": other}, device_id_type=MESH)
    loads = [
        pltpu.make_async_copy(source, dest, load_s.at[i])
        for i, (source, dest) in enumerate(
            (
                (features_in, features),
                (w_fine_in, w_fine),
                (w_down_in, w_down),
                (mixing_in, mixing),
                (cotangent_in, cotangent),
            )
        )
    ]
    for load in loads:
        load.start()

    def halo_copies(first, last, halo, send, recv):
        down = to_space(first, halo.at[1], send.at[0], recv.at[1], me - 1)
        up = to_space(last, halo.at[0], send.at[1], recv.at[0], me + 1)
        return down, up

    def start_halo(copies):
        pl.when(has_prev)(copies[0].start)
        pl.when(has_next)(copies[1].start)

    def wait_halo(copies):
        def with_prev():
            copies[0].wait_send()
            copies[1].wait_recv()

        def with_next():
            copies[1].wait_send()
            copies[0].wait_recv()

        pl.when(has_prev)(with_prev)
        pl.when(has_next)(with_next)

    x_copies = halo_copies(features.at[0, 0], features.at[0, 1], x_halo, halo_s, halo_r)
    loads[0].wait()
    pl.semaphore_wait(barrier, greeted)
    start_halo(x_copies)
    gates = ((group > 0, group < groups - 1, me + 2), (group < groups - 1, group > 0, me - 2))
    ends = jnp.logical_or(group == 0, group == groups - 1)

    def await_gate(slot):
        pl.when(gates[slot][0])(lambda: pl.semaphore_wait(gate.at[slot], 1))

    for slot, (_, onward, after) in enumerate(gates):
        pl.when(jnp.logical_not(ends))(lambda slot=slot: await_gate(slot))

        @pl.when(onward)
        def _(slot=slot, after=after):
            pl.semaphore_signal(
                gate.at[slot], inc=1, device_id={"space": after}, device_id_type=MESH
            )

    @pl.when(me == 0)
    def _():
        x_halo[0] = jnp.zeros(x_halo.shape[1:], BF16)
        g_halo[0] = jnp.zeros(g_halo.shape[1:], BF16)

    @pl.when(me == n - 1)
    def _():
        x_halo[1] = jnp.zeros(x_halo.shape[1:], BF16)
        g_halo[1] = jnp.zeros(g_halo.shape[1:], BF16)

    pad[:, :, 0:8, :] = jnp.zeros((2, ex, 8, ch), F32)
    pad[:, :, 8 + ez : 16 + ez, :] = jnp.zeros((2, ex, 8, ch), F32)
    for rim in (0, ex + 1):
        x3[:, rim] = jnp.zeros((4, ez, 3 * ch), BF16)
        g3[:, rim] = jnp.zeros((4, ez, 3 * ch), BF16)

    def spread_rows(dest, index, row, slot):
        pad[slot, :, 8 : 8 + ez, :] = row.astype(F32)
        dest[index, 1 : 1 + ex, :, 0:ch] = pad[slot, :, 7 : 7 + ez, :].astype(BF16)
        dest[index, 1 : 1 + ex, :, ch : 2 * ch] = row
        dest[index, 1 : 1 + ex, :, 2 * ch : 3 * ch] = pad[slot, :, 9 : 9 + ez, :].astype(BF16)

    def window(source, index, shift):
        return source[index, shift : shift + ex].reshape(plane, 3 * ch)

    def taps(sy, sx):
        first = sy * 9 + sx * 3
        return w_fine[first : first + 3].reshape(3 * ch, ch)

    def mm(a, b):
        return jnp.dot(a, b, preferred_element_type=F32)

    spread_rows(x3, 1, features[0, 0], 0)
    spread_rows(x3, 2, features[0, 1], 1)
    loads[1].wait()
    total = None
    for sx in range(3):
        term = mm(window(x3, 1, sx), jnp.concatenate([taps(1, sx), taps(0, sx)], axis=1))
        total = term if total is None else total + term
        total = total + mm(
            window(x3, 2, sx), jnp.concatenate([taps(2, sx), taps(1, sx)], axis=1)
        )
    act[...] = total
    for slot in range(2):
        pl.when(ends)(lambda slot=slot: await_gate(slot))
    wait_halo(x_copies)
    spread_rows(x3, 0, x_halo[0], 0)
    spread_rows(x3, 3, x_halo[1], 1)
    for side in range(2):
        total = act[:, side * ch : (side + 1) * ch]
        for sx in range(3):
            total = total + mm(window(x3, 3 * side, sx), taps(2 * side, sx))
        act[:, side * ch : (side + 1) * ch] = total
        value = features[0, side].reshape(plane, ch).astype(F32) + total * jax.nn.sigmoid(total)
        hid[side] = value.astype(BF16).astype(F32).reshape(hx, 2, ez, ch)

    for t in range(8):
        i, j, k = t // 4, t // 2 % 2, t % 2
        piece = hid[i, :, j, pl.ds(k, hz, stride=2), :].reshape(hx * hz, ch)
        folded[k, :, t // 2 * ch : (t // 2 + 1) * ch] = piece.astype(BF16)
    loads[2].wait()
    coarse = mm(folded[0], jnp.concatenate([w_down[t] for t in range(0, 8, 2)], axis=0))
    coarse = coarse + mm(folded[1], jnp.concatenate([w_down[t] for t in range(1, 8, 2)], axis=0))
    coarse = coarse.astype(BF16).astype(F32)
    for h in range(halves):
        stage[pl.ds(h, hx * hz, stride=halves), :] = coarse[:, h * lanes : (h + 1) * lanes]
    fwd_send[...] = stage[...].astype(BF16).reshape(n, rows, lanes)

    def exchange(src_of, slot, send, recv):
        out = []
        for k in range(n - 1, 0, -1):
            step = jnp.where(me < n // 2, k, n - k)
            who = lax.rem(me + step, n)
            copy = to_space(src_of(who), slot(), send.at[step - 1], recv.at[step - 1], who)
            copy.start()
            out.append(copy)
        return out

    coarse_copies = exchange(
        lambda who: fwd_send.at[who], lambda: fwd_recv.at[me], fwd_s, fwd_r
    )
    fold_copy = to_space(folded.at[1 - side_of], fold_met, fold_s, fold_r, partner)
    fold_copy.start()
    fwd_recv[me] = fwd_send[me]

    loads[3].wait()
    loads[4].wait()
    for sx in range(3):
        for j in range(4):
            xt[sx, :, j * plane : (j + 1) * plane] = window(x3, j, sx).T

    for copy in coarse_copies:
        copy.wait()
    stage[...] = fwd_recv[...].reshape(n * rows, lanes).astype(F32)
    columns = jnp.concatenate([stage[pl.ds(r, n, stride=rows), :] for r in range(rows)], axis=1)
    columns16 = columns.astype(BF16)
    mix = mixing[...]
    mixed = mm(mix, columns16)
    sigma = jax.nn.sigmoid(mixed)
    bottleneck[0] = (columns + mixed * sigma).astype(BF16)
    cot = cotangent[0].astype(F32)
    mixed_grad = (cot * (sigma * (1.0 + mixed * (1.0 - sigma)))).astype(BF16)
    spread = lax.dot_general(mix, mixed_grad, CONTRACT_FIRST, preferred_element_type=F32)
    column_grad = cot + spread
    for r in range(rows):
        stage[pl.ds(r, n, stride=rows), :] = column_grad[:, r * lanes : (r + 1) * lanes]
    back_send[...] = stage[...].astype(BF16).reshape(n, rows, lanes)
    back_copies = exchange(
        lambda who: back_send.at[pl.ds(who // 2 * 2, 2)], lambda: back_recv.at[:, me],
        back_s, back_r,
    )
    for side in range(2):
        back_recv[side, me] = back_send[2 * group + side]
    term = lax.dot_general(mixed_grad, columns16, CONTRACT_LAST, preferred_element_type=F32)
    mix_send[...] = jnp.zeros(mix_send.shape, F32)
    mix_send[:, 0:n] = term
    mix_copies = exchange(lambda who: mix_send, lambda: mix_recv.at[me], mix_s, mix_r)
    mix_recv[me] = mix_send[...]
    value = act[...]
    sig = jax.nn.sigmoid(value)
    act[...] = sig * (1.0 + value * (1.0 - sig))

    fold_copy.wait()
    turned_taps = jnp.concatenate([folded[side_of], fold_met[...]], axis=0).T
    folded_t[...] = turned_taps.reshape(groups, ch, 2 * hx * hz)
    turn_copy = to_peer(
        folded_t.at[:, pl.ds(pl.multiple_of(other * down_part, 16), down_part), :],
        fold_peer, turn_s, turn_r,
    )
    turn_copy.start()

    def flat_of(source, side):
        stage[...] = source[side].reshape(n * rows, lanes).astype(F32)
        return jnp.concatenate(
            [stage[pl.ds(h, hx * hz, stride=halves), :] for h in range(halves)], axis=1
        ).astype(BF16)

    for copy in back_copies:
        copy.wait()
    flat_copy = to_peer(back_recv, back_peer, dpeer_s, dpeer_r)
    flat_copy.start()
    flat = flat_of(back_recv, side_of)

    for t in range(8):
        i, j, k = t // 4, t // 2 % 2, t % 2
        piece = lax.dot_general(flat, w_down[t], CONTRACT_LAST, preferred_element_type=F32)
        hid_grad[i, :, j, pl.ds(k, hz, stride=2), :] = piece.reshape(hx, hz, ch)
    for side in range(2):
        grad = hid_grad[side].reshape(plane, ch) * act[:, side * ch : (side + 1) * ch]
        grad16[side] = grad.astype(BF16).reshape(ex, ez, ch)
    g_copies = halo_copies(grad16.at[0], grad16.at[1], g_halo, ghalo_s, ghalo_r)

    near = (side_of == 1, side_of == 0)
    away = (
        jnp.logical_and(side_of == 0, has_prev), jnp.logical_and(side_of == 1, has_next)
    )

    def start_some(conditions):
        for condition, copy in zip(conditions, g_copies):
            pl.when(condition)(copy.start)

    start_some(away)
    def send_down():
        turn_copy.wait()
        flat_copy.wait()
        taps_here = folded_t[:, pl.ds(pl.multiple_of(core * down_part, 16), down_part), :]
        left = jnp.concatenate([taps_here, fold_peer[...]], axis=2)
        right = jnp.concatenate(
            [
                flat, flat_of(back_recv, 1 - side_of),
                flat_of(back_peer, side_of), flat_of(back_peer, 1 - side_of),
            ],
            axis=0,
        )
        total = mm(left.reshape(groups * down_part, 4 * hx * hz), right)
        down16[...] = total.astype(BF16).reshape(groups, down_part, cc)

    def start_down():
        for step in range(groups - 1):
            to = lax.rem(group + step + 1, groups)
            to_space(
                down16.at[to], down_recv.at[group], down_s.at[step], down_r.at[step],
                2 * to + side_of,
            ).start()
        down_recv[group] = down16[group]

    def wait_down():
        for step in range(groups - 1):
            source = lax.rem(group - 1 - step + groups, groups)
            to_space(
                down16.at[source], down_recv.at[source], down_s.at[step], down_r.at[step], partner
            ).wait()

    flip = group + 1 - 2 * lax.rem(group, 2)
    across = lax.rem(group + 2, groups)
    owners = (lax.rem(flip + 2, groups), across, flip, group)
    orders = ((8, 7, 6, 5, 4, 3, 2, 1, 0), (6, 5, 4, 8, 7, 2, 1, 0, 3))
    orders = orders + tuple(tuple(8 - t for t in order) for order in orders[::-1])

    flat_grad = grad16[...].reshape(2 * plane, ch)

    def fine_block(i):
        t = orders[0][i]
        for g in range(1, groups):
            t = jnp.where(group == g, orders[g][i], t)
        sy, sx = t // 3, lax.rem(t, 3)
        window_t = xt[sx, :, pl.ds(pl.multiple_of(sy * plane, lanes), 2 * plane)]
        start = pl.multiple_of(t * 3 * ch, lanes)
        fine16[pl.ds(start, 3 * ch), :] = mm(window_t, flat_grad).astype(BF16)

    peer_copies = []

    def fine_to_peer(k):
        for j in range(2):
            who = 2 * owners[k] + j
            start = pl.multiple_of(who * fine_rows + other * fine_step, 16)
            copy = to_peer(
                fine16.at[pl.ds(start, part), :], fine_peer.at[who],
                peer_s.at[2 * k + j], peer_r.at[2 * k + j],
            )
            copy.start()
            peer_copies.append(copy)

    def fine_own(who):
        start = pl.multiple_of(who * fine_rows + core * fine_step, 16)
        return fine16[pl.ds(start, part), :].astype(F32) + fine_peer[who].astype(F32)

    pieces = 2
    height = part // pieces

    def own_rows(who, first, count):
        start = pl.multiple_of(who * fine_rows + core * fine_step + first, 16)
        mine = fine16[pl.ds(start, count), :].astype(F32)
        return mine + fine_peer[who, first : first + count].astype(F32)

    def slot_copy(slot, piece, who):
        rows_of = pl.ds(piece * height, height)
        index = slot * pieces + piece
        return to_space(
            fine_send.at[slot, rows_of], fine_recv.at[slot, rows_of],
            fine_s.at[index], fine_r.at[index], who,
        )

    def whole_copy(slot, who):
        return to_space(
            fine_send.at[slot], fine_recv.at[slot],
            fine_s.at[slot * pieces], fine_r.at[slot * pieces], who,
        )

    far_copies = [[None] * 3 for _ in range(pieces)]

    def met_peer(k):
        peer_copies[2 * k].wait()
        peer_copies[2 * k + 1].wait()

    def far_piece(piece, first, k):
        to = 2 * owners[k]
        targets = ((2, 1 - side_of), (1, side_of)) if k == 0 else ((0, 1 - side_of),)
        for slot, side in targets:
            fine_send[slot, first : first + height] = own_rows(to + side, first, height).astype(BF16)
            at = (partner, 2 * flip + side_of, 2 * flip + 1 - side_of)[slot]
            copy = slot_copy(slot, piece, at)
            copy.start()
            far_copies[piece][slot] = copy
        if k == 1:
            fine_keep[0, first : first + height] = own_rows(to + side_of, first, height)

    near_copies = {}

    def near_piece(k):
        met_peer(k)
        fine_send[k + 1] = fine_own(2 * owners[k] + 1 - side_of).astype(BF16)
        near_copies[k + 1] = whole_copy(k + 1, partner)
        near_copies[k + 1].start()
        fine_keep[k - 1] = fine_own(2 * owners[k] + side_of)

    def near_on():
        near_copies[3].wait()
        fine_send[5] = (fine_keep[1] + fine_recv[3].astype(F32)).astype(BF16)
        near_copies[5] = whole_copy(5, 2 * flip + side_of)
        near_copies[5].start()

    cross_copies = []

    def cross_piece(piece):
        for copy in far_copies[piece]:
            copy.wait_recv()
        first = piece * height
        rows_of = slice(first, first + height)
        total = fine_keep[0, rows_of] + sum(fine_recv[j, rows_of].astype(F32) for j in range(3))
        fine_send[6, rows_of] = total.astype(BF16)
        copy = slot_copy(6, piece, 2 * across + side_of)
        copy.start()
        cross_copies.append(copy)

    ready = {3: 0, 5: 1, 8: 2, 9: 3}
    for i in range(9):
        fine_block(i)
        if i + 1 in ready:
            fine_to_peer(ready[i + 1])
    met_peer(0)
    far_piece(0, 0, 0)
    met_peer(1)
    far_piece(0, 0, 1)
    for piece in range(1, pieces):
        far_piece(piece, piece * height, 0)
        far_piece(piece, piece * height, 1)
    near_piece(2)
    near_piece(3)
    send_down()
    start_down()

    def turned(i, sx):
        first = i * 9 + sx * 3
        return jnp.concatenate([w_fine[first + 2 - m] for m in range(3)], axis=1)

    def mt(a, b):
        return lax.dot_general(a, b, CONTRACT_LAST, preferred_element_type=F32)

    spread_rows(g3, 1, grad16[0], 0)
    spread_rows(g3, 2, grad16[1], 1)
    total = None
    for sx in range(3):
        term = mt(window(g3, 1, 2 - sx), jnp.concatenate([turned(1, sx), turned(2, sx)], axis=0))
        total = term if total is None else total + term
        total = total + mt(
            window(g3, 2, 2 - sx), jnp.concatenate([turned(0, sx), turned(1, sx)], axis=0)
        )
    act[...] = total
    start_some(near)
    for piece in range(pieces):
        cross_piece(piece)
    for copies in far_copies:
        for copy in copies:
            copy.wait_send()
    near_on()
    wait_halo(g_copies)
    spread_rows(g3, 0, g_halo[0], 0)
    spread_rows(g3, 3, g_halo[1], 1)
    for side in range(2):
        total = act[:, side * ch : (side + 1) * ch] + hid_grad[side].reshape(plane, ch)
        for sx in range(3):
            total = total + mt(window(g3, 3 * side, 2 - sx), turned(2 - 2 * side, sx))
        feature_grad[0, side] = total.astype(BF16).reshape(ex, ez, ch)


    for copy in mix_copies:
        copy.wait()
    mix_total[...] = sum(mix_recv[s] for s in range(n)) * scale
    mix_swap = to_peer(mix_total, mix_peer, last_s.at[0], last_r.at[0])
    mix_swap.start()

    wait_down()
    value = sum(down_recv[s].astype(F32) for s in range(groups)) * scale
    for h in range(halves):
        down_half[pl.ds(h, down_part, stride=halves), :] = value[:, h * lanes : (h + 1) * lanes]
    down_swap = to_peer(down_half, down_half_peer, last_s.at[1], last_r.at[1])
    down_swap.start()

    near_copies[4].wait()
    near_copies[5].wait()
    fine_swaps = []
    for piece, copy in enumerate(cross_copies):
        rows_of = slice(piece * height, (piece + 1) * height)
        value = fine_keep[2, rows_of] + sum(fine_recv[j, rows_of].astype(F32) for j in (4, 5))
        copy.wait()
        fine_half[rows_of] = (value + fine_recv[6, rows_of].astype(F32)) * scale
        swap = to_peer(
            fine_half.at[pl.ds(piece * height, height)],
            fine_half_peer.at[pl.ds(piece * height, height)],
            last_s.at[2 + piece], last_r.at[2 + piece],
        )
        swap.start()
        fine_swaps.append(swap)

    skew = fine_mine - fine_step

    def put_fine(source, whose):
        fine_out[pl.ds(pl.multiple_of(whose * fine_mine, 8), fine_mine), :] = source[
            pl.ds(pl.multiple_of(whose * skew, 8), fine_mine), :
        ]

    down_len = down_part * halves
    put_fine(fine_half, core)
    down_out[pl.ds(pl.multiple_of(core * down_len, 8), down_len), :] = down_half[...]
    mix_swap.wait()
    mix_total[...] = mix_total[...] + mix_peer[...]
    mixing_out[...] = mix_total[pl.ds(me, 1), 0:n]
    down_swap.wait()
    down_out[pl.ds(pl.multiple_of(other * down_len, 8), down_len), :] = down_half_peer[...]
    for swap in fine_swaps:
        swap.wait()
    put_fine(fine_half_peer, other)


def put_out(*refs):
    sources, dests, done = refs[:5], refs[5:10], refs[10]
    copies = [
        pltpu.make_async_copy(source, dest, done.at[i])
        for i, (source, dest) in enumerate(zip(sources, dests))
    ]
    for copy in copies:
        copy.start()
    for copy in copies:
        copy.wait()


def fused_fits(mesh, features, w_down):
    n = mesh.shape["space"]
    batch, ny, ex, ez, ch = features.shape
    cc = w_down.shape[2]
    spots = ex * ez // 4
    return (
        batch == mesh.shape["groups"] * mesh.shape["sample"]
        and ny == 2 * n
        and mesh.shape["sample"] == 2
        and n == 8
        and w_down.shape[0] == 8
        and -(27 * ch // n // 2) // 16 % 2 == 0
        and ch == 128
        and cc % 128 == 0
        and ez % 16 == 0
        and ex % 2 == 0
        and spots % 8 == 0
        and (spots * cc) % (n * 128 * 16) == 0
        and (27 * ch) % (n * 16) == 0
        and (8 * ch) % (n * 32) == 0
    )


def fused(mesh, features, w_fine, w_down, mixing, cotangent):
    n = lax.axis_size("space")
    _, _, ex, ez, ch = features.shape
    cc = w_down.shape[2]
    batch = lax.axis_size("sample")
    scale = float(batch * 2 * n * ex * ez) ** (-0.5)
    plane, spots, lanes = ex * ez, ex * ez // 4, 128
    rows = spots * cc // lanes // n
    fine_rows, down_rows = 27 * ch // n, 8 * ch // n
    half = fine_rows // 2
    part = -(-half // 16) * 16
    down_part = down_rows // 2
    down_len = down_part * cc // lanes
    vm = pltpu.VMEM
    dma = pltpu.SemaphoreType.DMA
    groups = n // 2
    arrays = (features, w_fine, w_down, mixing, cotangent)
    scratch = [
        *[vm(array.shape, BF16) for array in arrays], dma((5,)),
        vm((2, ex, ez, ch), BF16), vm((2, ex, ez, ch), BF16), vm((2, ex, ez, ch), BF16),
        vm((2, ex, ez + 16, ch), F32),
        vm((4, ex + 2, ez, 3 * ch), BF16), vm((4, ex + 2, ez, 3 * ch), BF16),
        vm((3, 3 * ch, 4 * plane), BF16),
        vm((plane, 2 * ch), F32),
        vm((2, ex // 2, 2, ez, ch), F32),
        vm((2, spots, 4 * ch), BF16), vm((spots, 4 * ch), BF16),
        vm((groups, ch, 2 * spots), BF16),
        vm((n * rows, lanes), F32),
        vm((n, rows, lanes), BF16), vm((n, rows, lanes), BF16),
        vm((n, rows, lanes), BF16), vm((2, n, rows, lanes), BF16),
        vm((2, ex // 2, 2, ez, ch), F32),
        vm((27 * ch, ch), BF16),
        vm((n, part, ch), BF16), *[vm((7, part, ch), BF16)] * 2, vm((3, part, ch), F32),
        vm((groups, down_part, 2 * spots), BF16), vm((2, n, rows, lanes), BF16),
        *[vm((groups, down_part, cc), BF16)] * 2,
        vm((n, lanes), F32), vm((n, n, lanes), F32), vm((n, lanes), F32), vm((n, lanes), F32),
        vm((part, ch), F32), vm((part, ch), F32),
        vm((down_len, lanes), F32), vm((down_len, lanes), F32),
        dma((2,)), dma((2,)), dma((n - 1,)), dma((n - 1,)), dma((n - 1,)), dma((n - 1,)),
        dma((n - 1,)), dma((n - 1,)),
        dma((2,)), dma((2,)), dma((n,)), dma((n,)), dma, dma,
        *[dma] * 4,
        *[dma((7 * 2,))] * 2, *[dma((groups - 1,))] * 2, dma((4,)), dma((4,)),
        pltpu.SemaphoreType.REGULAR((2,)),
    ]
    spec = pl.BlockSpec(memory_space=pltpu.VMEM)
    far = pl.BlockSpec(memory_space=pltpu.HBM)
    shapes = (
        jax.ShapeDtypeStruct(cotangent.shape, BF16),
        jax.ShapeDtypeStruct(features.shape, BF16),
        jax.ShapeDtypeStruct((fine_rows, ch), F32),
        jax.ShapeDtypeStruct((down_rows * cc // lanes, lanes), F32),
        jax.ShapeDtypeStruct((1, n), F32),
    )
    results = pl.pallas_call(
        functools.partial(fused_body, (n, ex, ez, ch, cc, scale)),
        out_shape=shapes,
        in_specs=[far] * 5,
        out_specs=tuple([spec] * 5),
        scratch_shapes=scratch,
        compiler_params=pltpu.CompilerParams(
            collective_id=0, has_side_effects=True, vmem_limit_bytes=65472 * 1024
        ),
    )(*arrays)
    a, b, c, d, e = pl.pallas_call(
        put_out,
        out_shape=shapes,
        in_specs=[spec] * 5,
        out_specs=tuple([far] * 5),
        scratch_shapes=[dma((5,))],
        compiler_params=pltpu.CompilerParams(vmem_limit_bytes=65472 * 1024),
    )(*results)
    return a, b, c.reshape(-1), d.reshape(-1), e


def with_halo(array, sides, width):
    for axis, dim in sides:
        devices, length = (lax.axis_size(axis), array.shape[dim])
        up = [(i, (i + 1) % devices) for i in range(devices - 1)]
        down = [(j, i) for i, j in up]
        last = lax.slice_in_dim(array, length - width, length, axis=dim)
        initial = lax.slice_in_dim(array, 0, width, axis=dim)
        before = lax.ppermute(last, axis, up)
        after = lax.ppermute(initial, axis, down)
        array = jnp.concatenate([before, array, after], axis=dim)
    return array


def forward_conv(padded, weight, count):
    extent_x = padded.shape[2] - 2
    extent_z = padded.shape[3] - 2
    channels = padded.shape[4]
    total = None
    for shift_y in range(3):
        for shift_x in range(3):
            pieces = [
                padded[
                    :,
                    shift_y : shift_y + count,
                    shift_x : shift_x + extent_x,
                    shift_z : shift_z + extent_z,
                    :,
                ]
                for shift_z in range(3)
            ]
            stacked = jnp.concatenate(pieces, axis=-1).reshape(-1, 3 * channels)
            first = shift_y * 9 + shift_x * 3
            kernel = weight[first : first + 3].reshape(3 * channels, weight.shape[2])
            term = jnp.dot(stacked, kernel, preferred_element_type=jnp.float32)
            total = term if total is None else total + term
    return total.reshape(padded.shape[0], count, extent_x, extent_z, weight.shape[2])


def transposed_conv(padded, weight, count):
    extent_x = padded.shape[2] - 2
    extent_z = padded.shape[3] - 2
    channels = padded.shape[4]
    total = None
    for shift_y in range(3):
        for shift_x in range(3):
            pieces = [
                padded[
                    :,
                    2 - shift_y : 2 - shift_y + count,
                    2 - shift_x : 2 - shift_x + extent_x,
                    2 - shift_z : 2 - shift_z + extent_z,
                    :,
                ]
                for shift_z in range(3)
            ]
            stacked = jnp.concatenate(pieces, axis=-1).reshape(-1, 3 * channels)
            first = shift_y * 9 + shift_x * 3
            kernel = jnp.swapaxes(weight[first : first + 3], 1, 2).reshape(
                3 * channels, weight.shape[1]
            )
            term = jnp.dot(stacked, kernel, preferred_element_type=jnp.float32)
            total = term if total is None else total + term
    return total.reshape(padded.shape[0], count, extent_x, extent_z, weight.shape[1])


def weight_terms(padded, grad, count):
    extent_x = padded.shape[2] - 2
    extent_z = padded.shape[3] - 2
    channels = padded.shape[4]
    flat_grad = grad.reshape(-1, grad.shape[4])
    blocks = []
    for shift_y in range(3):
        for shift_x in range(3):
            pieces = [
                padded[
                    :,
                    shift_y : shift_y + count,
                    shift_x : shift_x + extent_x,
                    shift_z : shift_z + extent_z,
                    :,
                ]
                for shift_z in range(3)
            ]
            stacked = jnp.concatenate(pieces, axis=-1).reshape(-1, 3 * channels)
            blocks.append(
                lax.dot_general(
                    stacked, flat_grad, (((0,), (0,)), ((), ())), preferred_element_type=jnp.float32
                )
            )
    return jnp.concatenate(blocks, axis=0).reshape(-1)


def fold_taps(hidden):
    batch, rows_here, extent_x, extent_z, channels = hidden.shape
    shaped = hidden.reshape(batch, rows_here // 2, 2, extent_x // 2, 2, extent_z // 2, 2, channels)
    return shaped.transpose(0, 1, 3, 5, 2, 4, 6, 7).reshape(-1, 8 * channels)


def unfold_taps(values, batch, rows_here, extent_x, extent_z, channels):
    shaped = values.reshape(batch, rows_here // 2, extent_x // 2, extent_z // 2, 2, 2, 2, channels)
    return shaped.transpose(0, 1, 4, 2, 5, 3, 6, 7).reshape(
        batch, rows_here, extent_x, extent_z, channels
    )


def silu_slope(value):
    sigma = jax.nn.sigmoid(value)
    return sigma * (1.0 + value * (1.0 - sigma))


def local(features, w_fine, w_down, mixing, cotangent):
    batch, rows_here, extent_x, extent_z, channels = features.shape
    coarse_ch = w_down.shape[2]
    rimmed = with_halo(features, (("space", 1),), 1)
    xpadded = jnp.pad(rimmed, ((0, 0), (0, 0), (1, 1), (1, 1), (0, 0)))
    act = forward_conv(xpadded, w_fine, rows_here)
    hidden = (features.astype(jnp.float32) + jax.nn.silu(act)).astype(jnp.bfloat16)
    folded = fold_taps(hidden)
    down_matrix = w_down.reshape(8 * channels, coarse_ch)
    coarse = jnp.dot(folded, down_matrix, preferred_element_type=jnp.float32).astype(jnp.bfloat16)
    coarse = coarse.reshape(batch, rows_here // 2, -1)
    columns = lax.all_to_all(coarse, "space", split_axis=2, concat_axis=1, tiled=True)
    mixed = jnp.stack([jnp.dot(mixing, columns[0], preferred_element_type=jnp.float32)])
    bottleneck = (columns.astype(jnp.float32) + jax.nn.silu(mixed)).astype(jnp.bfloat16)
    cot = cotangent.astype(jnp.float32)
    mixed_grad = (cot * silu_slope(mixed)).astype(jnp.bfloat16)
    term = lax.dot_general(
        mixed_grad[0], columns[0], (((1,), (1,)), ((), ())), preferred_element_type=jnp.float32
    )
    spread_list = [
        lax.dot_general(
            mixing, mixed_grad[0], (((0,), (0,)), ((), ())), preferred_element_type=jnp.float32
        )
    ]
    column_grad = (cot + jnp.stack(spread_list)).astype(jnp.bfloat16)
    coarse_grad = lax.all_to_all(column_grad, "space", split_axis=1, concat_axis=2, tiled=True)
    flat_coarse = coarse_grad.reshape(-1, coarse_ch)
    down_terms = lax.dot_general(
        folded, flat_coarse, (((0,), (0,)), ((), ())), preferred_element_type=jnp.float32
    ).reshape(-1)
    hidden_grad = unfold_taps(
        jnp.dot(flat_coarse, down_matrix.T, preferred_element_type=jnp.float32),
        batch,
        rows_here,
        extent_x,
        extent_z,
        channels,
    )
    act_grad = (hidden_grad * silu_slope(act)).astype(jnp.bfloat16)
    grad_rim = with_halo(act_grad, (("space", 1),), 1)
    gpadded = jnp.pad(grad_rim, ((0, 0), (0, 0), (1, 1), (1, 1), (0, 0)))
    spread = transposed_conv(gpadded, w_fine, rows_here)
    feature_grad = (hidden_grad + spread).astype(jnp.bfloat16)
    fine_terms = weight_terms(xpadded, act_grad, rows_here)
    scale = float(
        batch * lax.axis_size("sample") * rows_here * lax.axis_size("space") * extent_x * extent_z
    ) ** (-0.5)
    shares = (
        lax.psum_scatter(fine_terms, "space", scatter_dimension=0, tiled=True),
        lax.psum_scatter(down_terms, "space", scatter_dimension=0, tiled=True),
        lax.psum_scatter(term, "space", scatter_dimension=0, tiled=True),
    )
    totals = lax.psum((shares[0], shares[1], shares[2]), "sample")
    return (bottleneck, feature_grad, totals[0] * scale, totals[1] * scale, totals[2] * scale)


def solution(mesh):
    placed = (
        P(("groups", "sample"), "space", None, None, None),
        P(),
        P(),
        P(),
        P(("groups", "sample"), None, "space"),
    )
    out_specs = (
        P(("groups", "sample"), None, "space"),
        P(("groups", "sample"), "space", None, None, None),
        P(("groups", "space")),
        P(("groups", "space")),
        P(("groups", "space"), None),
    )

    def step(features, w_fine, w_down, mixing, cotangent):
        kernel = functools.partial(fused, mesh) if fused_fits(mesh, features, w_down) else local
        mapped = jax.shard_map(
            kernel, mesh=mesh, in_specs=placed, out_specs=out_specs, check_vma=False
        )
        return mapped(features, w_fine, w_down, mixing, cotangent)

    return step
```

```python
import functools

import jax
import jax.numpy as jnp
from jax import lax
from jax.experimental import pallas as pl
from jax.experimental.pallas import tpu as pltpu
from jax.sharding import PartitionSpec as P

MESH = pl.DeviceIdType.MESH
F32 = jnp.float32
BF16 = jnp.bfloat16
CONTRACT_LAST = (((1,), (1,)), ((), ()))
CONTRACT_FIRST = (((0,), (0,)), ((), ()))


def fused_body(
    cfg,
    features_in, w_fine_in, w_down_in, mixing_in, cotangent_in,
    bottleneck, feature_grad, fine_out, down_out, mixing_out,
    features, w_fine, w_down, mixing, cotangent, load_s,
    x_halo, g_halo, grad16, pad, x3, g3, xt, act, hid, folded, fold_met, folded_t,
    stage, fwd_send, fwd_recv, back_send, back_recv, hid_grad,
    fine16, fine_peer, fine_send, fine_recv, fine_keep,
    fold_peer, back_peer, down16, down_recv,
    mix_send, mix_recv, mix_total, mix_peer,
    fine_half, fine_half_peer, down_half, down_half_peer,
    halo_s, halo_r, fwd_s, fwd_r, back_s, back_r, mix_s, mix_r,
    ghalo_s, ghalo_r, peer_s, peer_r, dpeer_s, dpeer_r,
    fold_s, fold_r, turn_s, turn_r, fine_s, fine_r, down_s, down_r, last_s, last_r,
    gate,
):
    n, ex, ez, ch, cc, scale = cfg
    plane = ex * ez
    hx, hz = ex // 2, ez // 2
    lanes = 128
    rows = hx * hz * cc // lanes // n
    halves = cc // lanes
    fine_rows = 27 * ch // n
    part = fine_send.shape[1]
    fine_step = fine_rows - part
    fine_mine = fine_rows // 2
    down_rows = 8 * ch // n
    down_part = down_rows // 2
    me = lax.axis_index("space")
    core = lax.axis_index("sample")
    other = 1 - core

    def to_space(src, dst, send, recv, who):
        return pltpu.make_async_remote_copy(
            src_ref=src, dst_ref=dst, send_sem=send, recv_sem=recv,
            device_id={"space": who}, device_id_type=MESH,
        )

    def to_peer(src, dst, send, recv):
        return pltpu.make_async_remote_copy(
            src_ref=src, dst_ref=dst, send_sem=send, recv_sem=recv,
            device_id={"sample": other}, device_id_type=MESH,
        )

    has_prev, has_next = me > 0, me < n - 1
    groups = n // 2
    group, side_of = me // 2, lax.rem(me, 2)
    partner = me + 1 - 2 * side_of

    barrier = pltpu.get_barrier_semaphore()
    greeted = 1
    for shift in (-2, -1, 1, 2):
        who = me + shift
        inside = jnp.logical_and(who >= 0, who < n)
        greeted = greeted + inside.astype(jnp.int32)

        @pl.when(inside)
        def _(who=who):
            pl.semaphore_signal(barrier, inc=1, device_id={"space": who}, device_id_type=MESH)

    pl.semaphore_signal(barrier, inc=1, device_id={"sample": other}, device_id_type=MESH)
    loads = [
        pltpu.make_async_copy(source, dest, load_s.at[i])
        for i, (source, dest) in enumerate(
            (
                (features_in, features),
                (w_fine_in, w_fine),
                (w_down_in, w_down),
                (mixing_in, mixing),
                (cotangent_in, cotangent),
            )
        )
    ]
    for load in loads:
        load.start()

    def halo_copies(first, last, halo, send, recv):
        down = to_space(first, halo.at[1], send.at[0], recv.at[1], me - 1)
        up = to_space(last, halo.at[0], send.at[1], recv.at[0], me + 1)
        return down, up

    def start_halo(copies):
        pl.when(has_prev)(copies[0].start)
        pl.when(has_next)(copies[1].start)

    def wait_halo(copies):
        def with_prev():
            copies[0].wait_send()
            copies[1].wait_recv()

        def with_next():
            copies[1].wait_send()
            copies[0].wait_recv()

        pl.when(has_prev)(with_prev)
        pl.when(has_next)(with_next)

    x_copies = halo_copies(features.at[0, 0], features.at[0, 1], x_halo, halo_s, halo_r)
    loads[0].wait()
    pl.semaphore_wait(barrier, greeted)
    start_halo(x_copies)
    gates = ((group > 0, group < groups - 1, me + 2), (group < groups - 1, group > 0, me - 2))
    ends = jnp.logical_or(group == 0, group == groups - 1)

    def await_gate(slot):
        pl.when(gates[slot][0])(lambda: pl.semaphore_wait(gate.at[slot], 1))

    for slot, (_, onward, after) in enumerate(gates):
        pl.when(jnp.logical_not(ends))(lambda slot=slot: await_gate(slot))

        @pl.when(onward)
        def _(slot=slot, after=after):
            pl.semaphore_signal(
                gate.at[slot], inc=1, device_id={"space": after}, device_id_type=MESH
            )

    @pl.when(me == 0)
    def _():
        x_halo[0] = jnp.zeros(x_halo.shape[1:], BF16)
        g_halo[0] = jnp.zeros(g_halo.shape[1:], BF16)

    @pl.when(me == n - 1)
    def _():
        x_halo[1] = jnp.zeros(x_halo.shape[1:], BF16)
        g_halo[1] = jnp.zeros(g_halo.shape[1:], BF16)

    pad[:, :, 0:8, :] = jnp.zeros((2, ex, 8, ch), F32)
    pad[:, :, 8 + ez : 16 + ez, :] = jnp.zeros((2, ex, 8, ch), F32)
    for rim in (0, ex + 1):
        x3[:, rim] = jnp.zeros((4, ez, 3 * ch), BF16)
        g3[:, rim] = jnp.zeros((4, ez, 3 * ch), BF16)

    def spread_rows(dest, index, row, slot):
        pad[slot, :, 8 : 8 + ez, :] = row.astype(F32)
        dest[index, 1 : 1 + ex, :, 0:ch] = pad[slot, :, 7 : 7 + ez, :].astype(BF16)
        dest[index, 1 : 1 + ex, :, ch : 2 * ch] = row
        dest[index, 1 : 1 + ex, :, 2 * ch : 3 * ch] = pad[slot, :, 9 : 9 + ez, :].astype(BF16)

    def window(source, index, shift):
        return source[index, shift : shift + ex].reshape(plane, 3 * ch)

    def taps(sy, sx):
        first = sy * 9 + sx * 3
        return w_fine[first : first + 3].reshape(3 * ch, ch)

    def mm(a, b):
        return jnp.dot(a, b, preferred_element_type=F32)

    spread_rows(x3, 1, features[0, 0], 0)
    spread_rows(x3, 2, features[0, 1], 1)
    loads[1].wait()
    total = None
    for sx in range(3):
        term = mm(window(x3, 1, sx), jnp.concatenate([taps(1, sx), taps(0, sx)], axis=1))
        total = term if total is None else total + term
        total = total + mm(
            window(x3, 2, sx), jnp.concatenate([taps(2, sx), taps(1, sx)], axis=1)
        )
    act[...] = total
    for slot in range(2):
        pl.when(ends)(lambda slot=slot: await_gate(slot))
    wait_halo(x_copies)
    spread_rows(x3, 0, x_halo[0], 0)
    spread_rows(x3, 3, x_halo[1], 1)
    for side in range(2):
        total = act[:, side * ch : (side + 1) * ch]
        for sx in range(3):
            total = total + mm(window(x3, 3 * side, sx), taps(2 * side, sx))
        act[:, side * ch : (side + 1) * ch] = total
        value = features[0, side].reshape(plane, ch).astype(F32) + total * jax.nn.sigmoid(total)
        hid[side] = value.astype(BF16).astype(F32).reshape(hx, 2, ez, ch)

    for t in range(8):
        i, j, k = t // 4, t // 2 % 2, t % 2
        piece = hid[i, :, j, pl.ds(k, hz, stride=2), :].reshape(hx * hz, ch)
        folded[k, :, t // 2 * ch : (t // 2 + 1) * ch] = piece.astype(BF16)
    loads[2].wait()
    coarse = mm(folded[0], jnp.concatenate([w_down[t] for t in range(0, 8, 2)], axis=0))
    coarse = coarse + mm(folded[1], jnp.concatenate([w_down[t] for t in range(1, 8, 2)], axis=0))
    coarse = coarse.astype(BF16).astype(F32)
    for h in range(halves):
        stage[pl.ds(h, hx * hz, stride=halves), :] = coarse[:, h * lanes : (h + 1) * lanes]
    fwd_send[...] = stage[...].astype(BF16).reshape(n, rows, lanes)

    def exchange(src_of, slot, send, recv):
        out = []
        for k in range(n - 1, 0, -1):
            step = jnp.where(me < n // 2, k, n - k)
            who = lax.rem(me + step, n)
            copy = to_space(src_of(who), slot(), send.at[step - 1], recv.at[step - 1], who)
            copy.start()
            out.append(copy)
        return out

    coarse_copies = exchange(
        lambda who: fwd_send.at[who], lambda: fwd_recv.at[me], fwd_s, fwd_r
    )
    fold_copy = to_space(folded.at[1 - side_of], fold_met, fold_s, fold_r, partner)
    fold_copy.start()
    fwd_recv[me] = fwd_send[me]

    loads[3].wait()
    loads[4].wait()
    for sx in range(3):
        for j in range(4):
            xt[sx, :, j * plane : (j + 1) * plane] = window(x3, j, sx).T

    for copy in coarse_copies:
        copy.wait()
    stage[...] = fwd_recv[...].reshape(n * rows, lanes).astype(F32)
    columns = jnp.concatenate([stage[pl.ds(r, n, stride=rows), :] for r in range(rows)], axis=1)
    columns16 = columns.astype(BF16)
    mix = mixing[...]
    mixed = mm(mix, columns16)
    sigma = jax.nn.sigmoid(mixed)
    cot = cotangent[0].astype(F32)
    mixed_grad = (cot * (sigma * (1.0 + mixed * (1.0 - sigma)))).astype(BF16)
    spread = lax.dot_general(mix, mixed_grad, CONTRACT_FIRST, preferred_element_type=F32)
    column_grad = cot + spread
    for r in range(rows):
        stage[pl.ds(r, n, stride=rows), :] = column_grad[:, r * lanes : (r + 1) * lanes]
    back_send[...] = stage[...].astype(BF16).reshape(n, rows, lanes)
    back_copies = exchange(
        lambda who: back_send.at[pl.ds(who // 2 * 2, 2)], lambda: back_recv.at[:, me],
        back_s, back_r,
    )
    for side in range(2):
        back_recv[side, me] = back_send[2 * group + side]
    term = lax.dot_general(mixed_grad, columns16, CONTRACT_LAST, preferred_element_type=F32)
    mix_send[...] = jnp.zeros(mix_send.shape, F32)
    mix_send[:, 0:n] = term
    mix_copies = exchange(lambda who: mix_send, lambda: mix_recv.at[me], mix_s, mix_r)
    mix_recv[me] = mix_send[...]
    bottleneck[0] = (columns + mixed * sigma).astype(BF16)
    value = act[...]
    sig = jax.nn.sigmoid(value)
    act[...] = sig * (1.0 + value * (1.0 - sig))

    fold_copy.wait()
    turned_taps = jnp.concatenate([folded[side_of], fold_met[...]], axis=0).T
    folded_t[...] = turned_taps.reshape(groups, ch, 2 * hx * hz)
    turn_copy = to_peer(
        folded_t.at[:, pl.ds(pl.multiple_of(other * down_part, 16), down_part), :],
        fold_peer, turn_s, turn_r,
    )
    turn_copy.start()

    def flat_of(source, side):
        stage[...] = source[side].reshape(n * rows, lanes).astype(F32)
        return jnp.concatenate(
            [stage[pl.ds(h, hx * hz, stride=halves), :] for h in range(halves)], axis=1
        ).astype(BF16)

    for copy in back_copies:
        copy.wait()
    flat_copy = to_peer(back_recv, back_peer, dpeer_s, dpeer_r)
    flat_copy.start()
    flat = flat_of(back_recv, side_of)

    for t in range(8):
        i, j, k = t // 4, t // 2 % 2, t % 2
        piece = lax.dot_general(flat, w_down[t], CONTRACT_LAST, preferred_element_type=F32)
        hid_grad[i, :, j, pl.ds(k, hz, stride=2), :] = piece.reshape(hx, hz, ch)
    for side in range(2):
        grad = hid_grad[side].reshape(plane, ch) * act[:, side * ch : (side + 1) * ch]
        grad16[side] = grad.astype(BF16).reshape(ex, ez, ch)
    g_copies = halo_copies(grad16.at[0], grad16.at[1], g_halo, ghalo_s, ghalo_r)

    near = (side_of == 1, side_of == 0)
    away = (
        jnp.logical_and(side_of == 0, has_prev), jnp.logical_and(side_of == 1, has_next)
    )

    def start_some(conditions):
        for condition, copy in zip(conditions, g_copies):
            pl.when(condition)(copy.start)

    start_some(away)
    def send_down():
        turn_copy.wait()
        flat_copy.wait()
        taps_here = folded_t[:, pl.ds(pl.multiple_of(core * down_part, 16), down_part), :]
        left = jnp.concatenate([taps_here, fold_peer[...]], axis=2)
        right = jnp.concatenate(
            [
                flat, flat_of(back_recv, 1 - side_of),
                flat_of(back_peer, side_of), flat_of(back_peer, 1 - side_of),
            ],
            axis=0,
        )
        total = mm(left.reshape(groups * down_part, 4 * hx * hz), right)
        down16[...] = total.astype(BF16).reshape(groups, down_part, cc)

    def start_down():
        for step in range(groups - 1):
            to = lax.rem(group + step + 1, groups)
            to_space(
                down16.at[to], down_recv.at[group], down_s.at[step], down_r.at[step],
                2 * to + side_of,
            ).start()
        down_recv[group] = down16[group]

    def wait_down():
        for step in range(groups - 1):
            source = lax.rem(group - 1 - step + groups, groups)
            to_space(
                down16.at[source], down_recv.at[source], down_s.at[step], down_r.at[step], partner
            ).wait()

    flip = group + 1 - 2 * lax.rem(group, 2)
    across = lax.rem(group + 2, groups)
    owners = (lax.rem(flip + 2, groups), across, flip, group)
    orders = ((8, 7, 6, 5, 4, 3, 2, 1, 0), (6, 5, 4, 8, 7, 2, 1, 0, 3))
    orders = orders + tuple(tuple(8 - t for t in order) for order in orders[::-1])

    flat_grad = grad16[...].reshape(2 * plane, ch)

    def fine_block(i):
        t = orders[0][i]
        for g in range(1, groups):
            t = jnp.where(group == g, orders[g][i], t)
        sy, sx = t // 3, lax.rem(t, 3)
        window_t = xt[sx, :, pl.ds(pl.multiple_of(sy * plane, lanes), 2 * plane)]
        start = pl.multiple_of(t * 3 * ch, lanes)
        fine16[pl.ds(start, 3 * ch), :] = mm(window_t, flat_grad).astype(BF16)

    peer_copies = []

    def fine_to_peer(k):
        for j in range(2):
            who = 2 * owners[k] + j
            start = pl.multiple_of(who * fine_rows + other * fine_step, 16)
            copy = to_peer(
                fine16.at[pl.ds(start, part), :], fine_peer.at[who],
                peer_s.at[2 * k + j], peer_r.at[2 * k + j],
            )
            copy.start()
            peer_copies.append(copy)

    def fine_own(who):
        start = pl.multiple_of(who * fine_rows + core * fine_step, 16)
        return fine16[pl.ds(start, part), :].astype(F32) + fine_peer[who].astype(F32)

    pieces = 2
    height = part // pieces

    def own_rows(who, first, count):
        start = pl.multiple_of(who * fine_rows + core * fine_step + first, 16)
        mine = fine16[pl.ds(start, count), :].astype(F32)
        return mine + fine_peer[who, first : first + count].astype(F32)

    def slot_copy(slot, piece, who):
        rows_of = pl.ds(piece * height, height)
        index = slot * pieces + piece
        return to_space(
            fine_send.at[slot, rows_of], fine_recv.at[slot, rows_of],
            fine_s.at[index], fine_r.at[index], who,
        )

    def whole_copy(slot, who):
        return to_space(
            fine_send.at[slot], fine_recv.at[slot],
            fine_s.at[slot * pieces], fine_r.at[slot * pieces], who,
        )

    far_copies = [[None] * 3 for _ in range(pieces)]

    def met_peer(k):
        peer_copies[2 * k].wait()
        peer_copies[2 * k + 1].wait()

    def far_piece(piece, first, k):
        to = 2 * owners[k]
        targets = ((2, 1 - side_of), (1, side_of)) if k == 0 else ((0, 1 - side_of),)
        for slot, side in targets:
            fine_send[slot, first : first + height] = own_rows(to + side, first, height).astype(BF16)
            at = (partner, 2 * flip + side_of, 2 * flip + 1 - side_of)[slot]
            copy = slot_copy(slot, piece, at)
            copy.start()
            far_copies[piece][slot] = copy
        if k == 1:
            fine_keep[0, first : first + height] = own_rows(to + side_of, first, height)

    near_copies = {}

    def near_piece(k):
        met_peer(k)
        fine_send[k + 1] = fine_own(2 * owners[k] + 1 - side_of).astype(BF16)
        near_copies[k + 1] = whole_copy(k + 1, partner)
        near_copies[k + 1].start()
        fine_keep[k - 1] = fine_own(2 * owners[k] + side_of)

    def near_on():
        near_copies[3].wait()
        fine_send[5] = (fine_keep[1] + fine_recv[3].astype(F32)).astype(BF16)
        near_copies[5] = whole_copy(5, 2 * flip + side_of)
        near_copies[5].start()

    cross_copies = []

    def cross_piece(piece):
        for copy in far_copies[piece]:
            copy.wait_recv()
        first = piece * height
        rows_of = slice(first, first + height)
        total = fine_keep[0, rows_of] + sum(fine_recv[j, rows_of].astype(F32) for j in range(3))
        fine_send[6, rows_of] = total.astype(BF16)
        copy = slot_copy(6, piece, 2 * across + side_of)
        copy.start()
        cross_copies.append(copy)

    ready = {3: 0, 5: 1, 8: 2, 9: 3}
    for i in range(9):
        fine_block(i)
        if i + 1 in ready:
            fine_to_peer(ready[i + 1])
    met_peer(0)
    far_piece(0, 0, 0)
    met_peer(1)
    far_piece(0, 0, 1)
    for piece in range(1, pieces):
        far_piece(piece, piece * height, 0)
        far_piece(piece, piece * height, 1)
    send_down()
    start_down()
    near_piece(2)
    near_piece(3)

    def turned(i, sx):
        first = i * 9 + sx * 3
        return jnp.concatenate([w_fine[first + 2 - m] for m in range(3)], axis=1)

    def mt(a, b):
        return lax.dot_general(a, b, CONTRACT_LAST, preferred_element_type=F32)

    spread_rows(g3, 1, grad16[0], 0)
    spread_rows(g3, 2, grad16[1], 1)
    total = None
    for sx in range(3):
        term = mt(window(g3, 1, 2 - sx), jnp.concatenate([turned(1, sx), turned(2, sx)], axis=0))
        total = term if total is None else total + term
        total = total + mt(
            window(g3, 2, 2 - sx), jnp.concatenate([turned(0, sx), turned(1, sx)], axis=0)
        )
    act[...] = total
    start_some(near)
    for piece in range(pieces):
        cross_piece(piece)
    for copies in far_copies:
        for copy in copies:
            copy.wait_send()
    near_on()
    wait_halo(g_copies)
    spread_rows(g3, 0, g_halo[0], 0)
    spread_rows(g3, 3, g_halo[1], 1)
    for side in range(2):
        total = act[:, side * ch : (side + 1) * ch] + hid_grad[side].reshape(plane, ch)
        for sx in range(3):
            total = total + mt(window(g3, 3 * side, 2 - sx), turned(2 - 2 * side, sx))
        feature_grad[0, side] = total.astype(BF16).reshape(ex, ez, ch)


    for copy in mix_copies:
        copy.wait()
    mix_total[...] = sum(mix_recv[s] for s in range(n)) * scale
    mix_swap = to_peer(mix_total, mix_peer, last_s.at[0], last_r.at[0])
    mix_swap.start()

    wait_down()
    value = sum(down_recv[s].astype(F32) for s in range(groups)) * scale
    for h in range(halves):
        down_half[pl.ds(h, down_part, stride=halves), :] = value[:, h * lanes : (h + 1) * lanes]
    down_swap = to_peer(down_half, down_half_peer, last_s.at[1], last_r.at[1])
    down_swap.start()

    near_copies[4].wait()
    near_copies[5].wait()
    fine_swaps = []
    for piece, copy in enumerate(cross_copies):
        rows_of = slice(piece * height, (piece + 1) * height)
        value = fine_keep[2, rows_of] + sum(fine_recv[j, rows_of].astype(F32) for j in (4, 5))
        copy.wait()
        fine_half[rows_of] = (value + fine_recv[6, rows_of].astype(F32)) * scale
        swap = to_peer(
            fine_half.at[pl.ds(piece * height, height)],
            fine_half_peer.at[pl.ds(piece * height, height)],
            last_s.at[2 + piece], last_r.at[2 + piece],
        )
        swap.start()
        fine_swaps.append(swap)

    skew = fine_mine - fine_step

    def put_fine(source, whose):
        fine_out[pl.ds(pl.multiple_of(whose * fine_mine, 8), fine_mine), :] = source[
            pl.ds(pl.multiple_of(whose * skew, 8), fine_mine), :
        ]

    down_len = down_part * halves
    put_fine(fine_half, core)
    down_out[pl.ds(pl.multiple_of(core * down_len, 8), down_len), :] = down_half[...]
    mix_swap.wait()
    mix_total[...] = mix_total[...] + mix_peer[...]
    mixing_out[...] = mix_total[pl.ds(me, 1), 0:n]
    down_swap.wait()
    down_out[pl.ds(pl.multiple_of(other * down_len, 8), down_len), :] = down_half_peer[...]
    for swap in fine_swaps:
        swap.wait()
    put_fine(fine_half_peer, other)


def put_out(*refs):
    sources, dests, done = refs[:5], refs[5:10], refs[10]
    copies = [
        pltpu.make_async_copy(source, dest, done.at[i])
        for i, (source, dest) in enumerate(zip(sources, dests))
    ]
    for copy in copies:
        copy.start()
    for copy in copies:
        copy.wait()


def fused_fits(mesh, features, w_down):
    n = mesh.shape["space"]
    batch, ny, ex, ez, ch = features.shape
    cc = w_down.shape[2]
    spots = ex * ez // 4
    return (
        batch == mesh.shape["groups"] * mesh.shape["sample"]
        and ny == 2 * n
        and mesh.shape["sample"] == 2
        and n == 8
        and w_down.shape[0] == 8
        and -(27 * ch // n // 2) // 16 % 2 == 0
        and ch == 128
        and cc % 128 == 0
        and ez % 16 == 0
        and ex % 2 == 0
        and spots % 8 == 0
        and (spots * cc) % (n * 128 * 16) == 0
        and (27 * ch) % (n * 16) == 0
        and (8 * ch) % (n * 32) == 0
    )


def fused(mesh, features, w_fine, w_down, mixing, cotangent):
    n = lax.axis_size("space")
    _, _, ex, ez, ch = features.shape
    cc = w_down.shape[2]
    batch = lax.axis_size("sample")
    scale = float(batch * 2 * n * ex * ez) ** (-0.5)
    plane, spots, lanes = ex * ez, ex * ez // 4, 128
    rows = spots * cc // lanes // n
    fine_rows, down_rows = 27 * ch // n, 8 * ch // n
    half = fine_rows // 2
    part = -(-half // 16) * 16
    down_part = down_rows // 2
    down_len = down_part * cc // lanes
    vm = pltpu.VMEM
    dma = pltpu.SemaphoreType.DMA
    groups = n // 2
    arrays = (features, w_fine, w_down, mixing, cotangent)
    scratch = [
        *[vm(array.shape, BF16) for array in arrays], dma((5,)),
        vm((2, ex, ez, ch), BF16), vm((2, ex, ez, ch), BF16), vm((2, ex, ez, ch), BF16),
        vm((2, ex, ez + 16, ch), F32),
        vm((4, ex + 2, ez, 3 * ch), BF16), vm((4, ex + 2, ez, 3 * ch), BF16),
        vm((3, 3 * ch, 4 * plane), BF16),
        vm((plane, 2 * ch), F32),
        vm((2, ex // 2, 2, ez, ch), F32),
        vm((2, spots, 4 * ch), BF16), vm((spots, 4 * ch), BF16),
        vm((groups, ch, 2 * spots), BF16),
        vm((n * rows, lanes), F32),
        vm((n, rows, lanes), BF16), vm((n, rows, lanes), BF16),
        vm((n, rows, lanes), BF16), vm((2, n, rows, lanes), BF16),
        vm((2, ex // 2, 2, ez, ch), F32),
        vm((27 * ch, ch), BF16),
        vm((n, part, ch), BF16), *[vm((7, part, ch), BF16)] * 2, vm((3, part, ch), F32),
        vm((groups, down_part, 2 * spots), BF16), vm((2, n, rows, lanes), BF16),
        *[vm((groups, down_part, cc), BF16)] * 2,
        vm((n, lanes), F32), vm((n, n, lanes), F32), vm((n, lanes), F32), vm((n, lanes), F32),
        vm((part, ch), F32), vm((part, ch), F32),
        vm((down_len, lanes), F32), vm((down_len, lanes), F32),
        dma((2,)), dma((2,)), dma((n - 1,)), dma((n - 1,)), dma((n - 1,)), dma((n - 1,)),
        dma((n - 1,)), dma((n - 1,)),
        dma((2,)), dma((2,)), dma((n,)), dma((n,)), dma, dma,
        *[dma] * 4,
        *[dma((7 * 2,))] * 2, *[dma((groups - 1,))] * 2, dma((4,)), dma((4,)),
        pltpu.SemaphoreType.REGULAR((2,)),
    ]
    spec = pl.BlockSpec(memory_space=pltpu.VMEM)
    far = pl.BlockSpec(memory_space=pltpu.HBM)
    shapes = (
        jax.ShapeDtypeStruct(cotangent.shape, BF16),
        jax.ShapeDtypeStruct(features.shape, BF16),
        jax.ShapeDtypeStruct((fine_rows, ch), F32),
        jax.ShapeDtypeStruct((down_rows * cc // lanes, lanes), F32),
        jax.ShapeDtypeStruct((1, n), F32),
    )
    results = pl.pallas_call(
        functools.partial(fused_body, (n, ex, ez, ch, cc, scale)),
        out_shape=shapes,
        in_specs=[far] * 5,
        out_specs=tuple([spec] * 5),
        scratch_shapes=scratch,
        compiler_params=pltpu.CompilerParams(
            collective_id=0, has_side_effects=True, vmem_limit_bytes=65472 * 1024
        ),
    )(*arrays)
    a, b, c, d, e = pl.pallas_call(
        put_out,
        out_shape=shapes,
        in_specs=[spec] * 5,
        out_specs=tuple([far] * 5),
        scratch_shapes=[dma((5,))],
        compiler_params=pltpu.CompilerParams(vmem_limit_bytes=65472 * 1024),
    )(*results)
    return a, b, c.reshape(-1), d.reshape(-1), e


def with_halo(array, sides, width):
    for axis, dim in sides:
        devices, length = (lax.axis_size(axis), array.shape[dim])
        up = [(i, (i + 1) % devices) for i in range(devices - 1)]
        down = [(j, i) for i, j in up]
        last = lax.slice_in_dim(array, length - width, length, axis=dim)
        initial = lax.slice_in_dim(array, 0, width, axis=dim)
        before = lax.ppermute(last, axis, up)
        after = lax.ppermute(initial, axis, down)
        array = jnp.concatenate([before, array, after], axis=dim)
    return array


def forward_conv(padded, weight, count):
    extent_x = padded.shape[2] - 2
    extent_z = padded.shape[3] - 2
    channels = padded.shape[4]
    total = None
    for shift_y in range(3):
        for shift_x in range(3):
            pieces = [
                padded[
                    :,
                    shift_y : shift_y + count,
                    shift_x : shift_x + extent_x,
                    shift_z : shift_z + extent_z,
                    :,
                ]
                for shift_z in range(3)
            ]
            stacked = jnp.concatenate(pieces, axis=-1).reshape(-1, 3 * channels)
            first = shift_y * 9 + shift_x * 3
            kernel = weight[first : first + 3].reshape(3 * channels, weight.shape[2])
            term = jnp.dot(stacked, kernel, preferred_element_type=jnp.float32)
            total = term if total is None else total + term
    return total.reshape(padded.shape[0], count, extent_x, extent_z, weight.shape[2])


def transposed_conv(padded, weight, count):
    extent_x = padded.shape[2] - 2
    extent_z = padded.shape[3] - 2
    channels = padded.shape[4]
    total = None
    for shift_y in range(3):
        for shift_x in range(3):
            pieces = [
                padded[
                    :,
                    2 - shift_y : 2 - shift_y + count,
                    2 - shift_x : 2 - shift_x + extent_x,
                    2 - shift_z : 2 - shift_z + extent_z,
                    :,
                ]
                for shift_z in range(3)
            ]
            stacked = jnp.concatenate(pieces, axis=-1).reshape(-1, 3 * channels)
            first = shift_y * 9 + shift_x * 3
            kernel = jnp.swapaxes(weight[first : first + 3], 1, 2).reshape(
                3 * channels, weight.shape[1]
            )
            term = jnp.dot(stacked, kernel, preferred_element_type=jnp.float32)
            total = term if total is None else total + term
    return total.reshape(padded.shape[0], count, extent_x, extent_z, weight.shape[1])


def weight_terms(padded, grad, count):
    extent_x = padded.shape[2] - 2
    extent_z = padded.shape[3] - 2
    channels = padded.shape[4]
    flat_grad = grad.reshape(-1, grad.shape[4])
    blocks = []
    for shift_y in range(3):
        for shift_x in range(3):
            pieces = [
                padded[
                    :,
                    shift_y : shift_y + count,
                    shift_x : shift_x + extent_x,
                    shift_z : shift_z + extent_z,
                    :,
                ]
                for shift_z in range(3)
            ]
            stacked = jnp.concatenate(pieces, axis=-1).reshape(-1, 3 * channels)
            blocks.append(
                lax.dot_general(
                    stacked, flat_grad, (((0,), (0,)), ((), ())), preferred_element_type=jnp.float32
                )
            )
    return jnp.concatenate(blocks, axis=0).reshape(-1)


def fold_taps(hidden):
    batch, rows_here, extent_x, extent_z, channels = hidden.shape
    shaped = hidden.reshape(batch, rows_here // 2, 2, extent_x // 2, 2, extent_z // 2, 2, channels)
    return shaped.transpose(0, 1, 3, 5, 2, 4, 6, 7).reshape(-1, 8 * channels)


def unfold_taps(values, batch, rows_here, extent_x, extent_z, channels):
    shaped = values.reshape(batch, rows_here // 2, extent_x // 2, extent_z // 2, 2, 2, 2, channels)
    return shaped.transpose(0, 1, 4, 2, 5, 3, 6, 7).reshape(
        batch, rows_here, extent_x, extent_z, channels
    )


def silu_slope(value):
    sigma = jax.nn.sigmoid(value)
    return sigma * (1.0 + value * (1.0 - sigma))


def local(features, w_fine, w_down, mixing, cotangent):
    batch, rows_here, extent_x, extent_z, channels = features.shape
    coarse_ch = w_down.shape[2]
    rimmed = with_halo(features, (("space", 1),), 1)
    xpadded = jnp.pad(rimmed, ((0, 0), (0, 0), (1, 1), (1, 1), (0, 0)))
    act = forward_conv(xpadded, w_fine, rows_here)
    hidden = (features.astype(jnp.float32) + jax.nn.silu(act)).astype(jnp.bfloat16)
    folded = fold_taps(hidden)
    down_matrix = w_down.reshape(8 * channels, coarse_ch)
    coarse = jnp.dot(folded, down_matrix, preferred_element_type=jnp.float32).astype(jnp.bfloat16)
    coarse = coarse.reshape(batch, rows_here // 2, -1)
    columns = lax.all_to_all(coarse, "space", split_axis=2, concat_axis=1, tiled=True)
    mixed = jnp.stack([jnp.dot(mixing, columns[0], preferred_element_type=jnp.float32)])
    bottleneck = (columns.astype(jnp.float32) + jax.nn.silu(mixed)).astype(jnp.bfloat16)
    cot = cotangent.astype(jnp.float32)
    mixed_grad = (cot * silu_slope(mixed)).astype(jnp.bfloat16)
    term = lax.dot_general(
        mixed_grad[0], columns[0], (((1,), (1,)), ((), ())), preferred_element_type=jnp.float32
    )
    spread_list = [
        lax.dot_general(
            mixing, mixed_grad[0], (((0,), (0,)), ((), ())), preferred_element_type=jnp.float32
        )
    ]
    column_grad = (cot + jnp.stack(spread_list)).astype(jnp.bfloat16)
    coarse_grad = lax.all_to_all(column_grad, "space", split_axis=1, concat_axis=2, tiled=True)
    flat_coarse = coarse_grad.reshape(-1, coarse_ch)
    down_terms = lax.dot_general(
        folded, flat_coarse, (((0,), (0,)), ((), ())), preferred_element_type=jnp.float32
    ).reshape(-1)
    hidden_grad = unfold_taps(
        jnp.dot(flat_coarse, down_matrix.T, preferred_element_type=jnp.float32),
        batch,
        rows_here,
        extent_x,
        extent_z,
        channels,
    )
    act_grad = (hidden_grad * silu_slope(act)).astype(jnp.bfloat16)
    grad_rim = with_halo(act_grad, (("space", 1),), 1)
    gpadded = jnp.pad(grad_rim, ((0, 0), (0, 0), (1, 1), (1, 1), (0, 0)))
    spread = transposed_conv(gpadded, w_fine, rows_here)
    feature_grad = (hidden_grad + spread).astype(jnp.bfloat16)
    fine_terms = weight_terms(xpadded, act_grad, rows_here)
    scale = float(
        batch * lax.axis_size("sample") * rows_here * lax.axis_size("space") * extent_x * extent_z
    ) ** (-0.5)
    shares = (
        lax.psum_scatter(fine_terms, "space", scatter_dimension=0, tiled=True),
        lax.psum_scatter(down_terms, "space", scatter_dimension=0, tiled=True),
        lax.psum_scatter(term, "space", scatter_dimension=0, tiled=True),
    )
    totals = lax.psum((shares[0], shares[1], shares[2]), "sample")
    return (bottleneck, feature_grad, totals[0] * scale, totals[1] * scale, totals[2] * scale)


def solution(mesh):
    placed = (
        P(("groups", "sample"), "space", None, None, None),
        P(),
        P(),
        P(),
        P(("groups", "sample"), None, "space"),
    )
    out_specs = (
        P(("groups", "sample"), None, "space"),
        P(("groups", "sample"), "space", None, None, None),
        P(("groups", "space")),
        P(("groups", "space")),
        P(("groups", "space"), None),
    )

    def step(features, w_fine, w_down, mixing, cotangent):
        kernel = functools.partial(fused, mesh) if fused_fits(mesh, features, w_down) else local
        mapped = jax.shard_map(
            kernel, mesh=mesh, in_specs=placed, out_specs=out_specs, check_vma=False
        )
        return mapped(features, w_fine, w_down, mixing, cotangent)

    return step
```

```python
import functools

import jax
import jax.numpy as jnp
from jax import lax
from jax.experimental import pallas as pl
from jax.experimental.pallas import tpu as pltpu
from jax.sharding import PartitionSpec as P

MESH = pl.DeviceIdType.MESH
F32 = jnp.float32
BF16 = jnp.bfloat16
CONTRACT_LAST = (((1,), (1,)), ((), ()))
CONTRACT_FIRST = (((0,), (0,)), ((), ()))


def fused_body(
    cfg,
    features_in, w_fine_in, w_down_in, mixing_in, cotangent_in,
    bottleneck, feature_grad, fine_out, down_out, mixing_out,
    features, w_fine, w_down, mixing, cotangent, load_s,
    x_halo, g_halo, grad16, pad, x3, g3, xt, act, hid, folded, fold_met, folded_t,
    stage, fwd_send, fwd_recv, back_send, back_recv, hid_grad,
    fine16, fine_peer, fine_send, fine_recv, fine_keep,
    fold_peer, back_peer, down16, down_recv,
    mix_send, mix_recv, mix_total, mix_peer,
    fine_half, fine_half_peer, down_half, down_half_peer,
    halo_s, halo_r, fwd_s, fwd_r, back_s, back_r, mix_s, mix_r,
    ghalo_s, ghalo_r, peer_s, peer_r, dpeer_s, dpeer_r,
    fold_s, fold_r, turn_s, turn_r, fine_s, fine_r, down_s, down_r, last_s, last_r,
    gate,
):
    n, ex, ez, ch, cc, scale = cfg
    plane = ex * ez
    hx, hz = ex // 2, ez // 2
    lanes = 128
    rows = hx * hz * cc // lanes // n
    halves = cc // lanes
    fine_rows = 27 * ch // n
    part = fine_send.shape[1]
    fine_step = fine_rows - part
    fine_mine = fine_rows // 2
    down_rows = 8 * ch // n
    down_part = down_rows // 2
    me = lax.axis_index("space")
    core = lax.axis_index("sample")
    other = 1 - core

    def to_space(src, dst, send, recv, who):
        return pltpu.make_async_remote_copy(
            src_ref=src, dst_ref=dst, send_sem=send, recv_sem=recv,
            device_id={"space": who}, device_id_type=MESH,
        )

    def to_peer(src, dst, send, recv):
        return pltpu.make_async_remote_copy(
            src_ref=src, dst_ref=dst, send_sem=send, recv_sem=recv,
            device_id={"sample": other}, device_id_type=MESH,
        )

    has_prev, has_next = me > 0, me < n - 1
    groups = n // 2
    group, side_of = me // 2, lax.rem(me, 2)
    partner = me + 1 - 2 * side_of

    barrier = pltpu.get_barrier_semaphore()
    greeted = 1
    for shift in (-2, -1, 1, 2):
        who = me + shift
        inside = jnp.logical_and(who >= 0, who < n)
        greeted = greeted + inside.astype(jnp.int32)

        @pl.when(inside)
        def _(who=who):
            pl.semaphore_signal(barrier, inc=1, device_id={"space": who}, device_id_type=MESH)

    pl.semaphore_signal(barrier, inc=1, device_id={"sample": other}, device_id_type=MESH)
    loads = [
        pltpu.make_async_copy(source, dest, load_s.at[i])
        for i, (source, dest) in enumerate(
            (
                (features_in, features),
                (w_fine_in, w_fine),
                (w_down_in, w_down),
                (mixing_in, mixing),
                (cotangent_in, cotangent),
            )
        )
    ]
    for load in loads:
        load.start()

    def halo_copies(first, last, halo, send, recv):
        down = to_space(first, halo.at[1], send.at[0], recv.at[1], me - 1)
        up = to_space(last, halo.at[0], send.at[1], recv.at[0], me + 1)
        return down, up

    def start_halo(copies):
        pl.when(has_prev)(copies[0].start)
        pl.when(has_next)(copies[1].start)

    def wait_halo(copies):
        def with_prev():
            copies[0].wait_send()
            copies[1].wait_recv()

        def with_next():
            copies[1].wait_send()
            copies[0].wait_recv()

        pl.when(has_prev)(with_prev)
        pl.when(has_next)(with_next)

    x_copies = halo_copies(features.at[0, 0], features.at[0, 1], x_halo, halo_s, halo_r)
    loads[0].wait()
    pl.semaphore_wait(barrier, greeted)
    start_halo(x_copies)
    gates = ((group > 0, group < groups - 1, me + 2), (group < groups - 1, group > 0, me - 2))
    ends = jnp.logical_or(group == 0, group == groups - 1)

    def await_gate(slot):
        pl.when(gates[slot][0])(lambda: pl.semaphore_wait(gate.at[slot], 1))

    for slot, (_, onward, after) in enumerate(gates):
        pl.when(jnp.logical_not(ends))(lambda slot=slot: await_gate(slot))

        @pl.when(onward)
        def _(slot=slot, after=after):
            pl.semaphore_signal(
                gate.at[slot], inc=1, device_id={"space": after}, device_id_type=MESH
            )

    @pl.when(me == 0)
    def _():
        x_halo[0] = jnp.zeros(x_halo.shape[1:], BF16)
        g_halo[0] = jnp.zeros(g_halo.shape[1:], BF16)

    @pl.when(me == n - 1)
    def _():
        x_halo[1] = jnp.zeros(x_halo.shape[1:], BF16)
        g_halo[1] = jnp.zeros(g_halo.shape[1:], BF16)

    pad[:, :, 0:8, :] = jnp.zeros((2, ex, 8, ch), F32)
    pad[:, :, 8 + ez : 16 + ez, :] = jnp.zeros((2, ex, 8, ch), F32)
    for rim in (0, ex + 1):
        x3[:, rim] = jnp.zeros((4, ez, 3 * ch), BF16)
        g3[:, rim] = jnp.zeros((4, ez, 3 * ch), BF16)

    def spread_rows(dest, index, row, slot):
        pad[slot, :, 8 : 8 + ez, :] = row.astype(F32)
        dest[index, 1 : 1 + ex, :, 0:ch] = pad[slot, :, 7 : 7 + ez, :].astype(BF16)
        dest[index, 1 : 1 + ex, :, ch : 2 * ch] = row
        dest[index, 1 : 1 + ex, :, 2 * ch : 3 * ch] = pad[slot, :, 9 : 9 + ez, :].astype(BF16)

    def window(source, index, shift):
        return source[index, shift : shift + ex].reshape(plane, 3 * ch)

    def taps(sy, sx):
        first = sy * 9 + sx * 3
        return w_fine[first : first + 3].reshape(3 * ch, ch)

    def mm(a, b):
        return jnp.dot(a, b, preferred_element_type=F32)

    spread_rows(x3, 1, features[0, 0], 0)
    spread_rows(x3, 2, features[0, 1], 1)
    loads[1].wait()
    total = None
    for sx in range(3):
        term = mm(window(x3, 1, sx), jnp.concatenate([taps(1, sx), taps(0, sx)], axis=1))
        total = term if total is None else total + term
        total = total + mm(
            window(x3, 2, sx), jnp.concatenate([taps(2, sx), taps(1, sx)], axis=1)
        )
    act[...] = total
    for slot in range(2):
        pl.when(ends)(lambda slot=slot: await_gate(slot))
    wait_halo(x_copies)
    spread_rows(x3, 0, x_halo[0], 0)
    spread_rows(x3, 3, x_halo[1], 1)
    for side in range(2):
        total = act[:, side * ch : (side + 1) * ch]
        for sx in range(3):
            total = total + mm(window(x3, 3 * side, sx), taps(2 * side, sx))
        act[:, side * ch : (side + 1) * ch] = total
        value = features[0, side].reshape(plane, ch).astype(F32) + total * jax.nn.sigmoid(total)
        hid[side] = value.astype(BF16).astype(F32).reshape(hx, 2, ez, ch)

    for t in range(8):
        i, j, k = t // 4, t // 2 % 2, t % 2
        piece = hid[i, :, j, pl.ds(k, hz, stride=2), :].reshape(hx * hz, ch)
        folded[k, :, t // 2 * ch : (t // 2 + 1) * ch] = piece.astype(BF16)
    loads[2].wait()
    coarse = mm(folded[0], jnp.concatenate([w_down[t] for t in range(0, 8, 2)], axis=0))
    coarse = coarse + mm(folded[1], jnp.concatenate([w_down[t] for t in range(1, 8, 2)], axis=0))
    coarse = coarse.astype(BF16).astype(F32)
    for h in range(halves):
        stage[pl.ds(h, hx * hz, stride=halves), :] = coarse[:, h * lanes : (h + 1) * lanes]
    fwd_send[...] = stage[...].astype(BF16).reshape(n, rows, lanes)

    def exchange(src_of, slot, send, recv):
        out = []
        for k in range(n - 1, 0, -1):
            step = jnp.where(me < n // 2, k, n - k)
            who = lax.rem(me + step, n)
            copy = to_space(src_of(who), slot(), send.at[step - 1], recv.at[step - 1], who)
            copy.start()
            out.append(copy)
        return out

    coarse_copies = exchange(
        lambda who: fwd_send.at[who], lambda: fwd_recv.at[me], fwd_s, fwd_r
    )
    fold_copy = to_space(folded.at[1 - side_of], fold_met, fold_s, fold_r, partner)
    fwd_recv[me] = fwd_send[me]

    loads[3].wait()
    loads[4].wait()
    for sx in range(3):
        for j in range(4):
            xt[sx, :, j * plane : (j + 1) * plane] = window(x3, j, sx).T

    for copy in coarse_copies:
        copy.wait()
    stage[...] = fwd_recv[...].reshape(n * rows, lanes).astype(F32)
    columns = jnp.concatenate([stage[pl.ds(r, n, stride=rows), :] for r in range(rows)], axis=1)
    columns16 = columns.astype(BF16)
    mix = mixing[...]
    mixed = mm(mix, columns16)
    sigma = jax.nn.sigmoid(mixed)
    cot = cotangent[0].astype(F32)
    mixed_grad = (cot * (sigma * (1.0 + mixed * (1.0 - sigma)))).astype(BF16)
    spread = lax.dot_general(mix, mixed_grad, CONTRACT_FIRST, preferred_element_type=F32)
    column_grad = cot + spread
    for r in range(rows):
        stage[pl.ds(r, n, stride=rows), :] = column_grad[:, r * lanes : (r + 1) * lanes]
    back_send[...] = stage[...].astype(BF16).reshape(n, rows, lanes)
    back_copies = exchange(
        lambda who: back_send.at[pl.ds(who // 2 * 2, 2)], lambda: back_recv.at[:, me],
        back_s, back_r,
    )
    fold_copy.start()
    for side in range(2):
        back_recv[side, me] = back_send[2 * group + side]
    term = lax.dot_general(mixed_grad, columns16, CONTRACT_LAST, preferred_element_type=F32)
    mix_send[...] = jnp.zeros(mix_send.shape, F32)
    mix_send[:, 0:n] = term
    mix_copies = exchange(lambda who: mix_send, lambda: mix_recv.at[me], mix_s, mix_r)
    mix_recv[me] = mix_send[...]
    bottleneck[0] = (columns + mixed * sigma).astype(BF16)
    value = act[...]
    sig = jax.nn.sigmoid(value)
    act[...] = sig * (1.0 + value * (1.0 - sig))

    fold_copy.wait()
    turned_taps = jnp.concatenate([folded[side_of], fold_met[...]], axis=0).T
    folded_t[...] = turned_taps.reshape(groups, ch, 2 * hx * hz)
    turn_copy = to_peer(
        folded_t.at[:, pl.ds(pl.multiple_of(other * down_part, 16), down_part), :],
        fold_peer, turn_s, turn_r,
    )
    turn_copy.start()

    def flat_of(source, side):
        stage[...] = source[side].reshape(n * rows, lanes).astype(F32)
        return jnp.concatenate(
            [stage[pl.ds(h, hx * hz, stride=halves), :] for h in range(halves)], axis=1
        ).astype(BF16)

    for copy in back_copies:
        copy.wait()
    flat_copy = to_peer(back_recv, back_peer, dpeer_s, dpeer_r)
    flat_copy.start()
    flat = flat_of(back_recv, side_of)

    for t in range(8):
        i, j, k = t // 4, t // 2 % 2, t % 2
        piece = lax.dot_general(flat, w_down[t], CONTRACT_LAST, preferred_element_type=F32)
        hid_grad[i, :, j, pl.ds(k, hz, stride=2), :] = piece.reshape(hx, hz, ch)
    for side in range(2):
        grad = hid_grad[side].reshape(plane, ch) * act[:, side * ch : (side + 1) * ch]
        grad16[side] = grad.astype(BF16).reshape(ex, ez, ch)
    g_copies = halo_copies(grad16.at[0], grad16.at[1], g_halo, ghalo_s, ghalo_r)

    near = (side_of == 1, side_of == 0)
    away = (
        jnp.logical_and(side_of == 0, has_prev), jnp.logical_and(side_of == 1, has_next)
    )

    def start_some(conditions):
        for condition, copy in zip(conditions, g_copies):
            pl.when(condition)(copy.start)

    start_some(away)
    def send_down():
        turn_copy.wait()
        flat_copy.wait()
        taps_here = folded_t[:, pl.ds(pl.multiple_of(core * down_part, 16), down_part), :]
        left = jnp.concatenate([taps_here, fold_peer[...]], axis=2)
        right = jnp.concatenate(
            [
                flat, flat_of(back_recv, 1 - side_of),
                flat_of(back_peer, side_of), flat_of(back_peer, 1 - side_of),
            ],
            axis=0,
        )
        total = mm(left.reshape(groups * down_part, 4 * hx * hz), right)
        down16[...] = total.astype(BF16).reshape(groups, down_part, cc)

    def start_down():
        for step in range(groups - 1):
            to = lax.rem(group + step + 1, groups)
            to_space(
                down16.at[to], down_recv.at[group], down_s.at[step], down_r.at[step],
                2 * to + side_of,
            ).start()
        down_recv[group] = down16[group]

    def wait_down():
        for step in range(groups - 1):
            source = lax.rem(group - 1 - step + groups, groups)
            to_space(
                down16.at[source], down_recv.at[source], down_s.at[step], down_r.at[step], partner
            ).wait()

    flip = group + 1 - 2 * lax.rem(group, 2)
    across = lax.rem(group + 2, groups)
    owners = (lax.rem(flip + 2, groups), across, flip, group)
    orders = ((8, 7, 6, 5, 4, 3, 2, 1, 0), (6, 5, 4, 8, 7, 2, 1, 0, 3))
    orders = orders + tuple(tuple(8 - t for t in order) for order in orders[::-1])

    flat_grad = grad16[...].reshape(2 * plane, ch)

    def fine_block(i):
        t = orders[0][i]
        for g in range(1, groups):
            t = jnp.where(group == g, orders[g][i], t)
        sy, sx = t // 3, lax.rem(t, 3)
        window_t = xt[sx, :, pl.ds(pl.multiple_of(sy * plane, lanes), 2 * plane)]
        start = pl.multiple_of(t * 3 * ch, lanes)
        fine16[pl.ds(start, 3 * ch), :] = mm(window_t, flat_grad).astype(BF16)

    peer_copies = []

    def fine_to_peer(k):
        for j in range(2):
            who = 2 * owners[k] + j
            start = pl.multiple_of(who * fine_rows + other * fine_step, 16)
            copy = to_peer(
                fine16.at[pl.ds(start, part), :], fine_peer.at[who],
                peer_s.at[2 * k + j], peer_r.at[2 * k + j],
            )
            copy.start()
            peer_copies.append(copy)

    def fine_own(who):
        start = pl.multiple_of(who * fine_rows + core * fine_step, 16)
        return fine16[pl.ds(start, part), :].astype(F32) + fine_peer[who].astype(F32)

    pieces = 2
    height = part // pieces

    def own_rows(who, first, count):
        start = pl.multiple_of(who * fine_rows + core * fine_step + first, 16)
        mine = fine16[pl.ds(start, count), :].astype(F32)
        return mine + fine_peer[who, first : first + count].astype(F32)

    def slot_copy(slot, piece, who):
        rows_of = pl.ds(piece * height, height)
        index = slot * pieces + piece
        return to_space(
            fine_send.at[slot, rows_of], fine_recv.at[slot, rows_of],
            fine_s.at[index], fine_r.at[index], who,
        )

    def whole_copy(slot, who):
        return to_space(
            fine_send.at[slot], fine_recv.at[slot],
            fine_s.at[slot * pieces], fine_r.at[slot * pieces], who,
        )

    far_copies = [[None] * 3 for _ in range(pieces)]

    def met_peer(k):
        peer_copies[2 * k].wait()
        peer_copies[2 * k + 1].wait()

    def far_piece(piece, first, k):
        to = 2 * owners[k]
        targets = ((2, 1 - side_of), (1, side_of)) if k == 0 else ((0, 1 - side_of),)
        for slot, side in targets:
            fine_send[slot, first : first + height] = own_rows(to + side, first, height).astype(BF16)
            at = (partner, 2 * flip + side_of, 2 * flip + 1 - side_of)[slot]
            copy = slot_copy(slot, piece, at)
            copy.start()
            far_copies[piece][slot] = copy
        if k == 1:
            fine_keep[0, first : first + height] = own_rows(to + side_of, first, height)

    near_copies = {}

    def near_piece(k):
        met_peer(k)
        fine_send[k + 1] = fine_own(2 * owners[k] + 1 - side_of).astype(BF16)
        near_copies[k + 1] = whole_copy(k + 1, partner)
        near_copies[k + 1].start()
        fine_keep[k - 1] = fine_own(2 * owners[k] + side_of)

    def near_on():
        near_copies[3].wait()
        fine_send[5] = (fine_keep[1] + fine_recv[3].astype(F32)).astype(BF16)
        near_copies[5] = whole_copy(5, 2 * flip + side_of)
        near_copies[5].start()

    cross_copies = []

    def cross_piece(piece):
        for copy in far_copies[piece]:
            copy.wait_recv()
        first = piece * height
        rows_of = slice(first, first + height)
        total = fine_keep[0, rows_of] + sum(fine_recv[j, rows_of].astype(F32) for j in range(3))
        fine_send[6, rows_of] = total.astype(BF16)
        copy = slot_copy(6, piece, 2 * across + side_of)
        copy.start()
        cross_copies.append(copy)

    ready = {3: 0, 5: 1, 8: 2, 9: 3}
    for i in range(9):
        fine_block(i)
        if i + 1 in ready:
            fine_to_peer(ready[i + 1])
    met_peer(0)
    far_piece(0, 0, 0)
    met_peer(1)
    far_piece(0, 0, 1)
    for piece in range(1, pieces):
        far_piece(piece, piece * height, 0)
        far_piece(piece, piece * height, 1)
    send_down()
    start_down()
    near_piece(2)
    near_piece(3)

    def turned(i, sx):
        first = i * 9 + sx * 3
        return jnp.concatenate([w_fine[first + 2 - m] for m in range(3)], axis=1)

    def mt(a, b):
        return lax.dot_general(a, b, CONTRACT_LAST, preferred_element_type=F32)

    spread_rows(g3, 1, grad16[0], 0)
    spread_rows(g3, 2, grad16[1], 1)
    total = None
    for sx in range(3):
        term = mt(window(g3, 1, 2 - sx), jnp.concatenate([turned(1, sx), turned(2, sx)], axis=0))
        total = term if total is None else total + term
        total = total + mt(
            window(g3, 2, 2 - sx), jnp.concatenate([turned(0, sx), turned(1, sx)], axis=0)
        )
    act[...] = total
    start_some(near)
    for piece in range(pieces):
        cross_piece(piece)
    for copies in far_copies:
        for copy in copies:
            copy.wait_send()
    near_on()
    wait_halo(g_copies)
    spread_rows(g3, 0, g_halo[0], 0)
    spread_rows(g3, 3, g_halo[1], 1)
    for side in range(2):
        total = act[:, side * ch : (side + 1) * ch] + hid_grad[side].reshape(plane, ch)
        for sx in range(3):
            total = total + mt(window(g3, 3 * side, 2 - sx), turned(2 - 2 * side, sx))
        feature_grad[0, side] = total.astype(BF16).reshape(ex, ez, ch)


    for copy in mix_copies:
        copy.wait()
    mix_total[...] = sum(mix_recv[s] for s in range(n)) * scale
    mix_swap = to_peer(mix_total, mix_peer, last_s.at[0], last_r.at[0])
    mix_swap.start()

    wait_down()
    value = sum(down_recv[s].astype(F32) for s in range(groups)) * scale
    for h in range(halves):
        down_half[pl.ds(h, down_part, stride=halves), :] = value[:, h * lanes : (h + 1) * lanes]
    down_swap = to_peer(down_half, down_half_peer, last_s.at[1], last_r.at[1])
    down_swap.start()

    near_copies[4].wait()
    near_copies[5].wait()
    fine_swaps = []
    for piece, copy in enumerate(cross_copies):
        rows_of = slice(piece * height, (piece + 1) * height)
        value = fine_keep[2, rows_of] + sum(fine_recv[j, rows_of].astype(F32) for j in (4, 5))
        copy.wait()
        fine_half[rows_of] = (value + fine_recv[6, rows_of].astype(F32)) * scale
        swap = to_peer(
            fine_half.at[pl.ds(piece * height, height)],
            fine_half_peer.at[pl.ds(piece * height, height)],
            last_s.at[2 + piece], last_r.at[2 + piece],
        )
        swap.start()
        fine_swaps.append(swap)

    skew = fine_mine - fine_step

    def put_fine(source, whose):
        fine_out[pl.ds(pl.multiple_of(whose * fine_mine, 8), fine_mine), :] = source[
            pl.ds(pl.multiple_of(whose * skew, 8), fine_mine), :
        ]

    down_len = down_part * halves
    put_fine(fine_half, core)
    down_out[pl.ds(pl.multiple_of(core * down_len, 8), down_len), :] = down_half[...]
    mix_swap.wait()
    mix_total[...] = mix_total[...] + mix_peer[...]
    mixing_out[...] = mix_total[pl.ds(me, 1), 0:n]
    down_swap.wait()
    down_out[pl.ds(pl.multiple_of(other * down_len, 8), down_len), :] = down_half_peer[...]
    for swap in fine_swaps:
        swap.wait()
    put_fine(fine_half_peer, other)


def put_out(*refs):
    sources, dests, done = refs[:5], refs[5:10], refs[10]
    copies = [
        pltpu.make_async_copy(source, dest, done.at[i])
        for i, (source, dest) in enumerate(zip(sources, dests))
    ]
    for copy in copies:
        copy.start()
    for copy in copies:
        copy.wait()


def fused_fits(mesh, features, w_down):
    n = mesh.shape["space"]
    batch, ny, ex, ez, ch = features.shape
    cc = w_down.shape[2]
    spots = ex * ez // 4
    return (
        batch == mesh.shape["groups"] * mesh.shape["sample"]
        and ny == 2 * n
        and mesh.shape["sample"] == 2
        and n == 8
        and w_down.shape[0] == 8
        and -(27 * ch // n // 2) // 16 % 2 == 0
        and ch == 128
        and cc % 128 == 0
        and ez % 16 == 0
        and ex % 2 == 0
        and spots % 8 == 0
        and (spots * cc) % (n * 128 * 16) == 0
        and (27 * ch) % (n * 16) == 0
        and (8 * ch) % (n * 32) == 0
    )


def fused(mesh, features, w_fine, w_down, mixing, cotangent):
    n = lax.axis_size("space")
    _, _, ex, ez, ch = features.shape
    cc = w_down.shape[2]
    batch = lax.axis_size("sample")
    scale = float(batch * 2 * n * ex * ez) ** (-0.5)
    plane, spots, lanes = ex * ez, ex * ez // 4, 128
    rows = spots * cc // lanes // n
    fine_rows, down_rows = 27 * ch // n, 8 * ch // n
    half = fine_rows // 2
    part = -(-half // 16) * 16
    down_part = down_rows // 2
    down_len = down_part * cc // lanes
    vm = pltpu.VMEM
    dma = pltpu.SemaphoreType.DMA
    groups = n // 2
    arrays = (features, w_fine, w_down, mixing, cotangent)
    scratch = [
        *[vm(array.shape, BF16) for array in arrays], dma((5,)),
        vm((2, ex, ez, ch), BF16), vm((2, ex, ez, ch), BF16), vm((2, ex, ez, ch), BF16),
        vm((2, ex, ez + 16, ch), F32),
        vm((4, ex + 2, ez, 3 * ch), BF16), vm((4, ex + 2, ez, 3 * ch), BF16),
        vm((3, 3 * ch, 4 * plane), BF16),
        vm((plane, 2 * ch), F32),
        vm((2, ex // 2, 2, ez, ch), F32),
        vm((2, spots, 4 * ch), BF16), vm((spots, 4 * ch), BF16),
        vm((groups, ch, 2 * spots), BF16),
        vm((n * rows, lanes), F32),
        vm((n, rows, lanes), BF16), vm((n, rows, lanes), BF16),
        vm((n, rows, lanes), BF16), vm((2, n, rows, lanes), BF16),
        vm((2, ex // 2, 2, ez, ch), F32),
        vm((27 * ch, ch), BF16),
        vm((n, part, ch), BF16), *[vm((7, part, ch), BF16)] * 2, vm((3, part, ch), F32),
        vm((groups, down_part, 2 * spots), BF16), vm((2, n, rows, lanes), BF16),
        *[vm((groups, down_part, cc), BF16)] * 2,
        vm((n, lanes), F32), vm((n, n, lanes), F32), vm((n, lanes), F32), vm((n, lanes), F32),
        vm((part, ch), F32), vm((part, ch), F32),
        vm((down_len, lanes), F32), vm((down_len, lanes), F32),
        dma((2,)), dma((2,)), dma((n - 1,)), dma((n - 1,)), dma((n - 1,)), dma((n - 1,)),
        dma((n - 1,)), dma((n - 1,)),
        dma((2,)), dma((2,)), dma((n,)), dma((n,)), dma, dma,
        *[dma] * 4,
        *[dma((7 * 2,))] * 2, *[dma((groups - 1,))] * 2, dma((4,)), dma((4,)),
        pltpu.SemaphoreType.REGULAR((2,)),
    ]
    spec = pl.BlockSpec(memory_space=pltpu.VMEM)
    far = pl.BlockSpec(memory_space=pltpu.HBM)
    shapes = (
        jax.ShapeDtypeStruct(cotangent.shape, BF16),
        jax.ShapeDtypeStruct(features.shape, BF16),
        jax.ShapeDtypeStruct((fine_rows, ch), F32),
        jax.ShapeDtypeStruct((down_rows * cc // lanes, lanes), F32),
        jax.ShapeDtypeStruct((1, n), F32),
    )
    results = pl.pallas_call(
        functools.partial(fused_body, (n, ex, ez, ch, cc, scale)),
        out_shape=shapes,
        in_specs=[far] * 5,
        out_specs=tuple([spec] * 5),
        scratch_shapes=scratch,
        compiler_params=pltpu.CompilerParams(
            collective_id=0, has_side_effects=True, vmem_limit_bytes=65472 * 1024
        ),
    )(*arrays)
    a, b, c, d, e = pl.pallas_call(
        put_out,
        out_shape=shapes,
        in_specs=[spec] * 5,
        out_specs=tuple([far] * 5),
        scratch_shapes=[dma((5,))],
        compiler_params=pltpu.CompilerParams(vmem_limit_bytes=65472 * 1024),
    )(*results)
    return a, b, c.reshape(-1), d.reshape(-1), e


def with_halo(array, sides, width):
    for axis, dim in sides:
        devices, length = (lax.axis_size(axis), array.shape[dim])
        up = [(i, (i + 1) % devices) for i in range(devices - 1)]
        down = [(j, i) for i, j in up]
        last = lax.slice_in_dim(array, length - width, length, axis=dim)
        initial = lax.slice_in_dim(array, 0, width, axis=dim)
        before = lax.ppermute(last, axis, up)
        after = lax.ppermute(initial, axis, down)
        array = jnp.concatenate([before, array, after], axis=dim)
    return array


def forward_conv(padded, weight, count):
    extent_x = padded.shape[2] - 2
    extent_z = padded.shape[3] - 2
    channels = padded.shape[4]
    total = None
    for shift_y in range(3):
        for shift_x in range(3):
            pieces = [
                padded[
                    :,
                    shift_y : shift_y + count,
                    shift_x : shift_x + extent_x,
                    shift_z : shift_z + extent_z,
                    :,
                ]
                for shift_z in range(3)
            ]
            stacked = jnp.concatenate(pieces, axis=-1).reshape(-1, 3 * channels)
            first = shift_y * 9 + shift_x * 3
            kernel = weight[first : first + 3].reshape(3 * channels, weight.shape[2])
            term = jnp.dot(stacked, kernel, preferred_element_type=jnp.float32)
            total = term if total is None else total + term
    return total.reshape(padded.shape[0], count, extent_x, extent_z, weight.shape[2])


def transposed_conv(padded, weight, count):
    extent_x = padded.shape[2] - 2
    extent_z = padded.shape[3] - 2
    channels = padded.shape[4]
    total = None
    for shift_y in range(3):
        for shift_x in range(3):
            pieces = [
                padded[
                    :,
                    2 - shift_y : 2 - shift_y + count,
                    2 - shift_x : 2 - shift_x + extent_x,
                    2 - shift_z : 2 - shift_z + extent_z,
                    :,
                ]
                for shift_z in range(3)
            ]
            stacked = jnp.concatenate(pieces, axis=-1).reshape(-1, 3 * channels)
            first = shift_y * 9 + shift_x * 3
            kernel = jnp.swapaxes(weight[first : first + 3], 1, 2).reshape(
                3 * channels, weight.shape[1]
            )
            term = jnp.dot(stacked, kernel, preferred_element_type=jnp.float32)
            total = term if total is None else total + term
    return total.reshape(padded.shape[0], count, extent_x, extent_z, weight.shape[1])


def weight_terms(padded, grad, count):
    extent_x = padded.shape[2] - 2
    extent_z = padded.shape[3] - 2
    channels = padded.shape[4]
    flat_grad = grad.reshape(-1, grad.shape[4])
    blocks = []
    for shift_y in range(3):
        for shift_x in range(3):
            pieces = [
                padded[
                    :,
                    shift_y : shift_y + count,
                    shift_x : shift_x + extent_x,
                    shift_z : shift_z + extent_z,
                    :,
                ]
                for shift_z in range(3)
            ]
            stacked = jnp.concatenate(pieces, axis=-1).reshape(-1, 3 * channels)
            blocks.append(
                lax.dot_general(
                    stacked, flat_grad, (((0,), (0,)), ((), ())), preferred_element_type=jnp.float32
                )
            )
    return jnp.concatenate(blocks, axis=0).reshape(-1)


def fold_taps(hidden):
    batch, rows_here, extent_x, extent_z, channels = hidden.shape
    shaped = hidden.reshape(batch, rows_here // 2, 2, extent_x // 2, 2, extent_z // 2, 2, channels)
    return shaped.transpose(0, 1, 3, 5, 2, 4, 6, 7).reshape(-1, 8 * channels)


def unfold_taps(values, batch, rows_here, extent_x, extent_z, channels):
    shaped = values.reshape(batch, rows_here // 2, extent_x // 2, extent_z // 2, 2, 2, 2, channels)
    return shaped.transpose(0, 1, 4, 2, 5, 3, 6, 7).reshape(
        batch, rows_here, extent_x, extent_z, channels
    )


def silu_slope(value):
    sigma = jax.nn.sigmoid(value)
    return sigma * (1.0 + value * (1.0 - sigma))


def local(features, w_fine, w_down, mixing, cotangent):
    batch, rows_here, extent_x, extent_z, channels = features.shape
    coarse_ch = w_down.shape[2]
    rimmed = with_halo(features, (("space", 1),), 1)
    xpadded = jnp.pad(rimmed, ((0, 0), (0, 0), (1, 1), (1, 1), (0, 0)))
    act = forward_conv(xpadded, w_fine, rows_here)
    hidden = (features.astype(jnp.float32) + jax.nn.silu(act)).astype(jnp.bfloat16)
    folded = fold_taps(hidden)
    down_matrix = w_down.reshape(8 * channels, coarse_ch)
    coarse = jnp.dot(folded, down_matrix, preferred_element_type=jnp.float32).astype(jnp.bfloat16)
    coarse = coarse.reshape(batch, rows_here // 2, -1)
    columns = lax.all_to_all(coarse, "space", split_axis=2, concat_axis=1, tiled=True)
    mixed = jnp.stack([jnp.dot(mixing, columns[0], preferred_element_type=jnp.float32)])
    bottleneck = (columns.astype(jnp.float32) + jax.nn.silu(mixed)).astype(jnp.bfloat16)
    cot = cotangent.astype(jnp.float32)
    mixed_grad = (cot * silu_slope(mixed)).astype(jnp.bfloat16)
    term = lax.dot_general(
        mixed_grad[0], columns[0], (((1,), (1,)), ((), ())), preferred_element_type=jnp.float32
    )
    spread_list = [
        lax.dot_general(
            mixing, mixed_grad[0], (((0,), (0,)), ((), ())), preferred_element_type=jnp.float32
        )
    ]
    column_grad = (cot + jnp.stack(spread_list)).astype(jnp.bfloat16)
    coarse_grad = lax.all_to_all(column_grad, "space", split_axis=1, concat_axis=2, tiled=True)
    flat_coarse = coarse_grad.reshape(-1, coarse_ch)
    down_terms = lax.dot_general(
        folded, flat_coarse, (((0,), (0,)), ((), ())), preferred_element_type=jnp.float32
    ).reshape(-1)
    hidden_grad = unfold_taps(
        jnp.dot(flat_coarse, down_matrix.T, preferred_element_type=jnp.float32),
        batch,
        rows_here,
        extent_x,
        extent_z,
        channels,
    )
    act_grad = (hidden_grad * silu_slope(act)).astype(jnp.bfloat16)
    grad_rim = with_halo(act_grad, (("space", 1),), 1)
    gpadded = jnp.pad(grad_rim, ((0, 0), (0, 0), (1, 1), (1, 1), (0, 0)))
    spread = transposed_conv(gpadded, w_fine, rows_here)
    feature_grad = (hidden_grad + spread).astype(jnp.bfloat16)
    fine_terms = weight_terms(xpadded, act_grad, rows_here)
    scale = float(
        batch * lax.axis_size("sample") * rows_here * lax.axis_size("space") * extent_x * extent_z
    ) ** (-0.5)
    shares = (
        lax.psum_scatter(fine_terms, "space", scatter_dimension=0, tiled=True),
        lax.psum_scatter(down_terms, "space", scatter_dimension=0, tiled=True),
        lax.psum_scatter(term, "space", scatter_dimension=0, tiled=True),
    )
    totals = lax.psum((shares[0], shares[1], shares[2]), "sample")
    return (bottleneck, feature_grad, totals[0] * scale, totals[1] * scale, totals[2] * scale)


def solution(mesh):
    placed = (
        P(("groups", "sample"), "space", None, None, None),
        P(),
        P(),
        P(),
        P(("groups", "sample"), None, "space"),
    )
    out_specs = (
        P(("groups", "sample"), None, "space"),
        P(("groups", "sample"), "space", None, None, None),
        P(("groups", "space")),
        P(("groups", "space")),
        P(("groups", "space"), None),
    )

    def step(features, w_fine, w_down, mixing, cotangent):
        kernel = functools.partial(fused, mesh) if fused_fits(mesh, features, w_down) else local
        mapped = jax.shard_map(
            kernel, mesh=mesh, in_specs=placed, out_specs=out_specs, check_vma=False
        )
        return mapped(features, w_fine, w_down, mixing, cotangent)

    return step
```
